256 devices in a mesh: gx: 4 (over x), gy: 8 (over y, core), gz: 8 (over z).
Axes of the slice: x: 4, y: 4, z: 8, core: 2. Of those that a mesh axis runs over, the one named last changes fastest.
Arguments:
- right_side: float32 [128, 128, 1024], P('gx', 'gy', 'gz'), may hold values from -24 to 24
- conductivity: float32 [128, 128, 1024], P('gx', 'gy', 'gz'), may hold values from 0.2 to 5
Outputs:
- solution: float32 [128, 128, 1024], P('gx', 'gy', 'gz')
- final_residual: float32 [128, 128, 1024], P('gx', 'gy', 'gz')
The draws below stay inside these ranges and needn't reach their ends.
All inputs are finite; a program needn't handle non-finite values.
Results may differ from the reference program's by a relative error of at most 0.0003.
Values sent between devices are 32-bit elements; how exact they have to be, the bound alone decides.
A program may use at most 64 MiB of HBM per device.

```python
import math
import jax
import jax.numpy as jnp
from jax import lax

LEVELS = 4
STEPS = 3
COARSE_STEPS = 8
NX = 128
NY = 128
NZ = 1024


def draw_right_side(key, part):
    noise_part = 4.0 * jax.random.normal(key, (NX, NY, NZ), jnp.float32)
    noise_part = jnp.clip(noise_part, -24.0, 24.0)
    return noise_part


def shard_levels(rng, shape, cuts, smallest, high):
    gain, own = 1.0, jax.random.fold_in(rng, 6)
    for dim, blocks in cuts:
        heights = jnp.exp(jax.random.uniform(jax.random.fold_in(own, dim), (blocks,), jnp.float32, smallest / len(cuts), high / len(cuts)))
        gain = gain * jnp.repeat(heights, shape[dim] // blocks).reshape([-1 if axis == dim else 1 for axis in range(len(shape))])
    return gain


def setup_inputs(seed: int = 0) -> dict:
    streams_of = jax.random.split(jax.random.key(seed), 3)
    right_side = draw_right_side(jax.random.fold_in(streams_of[2], 71), 0)
    conductivity = jnp.clip(jnp.exp(math.log(5.0) - 3.218876 * jax.random.uniform(streams_of[1], (NX, NY, NZ), jnp.float32) ** shard_levels(streams_of[1], (NX, NY, NZ), ((0, 4), (1, 8), (2, 8)), -0.2, 0.2)), 0.2, 5.0)
    return dict(right_side=right_side, conductivity=conductivity)


LOWER_EDGE = 0.3
UPPER_EDGE = 2.0


def chebyshev_factors(sweeps):
    centre_value = 0.5 * (UPPER_EDGE + LOWER_EDGE)
    half_width = 0.5 * (UPPER_EDGE - LOWER_EDGE)
    ratio_value = centre_value / half_width
    damping = 1.0 / ratio_value
    factors = [(0.0, 1.0 / centre_value)]
    for sweep_index in range(1, sweeps):
        damping_next = 1.0 / (2.0 * ratio_value - damping)
        factors.append((damping_next * damping, 2.0 * damping_next / half_width))
        damping = damping_next
    return factors


def neighbours(padded):
    return (padded[2:, 1:-1, 1:-1], padded[:-2, 1:-1, 1:-1], padded[1:-1, 2:, 1:-1],
            padded[1:-1, :-2, 1:-1], padded[1:-1, 1:-1, 2:], padded[1:-1, 1:-1, :-2])


def apply_operator(field_padded, coeff_padded, factor):
    centre_field = field_padded[1:-1, 1:-1, 1:-1]
    centre_coeff = coeff_padded[1:-1, 1:-1, 1:-1]
    summed = jnp.zeros(centre_field.shape, jnp.float32)
    for field_near, coeff_near in zip(neighbours(field_padded), neighbours(coeff_padded)):
        summed = summed + 0.5 * (centre_coeff + coeff_near) * (centre_field - field_near)
    return factor * summed


def diagonal_of(coeff_padded, factor):
    centre_coeff = coeff_padded[1:-1, 1:-1, 1:-1]
    summed = jnp.zeros(centre_coeff.shape, jnp.float32)
    for coeff_near in neighbours(coeff_padded):
        summed = summed + 0.5 * (centre_coeff + coeff_near)
    return factor * summed


def restrict_field(field):
    summed = field[0::2] + field[1::2]
    summed = summed[:, 0::2] + summed[:, 1::2]
    summed = summed[:, :, 0::2] + summed[:, :, 1::2]
    return 0.125 * summed


def prolong_field(padded):
    result = padded
    for axis_index in range(3):
        length = result.shape[axis_index] - 2
        middle = lax.slice_in_dim(result, 1, length + 1, axis=axis_index)
        preceding = lax.slice_in_dim(result, 0, length, axis=axis_index)
        following = lax.slice_in_dim(result, 2, length + 2, axis=axis_index)
        even_cells = 0.75 * middle + 0.25 * preceding
        odd_cells = 0.75 * middle + 0.25 * following
        joined = jnp.stack((even_cells, odd_cells), axis=axis_index + 1)
        new_shape = list(middle.shape)
        new_shape[axis_index] = 2 * length
        result = joined.reshape(new_shape)
    return result


def pad_zero(field):
    return jnp.pad(field, 1)


def smooth_field(source, initial, coeff_padded, factor, sweeps, want_residual, padder):
    diagonal = diagonal_of(coeff_padded, factor)
    if initial is None:
        residual = source
    else:
        residual = source - apply_operator(padder(initial), coeff_padded, factor)
    factors = chebyshev_factors(sweeps)
    direction = None
    solution = None
    for sweep_index in range(sweeps):
        keep_factor, push_factor = factors[sweep_index]
        if sweep_index > 0:
            residual = residual - apply_operator(padder(direction), coeff_padded, factor)
            direction = keep_factor * direction + push_factor * (residual / diagonal)
        else:
            direction = push_factor * (residual / diagonal)
        if solution is None and initial is None:
            solution = direction
        elif solution is None:
            solution = initial + direction
        else:
            solution = solution + direction
    if want_residual:
        residual = residual - apply_operator(padder(direction), coeff_padded, factor)
    return solution, residual


def reference(right_side, conductivity):
    conducts = [conductivity]
    for level_index in range(LEVELS):
        conducts.append(restrict_field(conducts[level_index]))
    padded_coeffs = [pad_zero(entry) for entry in conducts]
    sources = [right_side]
    presmoothed = []
    for level_index in range(LEVELS):
        factor = 0.25 ** level_index
        solution, residual = smooth_field(sources[level_index], None, padded_coeffs[level_index], factor, STEPS, True, pad_zero)
        presmoothed.append(solution)
        sources.append(restrict_field(residual))
    correction, unused = smooth_field(sources[LEVELS], None, padded_coeffs[LEVELS], 0.25 ** LEVELS, COARSE_STEPS, False, pad_zero)
    residual = sources[0]
    for level_index in reversed(range(LEVELS)):
        initial = presmoothed[level_index] + prolong_field(pad_zero(correction))
        correction, residual = smooth_field(sources[level_index], initial, padded_coeffs[level_index], 0.25 ** level_index, STEPS, level_index == 0, pad_zero)
    return correction, residual
```

```python
import jax
import jax.numpy as jnp
from jax import lax
from jax.experimental import pallas as pl
from jax.experimental.pallas import tpu as pltpu
from jax.sharding import PartitionSpec as P

STEPS = 3
COARSE_STEPS = 8
LOWER_EDGE = 0.3
UPPER_EDGE = 2.0
MESH = pl.DeviceIdType.MESH
LANES = 128
EXCHANGES = 8


def chebyshev_factors(sweeps):
    centre_value = 0.5 * (UPPER_EDGE + LOWER_EDGE)
    half_width = 0.5 * (UPPER_EDGE - LOWER_EDGE)
    ratio_value = centre_value / half_width
    damping = 1.0 / ratio_value
    factors = [(0.0, 1.0 / centre_value)]
    for _ in range(1, sweeps):
        damping_next = 1.0 / (2.0 * ratio_value - damping)
        factors.append((damping_next * damping, 2.0 * damping_next / half_width))
        damping = damping_next
    return factors


def up8(value):
    return -(-value // 8) * 8


class Level:
    def __init__(self, index, nx, ny, nz, shared):
        self.index, self.nx, self.ny, self.nz, self.shared = index, nx, ny, nz, shared
        self.pitch = ny + 2
        self.c0 = up8(self.pitch + 1)
        self.n = up8(nx * self.pitch)
        self.rows = 2 * self.c0 + self.n
        self.zo = 0 if nz == LANES else 1
        self.factor = 0.25**index
        self.wide = nz == LANES and not shared
        if self.wide:
            self.first, self.chunks = self.c0, self.n // 8
        else:
            self.first, self.chunks = 0, self.rows // 8
        self.half = -(-self.chunks // 2) if self.wide else self.chunks

    def scratch(self):
        field = pltpu.VMEM((self.n, LANES), jnp.float32)
        padded = pltpu.VMEM((self.rows, LANES), jnp.float32)
        shapes = {name: field for name in ("xm", "xp", "ym", "yp", "zm", "zp", "dg", "iv", "r", "u", "k")}
        shapes.update({name: padded for name in ("d0", "d1", "v")})
        if not self.shared:
            for name in ("s", "q"):
                shapes[name + "x"] = pltpu.VMEM((EXCHANGES, 2, up8(self.ny), LANES), jnp.float32)
                shapes[name + "y"] = pltpu.VMEM((EXCHANGES, 2, up8(self.nx + 2 * self.zo), LANES), jnp.float32)
            zrows = 16 if self.wide else 8
            shapes["sz"] = pltpu.VMEM((EXCHANGES, zrows, LANES), jnp.float32)
            shapes["qz"] = pltpu.VMEM((EXCHANGES, 2, zrows, LANES), jnp.float32)
            shapes["send"] = pltpu.SemaphoreType.DMA((EXCHANGES, 6))
            shapes["recv"] = pltpu.SemaphoreType.DMA((EXCHANGES, 6))
        return shapes

    def groups(self):
        count = -(-self.n // 96)
        size = up8(-(-self.n // count))
        return [(lo, min(size, self.n - lo)) for lo in range(0, self.n, size)]


def dot(a, b):
    return jnp.dot(a, b, precision=lax.Precision.HIGHEST, preferred_element_type=jnp.float32)


def iota(shape, dim):
    return lax.broadcasted_iota(jnp.int32, shape, dim)


def roll(value, shift):
    shift %= LANES
    return pltpu.roll(value, shift, 1) if shift else value


def build(mesh_shape, box):
    gxn, gyn, gzn = mesh_shape
    bx, by, bz = box
    local = [Level(i, bx >> i, by >> i, bz >> i, False) for i in range(3)]
    cx, cy, cz = bx >> 3, by >> 3, bz >> 3
    three = Level(3, gxn * cx, gyn * cy, gzn * cz, True)
    four = Level(4, three.nx // 2, three.ny // 2, three.nz // 2, True)
    levels = local + [three, four]
    blk = cx * cy
    names = [(lv.index, name) for lv in levels for name in lv.scratch()]
    shapes = [shape for lv in levels for shape in lv.scratch().values()]
    extra = {
        "t": pltpu.VMEM((max(lv.rows for lv in levels), LANES), jnp.float32),
        "te": pltpu.VMEM((max(lv.n for lv in levels[1:]) + 16, LANES), jnp.float32),
        "to": pltpu.VMEM((max(lv.n for lv in levels[1:]) + 16, LANES), jnp.float32),
        "half": pltpu.VMEM((128, LANES), jnp.float32),
        "zs": pltpu.VMEM((2, blk, LANES), jnp.float32),
        "zr": pltpu.VMEM((2, gzn, blk, LANES), jnp.float32),
        "ps": pltpu.VMEM((2, blk, LANES), jnp.float32),
        "pr": pltpu.VMEM((2, gxn * gyn, blk, LANES), jnp.float32),
        "zsend": pltpu.SemaphoreType.DMA((2, gzn)),
        "zrecv": pltpu.SemaphoreType.DMA((2, gzn)),
        "psend": pltpu.SemaphoreType.DMA((2, gxn * gyn)),
        "precv": pltpu.SemaphoreType.DMA((2, gxn * gyn)),
    }
    names += [(None, name) for name in extra]
    shapes += list(extra.values())

    def kernel(b_ref, k_ref, u_ref, res_ref, *scratch):
        ref = {key: value for key, value in zip(names, scratch)}
        gx, gy, gz = lax.axis_index("gx"), lax.axis_index("gy"), lax.axis_index("gz")
        has = (gx > 0, gx < gxn - 1, gy > 0, gy < gyn - 1, gz > 0, gz < gzn - 1)
        peer = (
            (gx - 1, gy, gz),
            (gx + 1, gy, gz),
            (gx, gy - 1, gz),
            (gx, gy + 1, gz),
            (gx, gy, gz - 1),
            (gx, gy, gz + 1),
        )
        lane = iota((8, LANES), 1)
        plane_peers = [(i, j) for i in range(gxn) for j in range(gyn) if i or j]

        def plane_peer(i, j):
            return lax.rem(gx + i, gxn), lax.rem(gy + j, gyn)

        def depth_peer(k):
            return lax.rem(gz + k, gzn)

        for lv in levels:
            for name in ("d0", "d1", "v"):
                ref[lv.index, name][...] = jnp.zeros((lv.rows, LANES), jnp.float32)
            if not lv.shared:
                for name in ("qx", "qy", "qz", "sx", "sy"):
                    target = ref[lv.index, name]
                    target[...] = jnp.zeros(target.shape, jnp.float32)

        barrier = pltpu.get_barrier_semaphore()
        for i, j in plane_peers:
            px, py = plane_peer(i, j)
            pl.semaphore_signal(barrier, inc=1, device_id=(px, py, gz), device_id_type=MESH)
        for k in range(1, gzn):
            pl.semaphore_signal(barrier, inc=1, device_id=(gx, gy, depth_peer(k)), device_id_type=MESH)

        counters = [0, 0, 0]

        def link(lv, slot, way):
            axis, side = "xyz"[way // 2], way % 2
            source = ref[lv.index, "s" + axis].at[slot]
            if axis != "z":
                source = source.at[side]
            return pltpu.make_async_remote_copy(
                src_ref=source,
                dst_ref=ref[lv.index, "q" + axis].at[slot, 1 - side],
                send_sem=ref[lv.index, "send"].at[slot, way],
                recv_sem=ref[lv.index, "recv"].at[slot, way ^ 1],
                device_id=peer[way],
                device_id_type=MESH,
            )

        def incoming(lv, slot, way):
            axis, side = "xyz"[way // 2], way % 2
            source = ref[lv.index, "s" + axis].at[slot]
            if axis != "z":
                source = source.at[side]
            return pltpu.make_async_remote_copy(
                src_ref=source,
                dst_ref=ref[lv.index, "q" + axis].at[slot, side],
                send_sem=ref[lv.index, "send"].at[slot, way],
                recv_sem=ref[lv.index, "recv"].at[slot, way],
                device_id=peer[way],
                device_id_type=MESH,
            )

        def start(lv, slot, ways):
            for way in ways:

                @pl.when(has[way])
                def _():
                    link(lv, slot, way).start()

        def finish(lv, slot, ways):
            for way in ways:

                @pl.when(has[way])
                def _():
                    incoming(lv, slot, way).wait_recv()

        def stage_x(lv, buf, slot):
            out = ref[lv.index, "sx"]
            out[slot, 0, pl.ds(0, lv.ny), :] = buf[pl.ds(lv.c0 + 1, lv.ny), :]
            out[slot, 1, pl.ds(0, lv.ny), :] = buf[pl.ds(lv.c0 + (lv.nx - 1) * lv.pitch + 1, lv.ny), :]

        def place_x(lv, buf, slot):
            got = ref[lv.index, "qx"]
            buf[pl.ds(lv.c0 - lv.pitch + 1, lv.ny), :] = got[slot, 0, pl.ds(0, lv.ny), :]
            buf[pl.ds(lv.c0 + lv.nx * lv.pitch + 1, lv.ny), :] = got[slot, 1, pl.ds(0, lv.ny), :]

        def y_span(lv, wide):
            return lv.c0 - wide * lv.pitch, lv.nx + 2 * wide

        def stage_y(lv, buf, slot, wide):
            base, count = y_span(lv, wide)
            out = ref[lv.index, "sy"]
            out[slot, 0, pl.ds(0, count), :] = buf[pl.ds(base + 1, count, stride=lv.pitch), :]
            out[slot, 1, pl.ds(0, count), :] = buf[pl.ds(base + lv.ny, count, stride=lv.pitch), :]

        def place_y(lv, buf, slot, wide):
            base, count = y_span(lv, wide)
            got = ref[lv.index, "qy"]
            buf[pl.ds(base, count, stride=lv.pitch), :] = got[slot, 0, pl.ds(0, count), :]
            buf[pl.ds(base + lv.pitch - 1, count, stride=lv.pitch), :] = got[slot, 1, pl.ds(0, count), :]

        def stage_z(lv, buf, slot):
            out = ref[lv.index, "sz"]
            packed = jnp.zeros((8, LANES), jnp.float32)
            for c in range(lv.chunks):
                cc = c % lv.half
                value = buf[pl.ds(lv.first + 8 * c, 8), :]
                if lv.wide:
                    packed = jnp.where(lane >= 2 * cc, roll(value, 2 * cc + 1), packed)
                else:
                    mine = (lane == 1 + 2 * cc) | (lane == lv.nz + 2 * cc)
                    packed = jnp.where(mine, roll(value, 2 * cc), packed)
                if cc == lv.half - 1 or c == lv.chunks - 1:
                    out[slot, pl.ds(8 * (c // lv.half), 8), :] = packed

        def place_z(lv, buf, slot):
            got = ref[lv.index, "qz"]
            if lv.wide:
                even = lane % 2 == 0
                return [
                    jnp.where(even, got[slot, 0, pl.ds(8 * h, 8), :], roll(got[slot, 1, pl.ds(8 * h, 8), :], -2))
                    for h in range(2)
                ]
            merged = jnp.where(
                lane <= lv.nz, roll(got[slot, 0], -lv.nz), roll(got[slot, 1], lv.nz)
            )
            edge = (lane == 0) | (lane == lv.nz + 1)
            for c in range(lv.chunks):
                span = pl.ds(8 * c, 8)
                buf[span, :] = jnp.where(edge, roll(merged, -2 * c), buf[span, :])
            return None

        def begin_faces(lv, buf):
            slot = counters[lv.index]
            counters[lv.index] += 1
            stage_x(lv, buf, slot)
            start(lv, slot, (0, 1))
            stage_y(lv, buf, slot, 0)
            start(lv, slot, (2, 3))
            stage_z(lv, buf, slot)
            start(lv, slot, (4, 5))
            return slot

        def end_faces(lv, buf, slot):
            finish(lv, slot, range(6))
            place_x(lv, buf, slot)
            place_y(lv, buf, slot, 0)
            return place_z(lv, buf, slot)

        def faces(lv, buf):
            if lv.shared:
                return None
            return end_faces(lv, buf, begin_faces(lv, buf))

        def corners(lv, buf):
            slot = counters[lv.index]
            counters[lv.index] += 1
            stage_x(lv, buf, slot)
            start(lv, slot, (0, 1))
            finish(lv, slot, (0, 1))
            place_x(lv, buf, slot)
            stage_y(lv, buf, slot, 1)
            start(lv, slot, (2, 3))
            finish(lv, slot, (2, 3))
            place_y(lv, buf, slot, 1)
            stage_z(lv, buf, slot)
            start(lv, slot, (4, 5))
            finish(lv, slot, (4, 5))
            place_z(lv, buf, slot)

        def sides(lv, mid, lo, rows, halo):
            below, above = roll(mid, 1), roll(mid, -1)
            if lv.wide:
                edge = jnp.concatenate(
                    [
                        roll(halo[c // lv.half], -2 * (c % lv.half))
                        for c in range(lo // 8, (lo + rows) // 8)
                    ],
                    axis=0,
                )
                where = iota((rows, LANES), 1)
                below = jnp.where(where == 0, edge, below)
                above = jnp.where(where == LANES - 1, edge, above)
            return below, above

        def around(lv, buf, lo, rows, halo):
            base = lv.c0 + lo
            mid = buf[pl.ds(base, rows), :]
            below, above = sides(lv, mid, lo, rows, halo)
            return mid, (
                buf[pl.ds(base - lv.pitch, rows), :],
                buf[pl.ds(base + lv.pitch, rows), :],
                buf[pl.ds(base - 1, rows), :],
                buf[pl.ds(base + 1, rows), :],
                below,
                above,
            )

        coeff_names = ("xm", "xp", "ym", "yp", "zm", "zp")

        def applied(lv, buf, lo, rows, halo):
            mid, near = around(lv, buf, lo, rows, halo)
            span = pl.ds(lo, rows)
            total = mid
            for name, value in zip(coeff_names, near):
                total = total - ref[lv.index, name][span, :] * value
            return mid, total

        def prepare(lv, buf, halo):
            keep = ref[lv.index, "k"]
            keep[...] = jnp.ones((lv.n, LANES), jnp.float32)
            keep[pl.ds(0, lv.nx, stride=lv.pitch), :] = jnp.zeros((lv.nx, LANES), jnp.float32)
            keep[pl.ds(lv.pitch - 1, lv.nx, stride=lv.pitch), :] = jnp.zeros((lv.nx, LANES), jnp.float32)
            for lo, rows in lv.groups():
                span = pl.ds(lo, rows)
                mid, near = around(lv, buf, lo, rows, halo)
                where = iota((rows, LANES), 1)
                near = list(near)
                if lv.shared and lv.nz == LANES:
                    near[4] = jnp.where(where == 0, 0.0, near[4])
                    near[5] = jnp.where(where == LANES - 1, 0.0, near[5])
                inside = keep[span, :] > 0.5
                if lv.nz < LANES:
                    inside = inside & (where >= lv.zo) & (where < lv.nz + lv.zo)
                couple = [(0.5 * lv.factor) * (mid + value) for value in near]
                diagonal = couple[0]
                for value in couple[1:]:
                    diagonal = diagonal + value
                inverse = jnp.where(inside, 1.0 / diagonal, 0.0)
                ref[lv.index, "dg"][span, :] = diagonal
                ref[lv.index, "iv"][span, :] = inverse
                couple = [value * inverse for value in couple]
                if lv.shared and lv.nz == LANES:
                    couple[4] = jnp.where(where == 0, 0.0, couple[4])
                    couple[5] = jnp.where(where == LANES - 1, 0.0, couple[5])
                for name, value in zip(coeff_names, couple):
                    ref[lv.index, name][span, :] = value

        def sweeps(lv, src, first, count, final, lift):
            factors = chebyshev_factors(count)
            r, u = ref[lv.index, "r"], ref[lv.index, "u"]
            buffers = [ref[lv.index, "d0"], ref[lv.index, "d1"]]
            held = src
            for step in range(count):
                keep, push = factors[step]
                target = buffers[step % 2]
                halo = faces(lv, held) if held is not None else None
                for lo, rows in lv.groups():
                    span = pl.ds(lo, rows)
                    value = r[span, :]
                    if held is not None:
                        mid, change = applied(lv, held, lo, rows, halo)
                        value = value - change
                        r[span, :] = value
                    direction = push * value
                    if step > 0:
                        direction = direction + keep * mid
                    target[pl.ds(lv.c0 + lo, rows), :] = direction
                    if step == 0 and src is None:
                        u[span, :] = direction
                    elif step == 0:
                        u[span, :] = u[span, :] + mid + direction
                    else:
                        u[span, :] = u[span, :] + direction
                held = target
            if final:
                halo = faces(lv, held)
                for lo, rows in lv.groups():
                    span = pl.ds(lo, rows)
                    mid, change = applied(lv, held, lo, rows, halo)
                    r[span, :] = r[span, :] - change
            return held

        def halve(lv, buf, base):
            out = ref[None, "half"]
            nx, ny = lv.nx // 2, lv.ny // 2
            for x in range(nx):
                total = None
                for px in range(2):
                    for py in range(2):
                        at = base + (2 * x + px) * lv.pitch + 1 + py
                        value = buf[pl.ds(at, ny, stride=2), :]
                        total = value if total is None else total + value
                out[pl.ds(x * ny, ny), :] = total
            return nx, ny

        def pair_matrix(lv, offset):
            fine, coarse = iota((LANES, LANES), 0), iota((LANES, LANES), 1)
            cell = fine - lv.zo
            inside = (cell >= 0) & (cell < lv.nz)
            match = lax.shift_right_arithmetic(cell, 1) + offset == coarse
            return jnp.where(inside & match, 0.125, 0.0)

        def restrict(lv, buf, base, offset):
            nx, ny = halve(lv, buf, base)
            return nx, ny, dot(ref[None, "half"][pl.ds(0, up8(nx * ny)), :], pair_matrix(lv, offset))

        def spread(nx, ny, value, coarse, buf, base):
            scratch_ref = ref[None, "half"]
            scratch_ref[pl.ds(0, up8(nx * ny)), :] = value
            for x in range(nx):
                buf[pl.ds(base + x * coarse.pitch + 1, ny), :] = scratch_ref[pl.ds(x * ny, ny), :]

        def stretch(cell, offset):
            coarse = iota((LANES, LANES), 0) - offset
            parent = lax.shift_right_arithmetic(cell, 1)
            other = parent + 2 * (cell & 1) - 1
            return jnp.where(coarse == parent, 0.75, 0.0) + jnp.where(coarse == other, 0.25, 0.0)

        def prolong(rows, pitch, c0, nx, ny, weights, value, fine, buf):
            t, te, to = ref[None, "t"], ref[None, "te"], ref[None, "to"]
            t[pl.ds(0, rows), :] = dot(value, weights)
            n = nx * pitch
            mid = t[pl.ds(c0, n), :]
            te[pl.ds(0, n), :] = 0.75 * mid + 0.25 * t[pl.ds(c0 - pitch, n), :]
            to[pl.ds(0, n), :] = 0.75 * mid + 0.25 * t[pl.ds(c0 + pitch, n), :]
            for x in range(nx):
                for px, src in ((0, te), (1, to)):
                    at = x * pitch + 1
                    mid = 0.75 * src[pl.ds(at, ny), :]
                    to_row = fine.c0 + (2 * x + px) * fine.pitch + 1
                    buf[pl.ds(to_row, ny, stride=2), :] = mid + 0.25 * src[pl.ds(at - 1, ny), :]
                    buf[pl.ds(to_row + 1, ny, stride=2), :] = mid + 0.25 * src[pl.ds(at + 1, ny), :]

        def columns(fine):
            return iota((LANES, LANES), 1) - fine.zo

        def masked(fine, weights):
            cell = columns(fine)
            return jnp.where((cell >= 0) & (cell < fine.nz), weights, 0.0)

        def depth_copy(which, k):
            return pltpu.make_async_remote_copy(
                src_ref=ref[None, "zs"].at[which],
                dst_ref=ref[None, "zr"].at[which, gz],
                send_sem=ref[None, "zsend"].at[which, k],
                recv_sem=ref[None, "zrecv"].at[which, k],
                device_id=(gx, gy, depth_peer(k)),
                device_id_type=MESH,
            )

        def depth_arrival(which, k):
            source = lax.rem(gz + gzn - k, gzn)
            return pltpu.make_async_remote_copy(
                src_ref=ref[None, "zs"].at[which],
                dst_ref=ref[None, "zr"].at[which, source],
                send_sem=ref[None, "zsend"].at[which, k],
                recv_sem=ref[None, "zrecv"].at[which, k],
                device_id=(gx, gy, depth_peer(k)),
                device_id_type=MESH,
            )

        def plane_copy(which, i, j):
            px, py = plane_peer(i, j)
            return pltpu.make_async_remote_copy(
                src_ref=ref[None, "ps"].at[which],
                dst_ref=ref[None, "pr"].at[which, gx * gyn + gy],
                send_sem=ref[None, "psend"].at[which, i * gyn + j],
                recv_sem=ref[None, "precv"].at[which, i * gyn + j],
                device_id=(px, py, gz),
                device_id_type=MESH,
            )

        def plane_arrival(which, i, j):
            sx, sy = lax.rem(gx + gxn - i, gxn), lax.rem(gy + gyn - j, gyn)
            px, py = plane_peer(i, j)
            return pltpu.make_async_remote_copy(
                src_ref=ref[None, "ps"].at[which],
                dst_ref=ref[None, "pr"].at[which, sx * gyn + sy],
                send_sem=ref[None, "psend"].at[which, i * gyn + j],
                recv_sem=ref[None, "precv"].at[which, i * gyn + j],
                device_id=(px, py, gz),
                device_id_type=MESH,
            )

        def gather_depth_start(which, block):
            ref[None, "zs"][which] = block[:blk]
            for k in range(1, gzn):
                depth_copy(which, k).start()

        def gather_plane_start(which):
            total = ref[None, "zs"][which]
            for k in range(1, gzn):
                depth_arrival(which, k).wait_recv()
            for k in range(1, gzn):
                total = total + ref[None, "zr"][which, lax.rem(gz + k, gzn)]
            ref[None, "ps"][which] = total
            for i, j in plane_peers:
                plane_copy(which, i, j).start()
            ref[None, "pr"][which, gx * gyn + gy] = total

        def gather_end(which, buf, base):
            for i, j in plane_peers:
                plane_arrival(which, i, j).wait_recv()
            for i in range(gxn):
                for x in range(cx):
                    for y in range(cy):
                        rows = [ref[None, "pr"][which, i * gyn + j, pl.ds(x * cy + y, 1), :] for j in range(gyn)]
                        at = base + (i * cx + x) * three.pitch + 1 + y
                        buf[pl.ds(at, gyn, stride=cy), :] = jnp.concatenate(rows, axis=0)

        def gather_waits():
            for which in range(2):
                for k in range(1, gzn):
                    depth_copy(which, k).wait_send()
                for i, j in plane_peers:
                    plane_copy(which, i, j).wait_send()

        first = local[0]
        for x in range(first.nx):
            ref[0, "v"][pl.ds(first.c0 + x * first.pitch + 1, first.ny), :] = k_ref[x]
        for index in range(2):
            fine, coarse = local[index], local[index + 1]
            nx, ny, value = restrict(fine, ref[index, "v"], fine.c0, coarse.zo)
            spread(nx, ny, value, coarse, ref[index + 1, "v"], coarse.c0)
        last = local[2]
        _, _, k_block = restrict(last, ref[2, "v"], last.c0, gz * cz + three.zo)

        pl.semaphore_wait(barrier, len(plane_peers) + gzn - 1)

        slots = [begin_faces(lv, ref[lv.index, "v"]) for lv in local]
        gather_depth_start(0, k_block)
        for x in range(first.nx):
            ref[0, "r"][pl.ds(x * first.pitch + 1, first.ny), :] = b_ref[x]
        halo = end_faces(local[0], ref[0, "v"], slots[0])
        prepare(local[0], ref[0, "v"], halo)
        for lv in local[1:]:
            end_faces(lv, ref[lv.index, "v"], slots[lv.index])
            prepare(lv, ref[lv.index, "v"], None)
        gather_plane_start(0)

        zero_edge = jnp.zeros((first.nx, LANES), jnp.float32)
        for at in (0, first.pitch - 1):
            ref[0, "r"][pl.ds(at, first.nx, stride=first.pitch), :] = zero_edge
        for lv in local:
            r, dg, iv = (ref[lv.index, name] for name in ("r", "dg", "iv"))
            r[...] = r[...] * iv[...]
            sweeps(lv, None, True, STEPS, True, False)
            residual = ref[lv.index, "v"]
            residual[pl.ds(lv.c0, lv.n), :] = r[...] * dg[...]
            if lv.index < 2:
                coarse = local[lv.index + 1]
                nx, ny, value = restrict(lv, residual, lv.c0, coarse.zo)
                ref[coarse.index, "r"][...] = jnp.zeros((coarse.n, LANES), jnp.float32)
                spread(nx, ny, value, coarse, ref[coarse.index, "r"], 0)
        _, _, b_block = restrict(last, ref[2, "v"], last.c0, gz * cz + three.zo)
        gather_depth_start(1, b_block)
        gather_end(0, ref[3, "v"], three.c0)
        prepare(three, ref[3, "v"], None)
        nx, ny, value = restrict(three, ref[3, "v"], three.c0, four.zo)
        spread(nx, ny, value, four, ref[4, "v"], four.c0)
        prepare(four, ref[4, "v"], None)
        ref[3, "r"][...] = jnp.zeros((three.n, LANES), jnp.float32)
        ref[4, "r"][...] = jnp.zeros((four.n, LANES), jnp.float32)
        gather_plane_start(1)
        gather_end(1, ref[3, "r"], 0)

        r3, r4 = ref[3, "r"], ref[4, "r"]
        r3[...] = r3[...] * ref[3, "iv"][...]
        sweeps(three, None, True, STEPS, True, False)
        ref[3, "v"][pl.ds(three.c0, three.n), :] = r3[...] * ref[3, "dg"][...]
        nx, ny, value = restrict(three, ref[3, "v"], three.c0, four.zo)
        spread(nx, ny, value, four, r4, 0)
        r4[...] = r4[...] * ref[4, "iv"][...]
        sweeps(four, None, True, COARSE_STEPS, False, False)

        ref[4, "v"][pl.ds(four.c0, four.n), :] = ref[4, "u"][...]
        prolong(
            four.rows, four.pitch, four.c0, four.nx, four.ny,
            masked(three, stretch(columns(three), four.zo)), ref[4, "v"][...], three, ref[3, "v"],
        )
        for at in (0, three.pitch - 1):
            ref[3, "v"][pl.ds(three.c0 + at, three.nx, stride=three.pitch), :] = jnp.zeros(
                (three.nx, LANES), jnp.float32
            )
        sweeps(three, ref[3, "v"], True, STEPS, False, False)
        ref[3, "v"][pl.ds(three.c0, three.n), :] = ref[3, "u"][...]

        pitch = cy + 2
        picked = up8((cx + 2) * pitch)
        row, source = iota((picked, three.rows), 0), iota((picked, three.rows), 1)
        box_x = row // pitch
        wanted = three.c0 + (gx * cx - 1 + box_x) * three.pitch + gy * cy + (row - box_x * pitch)
        window = dot(jnp.where(source == wanted, 1.0, 0.0), ref[3, "v"][...])
        weights = stretch(columns(last) + gz * last.nz, three.zo)
        prolong(picked, pitch, pitch, cx, cy, masked(last, weights), window, last, ref[2, "v"])
        for lv in reversed(local):
            sweeps(lv, ref[lv.index, "v"], True, STEPS, lv.index == 0, False)
            if lv.index:
                field = ref[lv.index, "v"]
                field[pl.ds(lv.c0, lv.n), :] = ref[lv.index, "u"][...]
                corners(lv, field)
                fine = local[lv.index - 1]
                weights = masked(fine, stretch(columns(fine), lv.zo))
                prolong(lv.rows, lv.pitch, lv.c0, lv.nx, lv.ny, weights, field[...], fine, ref[fine.index, "v"])

        for x in range(first.nx):
            span = pl.ds(x * first.pitch + 1, first.ny)
            u_ref[x] = ref[0, "u"][span, :]
            res_ref[x] = ref[0, "r"][span, :] * ref[0, "dg"][span, :]

        for lv in local:
            for slot in range(counters[lv.index]):
                for way in range(6):

                    @pl.when(has[way])
                    def _():
                        link(lv, slot, way).wait_send()

        gather_waits()

    def on_device(right_side, conductivity):
        out = jax.ShapeDtypeStruct(box, jnp.float32)
        return pl.pallas_call(
            kernel,
            out_shape=(out, out),
            in_specs=[pl.BlockSpec(memory_space=pltpu.VMEM)] * 2,
            out_specs=[pl.BlockSpec(memory_space=pltpu.VMEM)] * 2,
            scratch_shapes=shapes,
            compiler_params=pltpu.CompilerParams(
                collective_id=0, has_side_effects=True, vmem_limit_bytes=48 * 1024 * 1024
            ),
        )(right_side, conductivity)

    return on_device


def solution(mesh):
    sizes = tuple(mesh.shape[axis] for axis in ("gx", "gy", "gz"))
    spec = P("gx", "gy", "gz")
    return jax.shard_map(
        build(sizes, (32, 16, 128)), mesh=mesh, in_specs=(spec, spec), out_specs=(spec, spec), check_vma=False
    )
```

```python
import jax
import jax.numpy as jnp
from jax import lax
from jax.experimental import pallas as pl
from jax.experimental.pallas import tpu as pltpu
from jax.sharding import PartitionSpec as P

STEPS = 3
COARSE_STEPS = 8
LOWER_EDGE = 0.3
UPPER_EDGE = 2.0
MESH = pl.DeviceIdType.MESH
LANES = 128
EXCHANGES = 8
DEEP = 4
HALO = 4
OFFSETS = [(i, j, k) for i in (-1, 0, 1) for j in (-1, 0, 1) for k in (-1, 0, 1) if i or j or k]
EDGES = [offset for offset in OFFSETS if offset[2]]


def chebyshev_factors(sweeps):
    centre_value = 0.5 * (UPPER_EDGE + LOWER_EDGE)
    half_width = 0.5 * (UPPER_EDGE - LOWER_EDGE)
    ratio_value = centre_value / half_width
    damping = 1.0 / ratio_value
    factors = [(0.0, 1.0 / centre_value)]
    for _ in range(1, sweeps):
        damping_next = 1.0 / (2.0 * ratio_value - damping)
        factors.append((damping_next * damping, 2.0 * damping_next / half_width))
        damping = damping_next
    return factors


def up8(value):
    return -(-value // 8) * 8


class Level:
    def __init__(self, index, nx, ny, nz, h, shared):
        self.index, self.nx, self.ny, self.nz, self.h, self.shared = index, nx, ny, nz, h, shared
        self.pitch = ny + 2 * h
        self.c0 = up8(self.pitch + 1)
        self.n = up8((nx + 2 * h - 2) * self.pitch)
        self.rows = self.c0 + self.n + up8(self.pitch + 1)
        self.zo = 0 if nz == LANES else h
        self.factor = 0.25**index
        self.wide = nz == LANES and not shared
        self.deep = h > 1
        self.chunks = self.n // 8
        self.half = -(-self.chunks // 2)

    def row(self, x, y):
        return self.c0 + (x + self.h - 1) * self.pitch + y + self.h

    def scratch(self):
        field = pltpu.VMEM((self.n, LANES), jnp.float32)
        padded = pltpu.VMEM((self.rows, LANES), jnp.float32)
        shapes = {name: field for name in ("xm", "xp", "ym", "yp", "zm", "zp", "dg", "iv", "r", "u")}
        shapes.update({name: padded for name in ("d0", "d1", "v", "w")})
        count = EXCHANGES
        if self.deep:
            for name in ("s", "q"):
                shapes[name + "x"] = pltpu.VMEM((DEEP, 2, self.h * self.ny, LANES), jnp.float32)
                shapes[name + "y"] = pltpu.VMEM((DEEP, 2, self.h * self.nx, LANES), jnp.float32)
                shapes[name + "c"] = pltpu.VMEM((DEEP, 4, self.h * self.h, LANES), jnp.float32)
            shapes["sz"] = pltpu.VMEM((DEEP, 8, LANES), jnp.float32)
            shapes["qz"] = pltpu.VMEM((DEEP, 18, 8, LANES), jnp.float32)
            shapes["zone"] = pltpu.VMEM((6, up8(self.pitch), LANES), jnp.float32)
            shapes["send"] = pltpu.SemaphoreType.DMA((DEEP, 26))
            shapes["recv"] = pltpu.SemaphoreType.DMA((DEEP, 26))
        elif not self.shared:
            for name in ("s", "q"):
                shapes[name + "x"] = pltpu.VMEM((count, 2, self.ny, LANES), jnp.float32)
                shapes[name + "y"] = pltpu.VMEM((count, 2, self.nx, LANES), jnp.float32)
            shapes["sz"] = pltpu.VMEM((count, 16, LANES), jnp.float32)
            shapes["qz"] = pltpu.VMEM((count, 2, 16, LANES), jnp.float32)
            shapes["send"] = pltpu.SemaphoreType.DMA((count, 6))
            shapes["recv"] = pltpu.SemaphoreType.DMA((count, 6))
        return shapes

    def groups(self):
        count = -(-self.n // 96)
        size = up8(-(-self.n // count))
        return [(lo, min(size, self.n - lo)) for lo in range(0, self.n, size)]


def dot(a, b):
    return jnp.dot(a, b, precision=lax.Precision.HIGHEST, preferred_element_type=jnp.float32)


def iota(shape, dim):
    return lax.broadcasted_iota(jnp.int32, shape, dim)


def roll(value, shift):
    shift %= LANES
    return pltpu.roll(value, shift, 1) if shift else value


def build(mesh_shape, box):
    gxn, gyn, gzn = mesh_shape
    bx, by, bz = box
    local = [Level(i, bx >> i, by >> i, bz >> i, HALO if i else 1, False) for i in range(3)]
    cx, cy, cz = bx >> 3, by >> 3, bz >> 3
    three = Level(3, gxn * cx, gyn * cy, gzn * cz, 1, True)
    four = Level(4, three.nx // 2, three.ny // 2, three.nz // 2, 1, True)
    levels = local + [three, four]
    blk = cx * cy
    names = [(lv.index, name) for lv in levels for name in lv.scratch()]
    shapes = [shape for lv in levels for shape in lv.scratch().values()]
    extra = {
        "t": pltpu.VMEM((max(lv.rows for lv in levels), LANES), jnp.float32),
        "te": pltpu.VMEM((max(lv.n for lv in levels) + 16, LANES), jnp.float32),
        "to": pltpu.VMEM((max(lv.n for lv in levels) + 16, LANES), jnp.float32),
        "half": pltpu.VMEM((128, LANES), jnp.float32),
        "zs": pltpu.VMEM((2, blk, LANES), jnp.float32),
        "zr": pltpu.VMEM((2, gzn, blk, LANES), jnp.float32),
        "ps": pltpu.VMEM((2, blk, LANES), jnp.float32),
        "pr": pltpu.VMEM((2, gxn * gyn, blk, LANES), jnp.float32),
        "zsend": pltpu.SemaphoreType.DMA((2, gzn)),
        "zrecv": pltpu.SemaphoreType.DMA((2, gzn)),
        "psend": pltpu.SemaphoreType.DMA((2, gxn * gyn)),
        "precv": pltpu.SemaphoreType.DMA((2, gxn * gyn)),
    }
    names += [(None, name) for name in extra]
    shapes += list(extra.values())

    def kernel(b_ref, k_ref, u_ref, res_ref, *scratch):
        ref = {key: value for key, value in zip(names, scratch)}
        gx, gy, gz = lax.axis_index("gx"), lax.axis_index("gy"), lax.axis_index("gz")
        has = (gx > 0, gx < gxn - 1, gy > 0, gy < gyn - 1, gz > 0, gz < gzn - 1)
        peer = (
            (gx - 1, gy, gz),
            (gx + 1, gy, gz),
            (gx, gy - 1, gz),
            (gx, gy + 1, gz),
            (gx, gy, gz - 1),
            (gx, gy, gz + 1),
        )
        lane = iota((8, LANES), 1)
        plane_peers = [(i, j) for i in range(gxn) for j in range(gyn) if i or j]

        def plane_peer(i, j):
            return lax.rem(gx + i, gxn), lax.rem(gy + j, gyn)

        def depth_peer(k):
            return lax.rem(gz + k, gzn)

        for lv in levels:
            for name in ("d0", "d1", "v", "w"):
                ref[lv.index, name][...] = jnp.zeros((lv.rows, LANES), jnp.float32)
            if not lv.shared:
                for name in ("qx", "qy", "qz") + (("qc",) if lv.deep else ()):
                    target = ref[lv.index, name]
                    target[...] = jnp.zeros(target.shape, jnp.float32)

        barrier = pltpu.get_barrier_semaphore()
        for i, j in plane_peers:
            px, py = plane_peer(i, j)
            pl.semaphore_signal(barrier, inc=1, device_id=(px, py, gz), device_id_type=MESH)
        for k in range(1, gzn):
            pl.semaphore_signal(barrier, inc=1, device_id=(gx, gy, depth_peer(k)), device_id_type=MESH)

        counters = [0, 0, 0]
        at = (gx, gy, gz)
        sizes = (gxn, gyn, gzn)

        def there(offset):
            found = jnp.bool_(True)
            for a in range(3):
                if offset[a] < 0:
                    found = found & (at[a] > 0)
                elif offset[a] > 0:
                    found = found & (at[a] < sizes[a] - 1)
            return found

        exists = {offset: there(offset) for offset in OFFSETS}

        def device(offset):
            return tuple(at[a] + offset[a] for a in range(3))

        diagonal = [offset for offset in EDGES if offset[0] or offset[1]]
        for offset in diagonal:
            around_edge = tuple(lax.rem(at[a] + offset[a] + sizes[a], sizes[a]) for a in range(3))
            pl.semaphore_signal(barrier, inc=1, device_id=around_edge, device_id_type=MESH)

        def link(lv, slot, way):
            axis, side = "xyz"[way // 2], way % 2
            source = ref[lv.index, "s" + axis].at[slot]
            if axis != "z":
                source = source.at[side]
            return pltpu.make_async_remote_copy(
                src_ref=source,
                dst_ref=ref[lv.index, "q" + axis].at[slot, 1 - side],
                send_sem=ref[lv.index, "send"].at[slot, way],
                recv_sem=ref[lv.index, "recv"].at[slot, way ^ 1],
                device_id=peer[way],
                device_id_type=MESH,
            )

        def incoming(lv, slot, way):
            axis, side = "xyz"[way // 2], way % 2
            source = ref[lv.index, "s" + axis].at[slot]
            if axis != "z":
                source = source.at[side]
            return pltpu.make_async_remote_copy(
                src_ref=source,
                dst_ref=ref[lv.index, "q" + axis].at[slot, side],
                send_sem=ref[lv.index, "send"].at[slot, way],
                recv_sem=ref[lv.index, "recv"].at[slot, way],
                device_id=peer[way],
                device_id_type=MESH,
            )

        def start(lv, slot, ways):
            for way in ways:

                @pl.when(has[way])
                def _():
                    link(lv, slot, way).start()

        def finish(lv, slot, ways):
            for way in ways:

                @pl.when(has[way])
                def _():
                    incoming(lv, slot, way).wait_recv()

        def begin_faces(lv, buf):
            slot = counters[lv.index]
            counters[lv.index] += 1
            out = ref[lv.index, "sx"]
            out[slot, 0] = buf[pl.ds(lv.row(0, 0), lv.ny), :]
            out[slot, 1] = buf[pl.ds(lv.row(lv.nx - 1, 0), lv.ny), :]
            start(lv, slot, (0, 1))
            out = ref[lv.index, "sy"]
            out[slot, 0] = buf[pl.ds(lv.row(0, 0), lv.nx, stride=lv.pitch), :]
            out[slot, 1] = buf[pl.ds(lv.row(0, lv.ny - 1), lv.nx, stride=lv.pitch), :]
            start(lv, slot, (2, 3))
            out = ref[lv.index, "sz"]
            packed = jnp.zeros((8, LANES), jnp.float32)
            for c in range(lv.chunks):
                cc = c % lv.half
                value = buf[pl.ds(lv.c0 + 8 * c, 8), :]
                packed = jnp.where(lane >= 2 * cc, roll(value, 2 * cc + 1), packed)
                if cc == lv.half - 1 or c == lv.chunks - 1:
                    out[slot, pl.ds(8 * (c // lv.half), 8), :] = packed
            start(lv, slot, (4, 5))
            return slot

        def end_faces(lv, buf, slot):
            finish(lv, slot, range(6))
            got = ref[lv.index, "qx"]
            buf[pl.ds(lv.row(-1, 0), lv.ny), :] = got[slot, 0]
            buf[pl.ds(lv.row(lv.nx, 0), lv.ny), :] = got[slot, 1]
            got = ref[lv.index, "qy"]
            buf[pl.ds(lv.row(0, -1), lv.nx, stride=lv.pitch), :] = got[slot, 0]
            buf[pl.ds(lv.row(0, lv.ny), lv.nx, stride=lv.pitch), :] = got[slot, 1]
            got = ref[lv.index, "qz"]
            even = lane % 2 == 0
            return [
                jnp.where(even, got[slot, 0, pl.ds(8 * h, 8), :], roll(got[slot, 1, pl.ds(8 * h, 8), :], -2))
                for h in range(2)
            ]

        def faces(lv, buf):
            return end_faces(lv, buf, begin_faces(lv, buf)) if lv.wide else None

        def deep_link(lv, slot, offset, arriving):
            i, j, k = offset
            sent = OFFSETS.index(offset)
            landed = sent if arriving else OFFSETS.index((-i, -j, -k))

            def part(kind, which):
                if k:
                    return ref[lv.index, kind + "z"].at[(slot,) if which is None else (slot, which)]
                name = "c" if i and j else "x" if i else "y"
                return ref[lv.index, kind + name].at[slot, which]

            def place(offset):
                if offset[2]:
                    return EDGES.index(offset)
                low_x, low_y = offset[0] > 0, offset[1] > 0
                return 2 * low_x + low_y if offset[0] and offset[1] else int(low_x or low_y)

            return pltpu.make_async_remote_copy(
                src_ref=part("s", None if k else place(offset)),
                dst_ref=part("q", place(OFFSETS[landed])),
                send_sem=ref[lv.index, "send"].at[slot, sent],
                recv_sem=ref[lv.index, "recv"].at[slot, landed],
                device_id=device(offset),
                device_id_type=MESH,
            )

        def deep_start(lv, slot, offsets):
            for offset in offsets:

                @pl.when(exists[offset])
                def _():
                    deep_link(lv, slot, offset, False).start()

        def deep_finish(lv, slot, offsets):
            for offset in offsets:

                @pl.when(exists[offset])
                def _():
                    deep_link(lv, slot, offset, True).wait_recv()

        def near_side(size, direction, h):
            return 0 if direction < 0 else size - h

        def far_side(size, direction, h):
            return -h if direction < 0 else size

        def begin_deep(lv, buf):
            slot = counters[lv.index]
            counters[lv.index] += 1
            h, nx, ny, nz = lv.h, lv.nx, lv.ny, lv.nz
            out = ref[lv.index, "sz"]
            packed = jnp.zeros((ny, LANES), jnp.float32)
            where = iota((ny, LANES), 1)
            for x in range(nx):
                value = buf[pl.ds(lv.row(x, 0), ny), :]
                low = 2 * h * x
                packed = jnp.where(where >= low, roll(value, low - h), packed)
                packed = jnp.where(where >= low + h, roll(value, low + h - nz), packed)
            out[slot, pl.ds(0, ny), :] = packed
            if ny < 8:
                out[slot, pl.ds(ny, 8 - ny), :] = packed[: 8 - ny]
            deep_start(lv, slot, EDGES)
            for side in (-1, 1):
                x0, y0 = near_side(nx, side, h), near_side(ny, side, h)
                for p in range(h):
                    ref[lv.index, "sx"][slot, int(side > 0), pl.ds(p * ny, ny), :] = buf[pl.ds(lv.row(x0 + p, 0), ny), :]
                    ref[lv.index, "sy"][slot, int(side > 0), pl.ds(p * nx, nx), :] = buf[
                        pl.ds(lv.row(0, y0 + p), nx, stride=lv.pitch), :
                    ]
            for i in (-1, 1):
                for j in (-1, 1):
                    x0, y0 = near_side(nx, i, h), near_side(ny, j, h)
                    for p in range(h):
                        ref[lv.index, "sc"][slot, 2 * (i > 0) + (j > 0), pl.ds(p * h, h), :] = buf[
                            pl.ds(lv.row(x0 + p, y0), h), :
                        ]
            deep_start(lv, slot, [offset for offset in OFFSETS if not offset[2]])
            return slot

        def end_deep(lv, buf, slot):
            h, nx, ny, nz = lv.h, lv.nx, lv.ny, lv.nz
            deep_finish(lv, slot, [offset for offset in OFFSETS if not offset[2]])
            for side in (-1, 1):
                x0, y0 = far_side(nx, side, h), far_side(ny, side, h)
                for p in range(h):
                    buf[pl.ds(lv.row(x0 + p, 0), ny), :] = ref[lv.index, "qx"][slot, int(side > 0), pl.ds(p * ny, ny), :]
                    buf[pl.ds(lv.row(0, y0 + p), nx, stride=lv.pitch), :] = ref[lv.index, "qy"][
                        slot, int(side > 0), pl.ds(p * nx, nx), :
                    ]
            for i in (-1, 1):
                for j in (-1, 1):
                    x0, y0 = far_side(nx, i, h), far_side(ny, j, h)
                    for p in range(h):
                        buf[pl.ds(lv.row(x0 + p, y0), h), :] = ref[lv.index, "qc"][
                            slot, 2 * (i > 0) + (j > 0), pl.ds(p * h, h), :
                        ]
            deep_finish(lv, slot, EDGES)
            got, zone = ref[lv.index, "qz"], ref[lv.index, "zone"]
            for i in (-1, 0, 1):
                for k in (-1, 1):
                    place = 2 * (i + 1) + (k > 0)
                    zone[place, pl.ds(0, h), :] = got[slot, EDGES.index((i, -1, k)), pl.ds(ny - h, h), :]
                    middle = (i, 0, k)
                    zone[place, pl.ds(h, ny), :] = got[slot, EDGES.index(middle), pl.ds(0, ny), :]
                    zone[place, pl.ds(h + ny, h), :] = got[slot, EDGES.index((i, 1, k)), pl.ds(0, h), :]
            where = iota((lv.pitch, LANES), 1)
            edge = (where < h) | ((where >= nz + h) & (where < nz + 2 * h))
            high = (where & (2 * h - 1)) >= h
            for i in (-1, 0, 1):
                low, up = (zone[2 * (i + 1) + k, pl.ds(0, lv.pitch), :] for k in (0, 1))
                merged = jnp.where(high, low, roll(up, nz + 2 * h))
                planes = range(nx) if i == 0 else range(-h, 0) if i < 0 else range(nx, nx + h)
                for x in planes:
                    span = pl.ds(lv.row(x, -h), lv.pitch)
                    buf[span, :] = jnp.where(edge, roll(merged, -(2 * h * (x - i * nx) + h)), buf[span, :])

        def sides(lv, mid, lo, rows, halo):
            below, above = roll(mid, 1), roll(mid, -1)
            if lv.wide:
                edge = jnp.concatenate(
                    [
                        roll(halo[c // lv.half], -2 * (c % lv.half))
                        for c in range(lo // 8, (lo + rows) // 8)
                    ],
                    axis=0,
                )
                where = iota((rows, LANES), 1)
                below = jnp.where(where == 0, edge, below)
                above = jnp.where(where == LANES - 1, edge, above)
            return below, above

        def around(lv, buf, lo, rows, halo):
            base = lv.c0 + lo
            mid = buf[pl.ds(base, rows), :]
            below, above = sides(lv, mid, lo, rows, halo)
            return mid, (
                buf[pl.ds(base - lv.pitch, rows), :],
                buf[pl.ds(base + lv.pitch, rows), :],
                buf[pl.ds(base - 1, rows), :],
                buf[pl.ds(base + 1, rows), :],
                below,
                above,
            )

        coeff_names = ("xm", "xp", "ym", "yp", "zm", "zp")

        def applied(lv, buf, lo, rows, halo):
            mid, near = around(lv, buf, lo, rows, halo)
            span = pl.ds(lo, rows)
            total = mid
            for name, value in zip(coeff_names, near):
                total = total - ref[lv.index, name][span, :] * value
            return mid, total

        def prepare(lv, buf, halo):
            for lo, rows in lv.groups():
                span = pl.ds(lo, rows)
                mid, near = around(lv, buf, lo, rows, halo)
                where = iota((rows, LANES), 1)
                near = list(near)
                if lv.shared and lv.nz == LANES:
                    near[4] = jnp.where(where == 0, 0.0, near[4])
                    near[5] = jnp.where(where == LANES - 1, 0.0, near[5])
                couple = [(0.5 * lv.factor) * (mid + value) for value in near]
                diagonal = couple[0]
                for value in couple[1:]:
                    diagonal = diagonal + value
                inverse = jnp.where(mid > 0.0, 1.0 / diagonal, 0.0)
                ref[lv.index, "dg"][span, :] = diagonal
                ref[lv.index, "iv"][span, :] = inverse
                couple = [value * inverse for value in couple]
                if lv.shared and lv.nz == LANES:
                    couple[4] = jnp.where(where == 0, 0.0, couple[4])
                    couple[5] = jnp.where(where == LANES - 1, 0.0, couple[5])
                for name, value in zip(coeff_names, couple):
                    ref[lv.index, name][span, :] = value

        def sweeps(lv, src, count, final):
            factors = chebyshev_factors(count)
            r, u = ref[lv.index, "r"], ref[lv.index, "u"]
            buffers = [ref[lv.index, "d0"], ref[lv.index, "d1"]]
            held = src
            for step in range(count):
                keep, push = factors[step]
                target = buffers[step % 2]
                halo = faces(lv, held) if held is not None else None
                for lo, rows in lv.groups():
                    span = pl.ds(lo, rows)
                    value = r[span, :]
                    if held is not None:
                        mid, change = applied(lv, held, lo, rows, halo)
                        value = value - change
                        r[span, :] = value
                    direction = push * value
                    if step > 0:
                        direction = direction + keep * mid
                    target[pl.ds(lv.c0 + lo, rows), :] = direction
                    if step == 0 and src is None:
                        u[span, :] = direction
                    elif step == 0:
                        u[span, :] = u[span, :] + mid + direction
                    else:
                        u[span, :] = u[span, :] + direction
                held = target
            if final:
                halo = faces(lv, held)
                for lo, rows in lv.groups():
                    span = pl.ds(lo, rows)
                    mid, change = applied(lv, held, lo, rows, halo)
                    r[span, :] = r[span, :] - change
            return held

        def halve(lv, buf):
            out = ref[None, "half"]
            nx, ny = lv.nx // 2, lv.ny // 2
            for x in range(nx):
                total = None
                for px in range(2):
                    for py in range(2):
                        at = lv.row(2 * x + px, py)
                        value = buf[pl.ds(at, ny, stride=2), :]
                        total = value if total is None else total + value
                out[pl.ds(x * ny, ny), :] = total
            return nx, ny

        def pair_matrix(lv, offset):
            fine, coarse = iota((LANES, LANES), 0), iota((LANES, LANES), 1)
            cell = fine - lv.zo
            inside = (cell >= 0) & (cell < lv.nz)
            match = lax.shift_right_arithmetic(cell, 1) + offset == coarse
            return jnp.where(inside & match, 0.125, 0.0)

        def restrict(lv, buf, offset):
            nx, ny = halve(lv, buf)
            return nx, ny, dot(ref[None, "half"][pl.ds(0, up8(nx * ny)), :], pair_matrix(lv, offset))

        def spread(nx, ny, value, coarse, buf):
            scratch_ref = ref[None, "half"]
            scratch_ref[pl.ds(0, up8(nx * ny)), :] = value
            for x in range(nx):
                buf[pl.ds(coarse.row(x, 0), ny), :] = scratch_ref[pl.ds(x * ny, ny), :]

        def stretch(cell, offset):
            coarse = iota((LANES, LANES), 0) - offset
            parent = lax.shift_right_arithmetic(cell, 1)
            other = parent + 2 * (cell & 1) - 1
            return jnp.where(coarse == parent, 0.75, 0.0) + jnp.where(coarse == other, 0.25, 0.0)

        def prolong(rows, pitch, origin, weights, value, fine, buf):
            t, te, to = ref[None, "t"], ref[None, "te"], ref[None, "to"]
            t[pl.ds(0, rows), :] = dot(value, weights)
            reach = fine.h // 2
            x0, nx, ny = -reach, fine.nx // 2 + 2 * reach, fine.ny // 2 + 2 * reach
            low = origin + x0 * pitch - reach - 1
            n = (nx - 1) * pitch + ny + 2
            mid = 0.75 * t[pl.ds(low, n), :]
            te[pl.ds(0, n), :] = mid + 0.25 * t[pl.ds(low - pitch, n), :]
            to[pl.ds(0, n), :] = mid + 0.25 * t[pl.ds(low + pitch, n), :]
            for x in range(nx):
                for px, src in ((0, te), (1, to)):
                    at = x * pitch + 1
                    mid = 0.75 * src[pl.ds(at, ny), :]
                    to_row = fine.row(2 * (x + x0) + px, -2 * reach)
                    buf[pl.ds(to_row, ny, stride=2), :] = mid + 0.25 * src[pl.ds(at - 1, ny), :]
                    buf[pl.ds(to_row + 1, ny, stride=2), :] = mid + 0.25 * src[pl.ds(at + 1, ny), :]

        def columns(fine):
            return iota((LANES, LANES), 1) - fine.zo

        def depth_copy(which, k):
            return pltpu.make_async_remote_copy(
                src_ref=ref[None, "zs"].at[which],
                dst_ref=ref[None, "zr"].at[which, gz],
                send_sem=ref[None, "zsend"].at[which, k],
                recv_sem=ref[None, "zrecv"].at[which, k],
                device_id=(gx, gy, depth_peer(k)),
                device_id_type=MESH,
            )

        def depth_arrival(which, k):
            source = lax.rem(gz + gzn - k, gzn)
            return pltpu.make_async_remote_copy(
                src_ref=ref[None, "zs"].at[which],
                dst_ref=ref[None, "zr"].at[which, source],
                send_sem=ref[None, "zsend"].at[which, k],
                recv_sem=ref[None, "zrecv"].at[which, k],
                device_id=(gx, gy, depth_peer(k)),
                device_id_type=MESH,
            )

        def plane_copy(which, i, j):
            px, py = plane_peer(i, j)
            return pltpu.make_async_remote_copy(
                src_ref=ref[None, "ps"].at[which],
                dst_ref=ref[None, "pr"].at[which, gx * gyn + gy],
                send_sem=ref[None, "psend"].at[which, i * gyn + j],
                recv_sem=ref[None, "precv"].at[which, i * gyn + j],
                device_id=(px, py, gz),
                device_id_type=MESH,
            )

        def plane_arrival(which, i, j):
            sx, sy = lax.rem(gx + gxn - i, gxn), lax.rem(gy + gyn - j, gyn)
            px, py = plane_peer(i, j)
            return pltpu.make_async_remote_copy(
                src_ref=ref[None, "ps"].at[which],
                dst_ref=ref[None, "pr"].at[which, sx * gyn + sy],
                send_sem=ref[None, "psend"].at[which, i * gyn + j],
                recv_sem=ref[None, "precv"].at[which, i * gyn + j],
                device_id=(px, py, gz),
                device_id_type=MESH,
            )

        def gather_depth_start(which, block):
            ref[None, "zs"][which] = block[:blk]
            for k in range(1, gzn):
                depth_copy(which, k).start()

        def gather_plane_start(which):
            total = ref[None, "zs"][which]
            for k in range(1, gzn):
                depth_arrival(which, k).wait_recv()
            for k in range(1, gzn):
                total = total + ref[None, "zr"][which, lax.rem(gz + k, gzn)]
            ref[None, "ps"][which] = total
            for i, j in plane_peers:
                plane_copy(which, i, j).start()
            ref[None, "pr"][which, gx * gyn + gy] = total

        def gather_end(which, buf):
            for i, j in plane_peers:
                plane_arrival(which, i, j).wait_recv()
            for i in range(gxn):
                for x in range(cx):
                    for y in range(cy):
                        rows = [ref[None, "pr"][which, i * gyn + j, pl.ds(x * cy + y, 1), :] for j in range(gyn)]
                        at = three.row(i * cx + x, y)
                        buf[pl.ds(at, gyn, stride=cy), :] = jnp.concatenate(rows, axis=0)

        def gather_waits():
            for which in range(2):
                for k in range(1, gzn):
                    depth_copy(which, k).wait_send()
                for i, j in plane_peers:
                    plane_copy(which, i, j).wait_send()

        first, middle, last = local
        for x in range(first.nx):
            ref[0, "v"][pl.ds(first.row(x, 0), first.ny), :] = k_ref[x]
            ref[0, "w"][pl.ds(first.row(x, 0), first.ny), :] = b_ref[x]
        for fine, coarse in ((first, middle), (middle, last)):
            nx, ny, value = restrict(fine, ref[fine.index, "v"], coarse.zo)
            spread(nx, ny, value, coarse, ref[coarse.index, "v"])
        _, _, k_block = restrict(last, ref[2, "v"], gz * cz + three.zo)

        pl.semaphore_wait(barrier, len(plane_peers) + gzn - 1 + len(diagonal))
        slot0 = begin_faces(first, ref[0, "v"])
        gather_depth_start(0, k_block)
        slot1 = begin_deep(middle, ref[1, "v"])
        slot2 = begin_deep(last, ref[2, "v"])
        halo = end_faces(first, ref[0, "v"], slot0)
        prepare(first, ref[0, "v"], halo)

        def load(lv):
            ref[lv.index, "r"][...] = ref[lv.index, "w"][pl.ds(lv.c0, lv.n), :] * ref[lv.index, "iv"][...]

        def residual(lv, name):
            ref[lv.index, name][pl.ds(lv.c0, lv.n), :] = ref[lv.index, "r"][...] * ref[lv.index, "dg"][...]

        load(first)
        sweeps(first, None, STEPS, True)
        residual(first, "w")
        nx, ny, value = restrict(first, ref[0, "w"], middle.zo)
        spread(nx, ny, value, middle, ref[1, "w"])
        slot = begin_deep(middle, ref[1, "w"])
        end_deep(middle, ref[1, "v"], slot1)
        prepare(middle, ref[1, "v"], None)
        gather_plane_start(0)
        end_deep(middle, ref[1, "w"], slot)
        load(middle)
        sweeps(middle, None, STEPS, True)
        residual(middle, "w")
        nx, ny, value = restrict(middle, ref[1, "w"], last.zo)
        spread(nx, ny, value, last, ref[2, "w"])
        slot = begin_deep(last, ref[2, "w"])
        ref[1, "v"][pl.ds(middle.c0, middle.n), :] = ref[1, "r"][...]
        slot1 = begin_deep(middle, ref[1, "v"])
        end_deep(last, ref[2, "v"], slot2)
        prepare(last, ref[2, "v"], None)
        end_deep(last, ref[2, "w"], slot)
        load(last)
        sweeps(last, None, STEPS, True)
        residual(last, "w")
        _, _, b_block = restrict(last, ref[2, "w"], gz * cz + three.zo)
        gather_depth_start(1, b_block)
        ref[2, "v"][pl.ds(last.c0, last.n), :] = ref[2, "r"][...]
        slot2 = begin_deep(last, ref[2, "v"])
        gather_end(0, ref[3, "v"])
        prepare(three, ref[3, "v"], None)
        gather_plane_start(1)
        nx, ny, value = restrict(three, ref[3, "v"], four.zo)
        spread(nx, ny, value, four, ref[4, "v"])
        prepare(four, ref[4, "v"], None)
        end_deep(middle, ref[1, "v"], slot1)
        end_deep(last, ref[2, "v"], slot2)
        for lv in (middle, last):
            ref[lv.index, "r"][...] = ref[lv.index, "v"][pl.ds(lv.c0, lv.n), :]
        gather_end(1, ref[3, "w"])

        load(three)
        sweeps(three, None, STEPS, True)
        residual(three, "w")
        nx, ny, value = restrict(three, ref[3, "w"], four.zo)
        spread(nx, ny, value, four, ref[4, "w"])
        load(four)
        sweeps(four, None, COARSE_STEPS, False)

        def lift(lv):
            span = pl.ds(lv.c0, lv.n)
            ref[lv.index, "v"][span, :] = jnp.where(ref[lv.index, "iv"][...] > 0.0, ref[lv.index, "v"][span, :], 0.0)
            sweeps(lv, ref[lv.index, "v"], STEPS, lv.index == 0)

        def solved(lv):
            ref[lv.index, "w"][pl.ds(lv.c0, lv.n), :] = ref[lv.index, "u"][...]
            return ref[lv.index, "w"]

        field = solved(four)
        prolong(four.rows, four.pitch, four.row(0, 0), stretch(columns(three), four.zo), field[...], three, ref[3, "v"])
        lift(three)
        field = solved(three)

        reach = HALO // 2 + 1
        pitch = cy + 2 * reach
        picked = up8((cx + 2 * reach) * pitch)
        row, source = iota((picked, three.rows), 0), iota((picked, three.rows), 1)
        plane = row // pitch
        cell_x, cell_y = gx * cx - reach + plane, gy * cy - reach + (row - plane * pitch)
        inside = (cell_x >= 0) & (cell_x < three.nx) & (cell_y >= 0) & (cell_y < three.ny)
        wanted = three.row(0, 0) + cell_x * three.pitch + cell_y
        window = dot(jnp.where(inside & (source == wanted), 1.0, 0.0), field[...])
        weights = stretch(columns(last) + gz * last.nz, three.zo)
        prolong(picked, pitch, reach * pitch + reach, weights, window, last, ref[2, "v"])
        lift(last)
        field = solved(last)
        end_deep(last, field, begin_deep(last, field))
        weights = stretch(columns(middle), last.zo)
        prolong(last.rows, last.pitch, last.row(0, 0), weights, field[...], middle, ref[1, "v"])
        lift(middle)
        field = solved(middle)
        end_deep(middle, field, begin_deep(middle, field))
        weights = stretch(columns(first), middle.zo)
        prolong(middle.rows, middle.pitch, middle.row(0, 0), weights, field[...], first, ref[0, "v"])
        sweeps(first, ref[0, "v"], STEPS, True)

        for x in range(first.nx):
            span = pl.ds(first.row(x, 0) - first.c0, first.ny)
            u_ref[x] = ref[0, "u"][span, :]
            res_ref[x] = ref[0, "r"][span, :] * ref[0, "dg"][span, :]

        for slot in range(counters[0]):
            for way in range(6):

                @pl.when(has[way])
                def _():
                    link(first, slot, way).wait_send()

        for lv in (middle, last):
            for slot in range(counters[lv.index]):
                for offset in OFFSETS:

                    @pl.when(exists[offset])
                    def _():
                        deep_link(lv, slot, offset, False).wait_send()

        gather_waits()

    def on_device(right_side, conductivity):
        out = jax.ShapeDtypeStruct(box, jnp.float32)
        return pl.pallas_call(
            kernel,
            out_shape=(out, out),
            in_specs=[pl.BlockSpec(memory_space=pltpu.VMEM)] * 2,
            out_specs=[pl.BlockSpec(memory_space=pltpu.VMEM)] * 2,
            scratch_shapes=shapes,
            compiler_params=pltpu.CompilerParams(
                collective_id=0, has_side_effects=True, vmem_limit_bytes=48 * 1024 * 1024
            ),
        )(right_side, conductivity)

    return on_device


def solution(mesh):
    sizes = tuple(mesh.shape[axis] for axis in ("gx", "gy", "gz"))
    spec = P("gx", "gy", "gz")
    return jax.shard_map(
        build(sizes, (32, 16, 128)), mesh=mesh, in_specs=(spec, spec), out_specs=(spec, spec), check_vma=False
    )
```

```python
import jax
import jax.numpy as jnp
from jax import lax
from jax.experimental import pallas as pl
from jax.experimental.pallas import tpu as pltpu
from jax.sharding import PartitionSpec as P

STEPS = 3
COARSE_STEPS = 8
LOWER_EDGE = 0.3
UPPER_EDGE = 2.0
MESH = pl.DeviceIdType.MESH
LANES = 128
DEEP = 4
HALO = 4
OFFSETS = [(i, j, k) for i in (-1, 0, 1) for j in (-1, 0, 1) for k in (-1, 0, 1) if i or j or k]
EDGES = [offset for offset in OFFSETS if offset[2]]


def chebyshev_factors(sweeps):
    centre_value = 0.5 * (UPPER_EDGE + LOWER_EDGE)
    half_width = 0.5 * (UPPER_EDGE - LOWER_EDGE)
    ratio_value = centre_value / half_width
    damping = 1.0 / ratio_value
    factors = [(0.0, 1.0 / centre_value)]
    for _ in range(1, sweeps):
        damping_next = 1.0 / (2.0 * ratio_value - damping)
        factors.append((damping_next * damping, 2.0 * damping_next / half_width))
        damping = damping_next
    return factors


def up8(value):
    return -(-value // 8) * 8


class Level:
    def __init__(self, index, nx, ny, nz, h, shared):
        self.index, self.nx, self.ny, self.nz, self.h, self.shared = index, nx, ny, nz, h, shared
        self.pitch = ny + 2 * h
        self.c0 = up8(self.pitch + 1)
        self.n = up8((nx + 2 * h - 2) * self.pitch)
        self.rows = self.c0 + self.n + up8(self.pitch + 1)
        self.zo = 0 if nz == LANES else h
        self.factor = 0.25**index
        self.wide = nz == LANES and not shared
        self.per = LANES // (2 * h)
        self.halves, self.parts = up8(ny) // 8, -(-nx // self.per)
        self.sends = not shared

    def row(self, x, y):
        return self.c0 + (x + self.h - 1) * self.pitch + y + self.h

    def scratch(self):
        field = pltpu.VMEM((self.n, LANES), jnp.float32)
        padded = pltpu.VMEM((self.rows, LANES), jnp.float32)
        shapes = {name: field for name in ("xm", "xp", "ym", "yp", "zm", "zp", "dg", "iv", "r", "u")}
        shapes.update({name: padded for name in ("d0", "d1", "v", "w")})
        if self.sends:
            for name in ("s", "q"):
                shapes[name + "x"] = pltpu.VMEM((DEEP, 2, self.h * self.ny, LANES), jnp.float32)
                shapes[name + "y"] = pltpu.VMEM((DEEP, 2, self.h * self.nx, LANES), jnp.float32)
                shapes[name + "c"] = pltpu.VMEM((DEEP, 4, self.h * self.h, LANES), jnp.float32)
            shapes["sz"] = pltpu.VMEM((DEEP, self.halves, self.parts, 8, LANES), jnp.float32)
            shapes["qz"] = pltpu.VMEM((DEEP, 18, self.halves, self.parts, 8, LANES), jnp.float32)
            shapes["zone"] = pltpu.VMEM((2 * (2 + self.parts), up8(self.pitch), LANES), jnp.float32)
            shapes["send"] = pltpu.SemaphoreType.DMA((DEEP, 26))
            shapes["recv"] = pltpu.SemaphoreType.DMA((DEEP, 26))
        return shapes

    def groups(self, skip=0):
        skip = skip * self.pitch if self.h > 1 else 0
        first, last = skip, self.n - skip
        count = -(-(last - first) // 96)
        size = up8(-(-(last - first) // count))
        return [(lo, min(size, last - lo)) for lo in range(first, last, size)]


def dot(a, b):
    return jnp.dot(a, b, precision=lax.Precision.HIGHEST, preferred_element_type=jnp.float32)


def iota(shape, dim):
    return lax.broadcasted_iota(jnp.int32, shape, dim)


def roll(value, shift):
    shift %= LANES
    return pltpu.roll(value, shift, 1) if shift else value


def build(mesh_shape, box):
    gxn, gyn, gzn = mesh_shape
    bx, by, bz = box
    local = [Level(i, bx >> i, by >> i, bz >> i, HALO, False) for i in range(3)]
    rim = Level(0, bx, by, 4 * HALO, HALO, False)
    rim.index, rim.sends = "rim", False
    cx, cy, cz = bx >> 3, by >> 3, bz >> 3
    three = Level(3, gxn * cx, gyn * cy, gzn * cz, 1, True)
    four = Level(4, three.nx // 2, three.ny // 2, three.nz // 2, 1, True)
    levels = local + [rim, three, four]
    blk = cx * cy
    names = [(lv.index, name) for lv in levels for name in lv.scratch()]
    shapes = [shape for lv in levels for shape in lv.scratch().values()]
    extra = {
        "t": pltpu.VMEM((max(lv.rows for lv in levels), LANES), jnp.float32),
        "te": pltpu.VMEM((max(lv.n for lv in levels) + 16, LANES), jnp.float32),
        "to": pltpu.VMEM((max(lv.n for lv in levels) + 16, LANES), jnp.float32),
        "half": pltpu.VMEM((128, LANES), jnp.float32),
        "zs": pltpu.VMEM((2, blk, LANES), jnp.float32),
        "zr": pltpu.VMEM((2, gzn, blk, LANES), jnp.float32),
        "ps": pltpu.VMEM((2, blk, LANES), jnp.float32),
        "pr": pltpu.VMEM((2, gxn * gyn, blk, LANES), jnp.float32),
        "zsend": pltpu.SemaphoreType.DMA((2, gzn)),
        "zrecv": pltpu.SemaphoreType.DMA((2, gzn)),
        "psend": pltpu.SemaphoreType.DMA((2, gxn * gyn)),
        "precv": pltpu.SemaphoreType.DMA((2, gxn * gyn)),
    }
    names += [(None, name) for name in extra]
    shapes += list(extra.values())

    def kernel(b_ref, k_ref, u_ref, res_ref, *scratch):
        ref = {key: value for key, value in zip(names, scratch)}
        gx, gy, gz = lax.axis_index("gx"), lax.axis_index("gy"), lax.axis_index("gz")
        plane_peers = [(i, j) for i in range(gxn) for j in range(gyn) if i or j]

        def plane_peer(i, j):
            return lax.rem(gx + i, gxn), lax.rem(gy + j, gyn)

        def depth_peer(k):
            return lax.rem(gz + k, gzn)

        for lv in levels:
            for name in ("d0", "d1", "v", "w"):
                ref[lv.index, name][...] = jnp.zeros((lv.rows, LANES), jnp.float32)
            if lv.sends:
                for name in ("qx", "qy", "qz", "qc"):
                    target = ref[lv.index, name]
                    target[...] = jnp.zeros(target.shape, jnp.float32)

        barrier = pltpu.get_barrier_semaphore()
        for i, j in plane_peers:
            px, py = plane_peer(i, j)
            pl.semaphore_signal(barrier, inc=1, device_id=(px, py, gz), device_id_type=MESH)
        for k in range(1, gzn):
            pl.semaphore_signal(barrier, inc=1, device_id=(gx, gy, depth_peer(k)), device_id_type=MESH)

        counters = [0, 0, 0]
        at = (gx, gy, gz)
        sizes = (gxn, gyn, gzn)

        def there(offset):
            found = jnp.bool_(True)
            for a in range(3):
                if offset[a] < 0:
                    found = found & (at[a] > 0)
                elif offset[a] > 0:
                    found = found & (at[a] < sizes[a] - 1)
            return found

        exists = {offset: there(offset) for offset in OFFSETS}

        def device(offset):
            return tuple(at[a] + offset[a] for a in range(3))

        diagonal = [offset for offset in EDGES if offset[0] or offset[1]]
        for offset in diagonal:
            around_edge = tuple(lax.rem(at[a] + offset[a] + sizes[a], sizes[a]) for a in range(3))
            pl.semaphore_signal(barrier, inc=1, device_id=around_edge, device_id_type=MESH)

        def deep_link(lv, slot, offset, arriving):
            i, j, k = offset
            sent = OFFSETS.index(offset)
            landed = sent if arriving else OFFSETS.index((-i, -j, -k))

            def part(kind, which):
                if k:
                    way_x, way_y = (-i, -j) if arriving else (i, j)
                    rows = pl.ds(0, lv.halves) if not way_y else pl.ds(0 if way_y < 0 else lv.halves - 1, 1)
                    planes = pl.ds(0, lv.parts) if not way_x else pl.ds(0 if way_x < 0 else lv.parts - 1, 1)
                    index = (slot,) if which is None else (slot, which)
                    return ref[lv.index, kind + "z"].at[index + (rows, planes)]
                name = "c" if i and j else "x" if i else "y"
                return ref[lv.index, kind + name].at[slot, which]

            def place(offset):
                if offset[2]:
                    return EDGES.index(offset)
                low_x, low_y = offset[0] > 0, offset[1] > 0
                return 2 * low_x + low_y if offset[0] and offset[1] else int(low_x or low_y)

            return pltpu.make_async_remote_copy(
                src_ref=part("s", None if k else place(offset)),
                dst_ref=part("q", place(OFFSETS[landed])),
                send_sem=ref[lv.index, "send"].at[slot, sent],
                recv_sem=ref[lv.index, "recv"].at[slot, landed],
                device_id=device(offset),
                device_id_type=MESH,
            )

        def deep_start(lv, slot, offsets):
            for offset in offsets:

                @pl.when(exists[offset])
                def _():
                    deep_link(lv, slot, offset, False).start()

        def deep_finish(lv, slot, offsets):
            for offset in offsets:

                @pl.when(exists[offset])
                def _():
                    deep_link(lv, slot, offset, True).wait_recv()

        def near_side(size, direction, h):
            return 0 if direction < 0 else size - h

        def far_side(size, direction, h):
            return -h if direction < 0 else size

        def begin_deep(lv, buf):
            slot = counters[lv.index]
            counters[lv.index] += 1
            h, nx, ny, nz = lv.h, lv.nx, lv.ny, lv.nz
            out = ref[lv.index, "sz"]
            size = min(ny, 8)
            where = iota((size, LANES), 1)
            for part in range(lv.parts):
                for half in range(lv.halves):
                    packed = jnp.zeros((size, LANES), jnp.float32)
                    for x in range(part * lv.per, min(nx, (part + 1) * lv.per)):
                        value = buf[pl.ds(lv.row(x, 8 * half), size), :]
                        low = 2 * h * (x % lv.per)
                        packed = jnp.where(where >= low, roll(value, low - lv.zo), packed)
                        packed = jnp.where(where >= low + h, roll(value, low + 2 * h - nz - lv.zo), packed)
                    out[slot, half, part, pl.ds(0, size), :] = packed
                    if size < 8:
                        out[slot, half, part, pl.ds(size, 8 - size), :] = packed[: 8 - size]
            deep_start(lv, slot, EDGES)
            for side in (-1, 1):
                x0, y0 = near_side(nx, side, h), near_side(ny, side, h)
                for p in range(h):
                    ref[lv.index, "sx"][slot, int(side > 0), pl.ds(p * ny, ny), :] = buf[pl.ds(lv.row(x0 + p, 0), ny), :]
                    ref[lv.index, "sy"][slot, int(side > 0), pl.ds(p * nx, nx), :] = buf[
                        pl.ds(lv.row(0, y0 + p), nx, stride=lv.pitch), :
                    ]
            for i in (-1, 1):
                for j in (-1, 1):
                    x0, y0 = near_side(nx, i, h), near_side(ny, j, h)
                    for p in range(h):
                        ref[lv.index, "sc"][slot, 2 * (i > 0) + (j > 0), pl.ds(p * h, h), :] = buf[
                            pl.ds(lv.row(x0 + p, y0), h), :
                        ]
            deep_start(lv, slot, [offset for offset in OFFSETS if not offset[2]])
            return slot

        def end_deep(lv, buf, slot, target=None):
            h, nx, ny, nz = lv.h, lv.nx, lv.ny, lv.nz if target is None else rim.nz
            deep_finish(lv, slot, [offset for offset in OFFSETS if not offset[2]])
            for side in (-1, 1):
                x0, y0 = far_side(nx, side, h), far_side(ny, side, h)
                for p in range(h):
                    buf[pl.ds(lv.row(x0 + p, 0), ny), :] = ref[lv.index, "qx"][slot, int(side > 0), pl.ds(p * ny, ny), :]
                    buf[pl.ds(lv.row(0, y0 + p), nx, stride=lv.pitch), :] = ref[lv.index, "qy"][
                        slot, int(side > 0), pl.ds(p * nx, nx), :
                    ]
            for i in (-1, 1):
                for j in (-1, 1):
                    x0, y0 = far_side(nx, i, h), far_side(ny, j, h)
                    for p in range(h):
                        buf[pl.ds(lv.row(x0 + p, y0), h), :] = ref[lv.index, "qc"][
                            slot, 2 * (i > 0) + (j > 0), pl.ds(p * h, h), :
                        ]
            deep_finish(lv, slot, EDGES)
            got, zone = ref[lv.index, "qz"], ref[lv.index, "zone"]
            sources = [(-1, lv.parts - 1)] + [(0, part) for part in range(lv.parts)] + [(1, 0)]
            size = min(ny, 8)
            for place, (i, part) in enumerate(sources):
                for k in (0, 1):
                    side = 2 * k - 1
                    into = zone.at[2 * place + k]
                    into[pl.ds(0, h), :] = got[
                        slot, EDGES.index((i, -1, side)), lv.halves - 1, part, pl.ds(size - h, h), :
                    ]
                    for half in range(lv.halves):
                        into[pl.ds(h + 8 * half, size), :] = got[
                            slot, EDGES.index((i, 0, side)), half, part, pl.ds(0, size), :
                        ]
                    into[pl.ds(h + ny, h), :] = got[slot, EDGES.index((i, 1, side)), 0, part, pl.ds(0, h), :]
            where = iota((lv.pitch, LANES), 1)
            edge = (where < h) | ((where >= nz + h) & (where < nz + 2 * h))
            high = (where & (2 * h - 1)) >= h
            for place, (i, part) in enumerate(sources):
                low, up = (zone[2 * place + k, pl.ds(0, lv.pitch), :] for k in (0, 1))
                merged = jnp.where(high, low, roll(up, nz + 2 * h))
                if i:
                    planes = range(-h, 0) if i < 0 else range(nx, nx + h)
                else:
                    planes = range(part * lv.per, min(nx, (part + 1) * lv.per))
                for x in planes:
                    span = pl.ds(lv.row(x, -h), lv.pitch)
                    shifted = roll(merged, -(2 * h * ((x - i * nx) % lv.per) + h))
                    if target is None:
                        buf[span, :] = jnp.where(edge, shifted, buf[span, :])
                    else:
                        inner = buf[span, :]
                        inner = jnp.where(where < 3 * h, roll(inner, h), roll(inner, 5 * h))
                        inner = jnp.where(edge, shifted, inner)
                        target[span, :] = jnp.where(where < nz + 2 * h, inner, 0.0)

        def joined(inner, outer):
            where = iota(inner.shape, 1)
            outer = jnp.where(where < LANES // 2, roll(outer, -HALO), roll(outer, LANES - 5 * HALO))
            return jnp.where((where < HALO) | (where >= LANES - HALO), outer, inner)

        def around(lv, buf, lo, rows):
            base = lv.c0 + lo
            mid = buf[pl.ds(base, rows), :]
            return mid, (
                buf[pl.ds(base - lv.pitch, rows), :],
                buf[pl.ds(base + lv.pitch, rows), :],
                buf[pl.ds(base - 1, rows), :],
                buf[pl.ds(base + 1, rows), :],
                roll(mid, 1),
                roll(mid, -1),
            )

        coeff_names = ("xm", "xp", "ym", "yp", "zm", "zp")

        def applied(lv, buf, lo, rows):
            mid, near = around(lv, buf, lo, rows)
            span = pl.ds(lo, rows)
            total = mid
            for name, value in zip(coeff_names, near):
                total = total - ref[lv.index, name][span, :] * value
            return mid, total

        def prepare(lv, buf):
            for lo, rows in lv.groups():
                span = pl.ds(lo, rows)
                mid, near = around(lv, buf, lo, rows)
                where = iota((rows, LANES), 1)
                near = list(near)
                if lv.shared and lv.nz == LANES:
                    near[4] = jnp.where(where == 0, 0.0, near[4])
                    near[5] = jnp.where(where == LANES - 1, 0.0, near[5])
                couple = [(0.5 * lv.factor) * (mid + value) for value in near]
                diagonal = couple[0]
                for value in couple[1:]:
                    diagonal = diagonal + value
                inverse = jnp.where(mid > 0.0, 1.0 / diagonal, 0.0)
                ref[lv.index, "dg"][span, :] = diagonal
                ref[lv.index, "iv"][span, :] = inverse
                couple = [value * inverse for value in couple]
                if lv.shared and lv.nz == LANES:
                    couple[4] = jnp.where(where == 0, 0.0, couple[4])
                    couple[5] = jnp.where(where == LANES - 1, 0.0, couple[5])
                for name, value in zip(coeff_names, couple):
                    ref[lv.index, name][span, :] = value

        def sweeps(lv, src, count, final):
            factors = chebyshev_factors(count)
            r, u = ref[lv.index, "r"], ref[lv.index, "u"]
            buffers = [ref[lv.index, "d0"], ref[lv.index, "d1"]]
            held = src
            applications = count - 1 + (src is not None) + final
            skip = lv.h - 1 - applications
            for step in range(count):
                keep, push = factors[step]
                target = buffers[step % 2]
                if held is not None:
                    skip += 1
                for lo, rows in lv.groups(max(skip, 0)):
                    span = pl.ds(lo, rows)
                    value = r[span, :]
                    if held is not None:
                        mid, change = applied(lv, held, lo, rows)
                        value = value - change
                        r[span, :] = value
                    direction = push * value
                    if step > 0:
                        direction = direction + keep * mid
                    target[pl.ds(lv.c0 + lo, rows), :] = direction
                    if step == 0 and src is None:
                        u[span, :] = direction
                    elif step == 0:
                        u[span, :] = u[span, :] + mid + direction
                    else:
                        u[span, :] = u[span, :] + direction
                held = target
            if final:
                for lo, rows in lv.groups(max(skip + 1, 0)):
                    span = pl.ds(lo, rows)
                    mid, change = applied(lv, held, lo, rows)
                    r[span, :] = r[span, :] - change
            return held

        def halve(lv, buf):
            out = ref[None, "half"]
            nx, ny = lv.nx // 2, lv.ny // 2
            for x in range(nx):
                total = None
                for px in range(2):
                    for py in range(2):
                        at = lv.row(2 * x + px, py)
                        value = buf[pl.ds(at, ny, stride=2), :]
                        total = value if total is None else total + value
                out[pl.ds(x * ny, ny), :] = total
            return nx, ny

        def pair_matrix(lv, offset):
            fine, coarse = iota((LANES, LANES), 0), iota((LANES, LANES), 1)
            cell = fine - lv.zo
            inside = (cell >= 0) & (cell < lv.nz)
            match = lax.shift_right_arithmetic(cell, 1) + offset == coarse
            return jnp.where(inside & match, 0.125, 0.0)

        def restrict(lv, buf, offset):
            nx, ny = halve(lv, buf)
            return nx, ny, dot(ref[None, "half"][pl.ds(0, up8(nx * ny)), :], pair_matrix(lv, offset))

        def spread(nx, ny, value, coarse, buf):
            scratch_ref = ref[None, "half"]
            scratch_ref[pl.ds(0, up8(nx * ny)), :] = value
            for x in range(nx):
                buf[pl.ds(coarse.row(x, 0), ny), :] = scratch_ref[pl.ds(x * ny, ny), :]

        def stretch(cell, offset):
            coarse = iota((LANES, LANES), 0) - offset
            parent = lax.shift_right_arithmetic(cell, 1)
            other = parent + 2 * (cell & 1) - 1
            return jnp.where(coarse == parent, 0.75, 0.0) + jnp.where(coarse == other, 0.25, 0.0)

        def prolong(rows, pitch, origin, weights, value, fine, buf):
            t, te, to = ref[None, "t"], ref[None, "te"], ref[None, "to"]
            t[pl.ds(0, rows), :] = dot(value, weights)
            reach = fine.h // 2
            x0, nx, ny = -reach, fine.nx // 2 + 2 * reach, fine.ny // 2 + 2 * reach
            low = origin + x0 * pitch - reach - 1
            n = (nx - 1) * pitch + ny + 2
            mid = 0.75 * t[pl.ds(low, n), :]
            te[pl.ds(0, n), :] = mid + 0.25 * t[pl.ds(low - pitch, n), :]
            to[pl.ds(0, n), :] = mid + 0.25 * t[pl.ds(low + pitch, n), :]
            for x in range(nx):
                for px, src in ((0, te), (1, to)):
                    at = x * pitch + 1
                    mid = 0.75 * src[pl.ds(at, ny), :]
                    to_row = fine.row(2 * (x + x0) + px, -2 * reach)
                    buf[pl.ds(to_row, ny, stride=2), :] = mid + 0.25 * src[pl.ds(at - 1, ny), :]
                    buf[pl.ds(to_row + 1, ny, stride=2), :] = mid + 0.25 * src[pl.ds(at + 1, ny), :]

        def columns(fine):
            return iota((LANES, LANES), 1) - fine.zo

        def depth_copy(which, k):
            return pltpu.make_async_remote_copy(
                src_ref=ref[None, "zs"].at[which],
                dst_ref=ref[None, "zr"].at[which, gz],
                send_sem=ref[None, "zsend"].at[which, k],
                recv_sem=ref[None, "zrecv"].at[which, k],
                device_id=(gx, gy, depth_peer(k)),
                device_id_type=MESH,
            )

        def depth_arrival(which, k):
            source = lax.rem(gz + gzn - k, gzn)
            return pltpu.make_async_remote_copy(
                src_ref=ref[None, "zs"].at[which],
                dst_ref=ref[None, "zr"].at[which, source],
                send_sem=ref[None, "zsend"].at[which, k],
                recv_sem=ref[None, "zrecv"].at[which, k],
                device_id=(gx, gy, depth_peer(k)),
                device_id_type=MESH,
            )

        def plane_copy(which, i, j):
            px, py = plane_peer(i, j)
            return pltpu.make_async_remote_copy(
                src_ref=ref[None, "ps"].at[which],
                dst_ref=ref[None, "pr"].at[which, gx * gyn + gy],
                send_sem=ref[None, "psend"].at[which, i * gyn + j],
                recv_sem=ref[None, "precv"].at[which, i * gyn + j],
                device_id=(px, py, gz),
                device_id_type=MESH,
            )

        def plane_arrival(which, i, j):
            sx, sy = lax.rem(gx + gxn - i, gxn), lax.rem(gy + gyn - j, gyn)
            px, py = plane_peer(i, j)
            return pltpu.make_async_remote_copy(
                src_ref=ref[None, "ps"].at[which],
                dst_ref=ref[None, "pr"].at[which, sx * gyn + sy],
                send_sem=ref[None, "psend"].at[which, i * gyn + j],
                recv_sem=ref[None, "precv"].at[which, i * gyn + j],
                device_id=(px, py, gz),
                device_id_type=MESH,
            )

        def gather_depth_start(which, block):
            ref[None, "zs"][which] = block[:blk]
            for k in range(1, gzn):
                depth_copy(which, k).start()

        def gather_plane_start(which):
            total = ref[None, "zs"][which]
            for k in range(1, gzn):
                depth_arrival(which, k).wait_recv()
            for k in range(1, gzn):
                total = total + ref[None, "zr"][which, lax.rem(gz + k, gzn)]
            ref[None, "ps"][which] = total
            for i, j in plane_peers:
                plane_copy(which, i, j).start()
            ref[None, "pr"][which, gx * gyn + gy] = total

        def gather_end(which, buf):
            for i, j in plane_peers:
                plane_arrival(which, i, j).wait_recv()
            for i in range(gxn):
                for x in range(cx):
                    for y in range(cy):
                        rows = [ref[None, "pr"][which, i * gyn + j, pl.ds(x * cy + y, 1), :] for j in range(gyn)]
                        at = three.row(i * cx + x, y)
                        buf[pl.ds(at, gyn, stride=cy), :] = jnp.concatenate(rows, axis=0)

        def gather_waits():
            for which in range(2):
                for k in range(1, gzn):
                    depth_copy(which, k).wait_send()
                for i, j in plane_peers:
                    plane_copy(which, i, j).wait_send()

        first, middle, last = local
        for x in range(first.nx):
            ref[0, "v"][pl.ds(first.row(x, 0), first.ny), :] = k_ref[x]
            ref[0, "w"][pl.ds(first.row(x, 0), first.ny), :] = b_ref[x]
        for fine, coarse in ((first, middle), (middle, last)):
            nx, ny, value = restrict(fine, ref[fine.index, "v"], coarse.zo)
            spread(nx, ny, value, coarse, ref[coarse.index, "v"])
        _, _, k_block = restrict(last, ref[2, "v"], gz * cz + three.zo)

        pl.semaphore_wait(barrier, len(plane_peers) + gzn - 1 + len(diagonal))
        slot0 = begin_deep(first, ref[0, "v"])
        slot = begin_deep(first, ref[0, "w"])
        gather_depth_start(0, k_block)
        slot1 = begin_deep(middle, ref[1, "v"])
        slot2 = begin_deep(last, ref[2, "v"])
        end_deep(first, ref[0, "v"], slot0, ref["rim", "v"])
        prepare(first, ref[0, "v"])
        prepare(rim, ref["rim", "v"])
        end_deep(first, ref[0, "w"], slot, ref["rim", "w"])

        def load(lv):
            ref[lv.index, "r"][...] = ref[lv.index, "w"][pl.ds(lv.c0, lv.n), :] * ref[lv.index, "iv"][...]

        def residual(lv, name):
            ref[lv.index, name][pl.ds(lv.c0, lv.n), :] = ref[lv.index, "r"][...] * ref[lv.index, "dg"][...]

        for lv in (first, rim):
            load(lv)
            sweeps(lv, None, STEPS, True)
        r0, edge_r = ref[0, "r"], ref["rim", "r"]
        for lo, rows in first.groups(first.h - 1):
            span = pl.ds(lo, rows)
            value = joined(r0[span, :], edge_r[span, :])
            ref[0, "v"][pl.ds(first.c0 + lo, rows), :] = value
            diagonal = joined(ref[0, "dg"][span, :], ref["rim", "dg"][span, :])
            ref[0, "w"][pl.ds(first.c0 + lo, rows), :] = value * diagonal
        nx, ny, value = restrict(first, ref[0, "w"], middle.zo)
        spread(nx, ny, value, middle, ref[1, "w"])
        slot = begin_deep(middle, ref[1, "w"])
        slot0 = begin_deep(first, ref[0, "v"])
        end_deep(middle, ref[1, "v"], slot1)
        prepare(middle, ref[1, "v"])
        gather_plane_start(0)
        end_deep(middle, ref[1, "w"], slot)
        load(middle)
        sweeps(middle, None, STEPS, True)
        residual(middle, "w")
        nx, ny, value = restrict(middle, ref[1, "w"], last.zo)
        spread(nx, ny, value, last, ref[2, "w"])
        slot = begin_deep(last, ref[2, "w"])
        ref[1, "v"][pl.ds(middle.c0, middle.n), :] = ref[1, "r"][...]
        slot1 = begin_deep(middle, ref[1, "v"])
        end_deep(last, ref[2, "v"], slot2)
        prepare(last, ref[2, "v"])
        end_deep(last, ref[2, "w"], slot)
        load(last)
        sweeps(last, None, STEPS, True)
        residual(last, "w")
        _, _, b_block = restrict(last, ref[2, "w"], gz * cz + three.zo)
        gather_depth_start(1, b_block)
        ref[2, "v"][pl.ds(last.c0, last.n), :] = ref[2, "r"][...]
        slot2 = begin_deep(last, ref[2, "v"])
        gather_end(0, ref[3, "v"])
        prepare(three, ref[3, "v"])
        gather_plane_start(1)
        nx, ny, value = restrict(three, ref[3, "v"], four.zo)
        spread(nx, ny, value, four, ref[4, "v"])
        prepare(four, ref[4, "v"])
        end_deep(middle, ref[1, "v"], slot1)
        end_deep(last, ref[2, "v"], slot2)
        end_deep(first, ref[0, "v"], slot0, ref["rim", "v"])
        for lv in (first, rim, middle, last):
            ref[lv.index, "r"][...] = ref[lv.index, "v"][pl.ds(lv.c0, lv.n), :]
        gather_end(1, ref[3, "w"])

        load(three)
        sweeps(three, None, STEPS, True)
        residual(three, "w")
        nx, ny, value = restrict(three, ref[3, "w"], four.zo)
        spread(nx, ny, value, four, ref[4, "w"])
        load(four)
        sweeps(four, None, COARSE_STEPS, False)

        def lift(lv):
            span = pl.ds(lv.c0, lv.n)
            ref[lv.index, "v"][span, :] = jnp.where(ref[lv.index, "iv"][...] > 0.0, ref[lv.index, "v"][span, :], 0.0)
            sweeps(lv, ref[lv.index, "v"], STEPS, lv.index in (0, "rim"))

        def solved(lv):
            ref[lv.index, "w"][pl.ds(lv.c0, lv.n), :] = ref[lv.index, "u"][...]
            return ref[lv.index, "w"]

        field = solved(four)
        prolong(four.rows, four.pitch, four.row(0, 0), stretch(columns(three), four.zo), field[...], three, ref[3, "v"])
        lift(three)
        field = solved(three)

        reach = HALO // 2 + 1
        pitch = cy + 2 * reach
        picked = up8((cx + 2 * reach) * pitch)
        row, source = iota((picked, three.rows), 0), iota((picked, three.rows), 1)
        plane = row // pitch
        cell_x, cell_y = gx * cx - reach + plane, gy * cy - reach + (row - plane * pitch)
        inside = (cell_x >= 0) & (cell_x < three.nx) & (cell_y >= 0) & (cell_y < three.ny)
        wanted = three.row(0, 0) + cell_x * three.pitch + cell_y
        window = dot(jnp.where(inside & (source == wanted), 1.0, 0.0), field[...])
        weights = stretch(columns(last) + gz * last.nz, three.zo)
        prolong(picked, pitch, reach * pitch + reach, weights, window, last, ref[2, "v"])
        lift(last)
        field = solved(last)
        end_deep(last, field, begin_deep(last, field))
        weights = stretch(columns(middle), last.zo)
        prolong(last.rows, last.pitch, last.row(0, 0), weights, field[...], middle, ref[1, "v"])
        lift(middle)
        field = solved(middle)
        end_deep(middle, field, begin_deep(middle, field))
        column = iota((LANES, LANES), 1)
        near_low = jnp.where(column < 3 * HALO, column - HALO, column + (LANES - 5 * HALO))
        for lv, cells in ((first, column), (rim, near_low)):
            weights = stretch(cells, middle.zo)
            prolong(middle.rows, middle.pitch, middle.row(0, 0), weights, field[...], lv, ref[lv.index, "v"])
            lift(lv)

        for x in range(first.nx):
            span = pl.ds(first.row(x, 0) - first.c0, first.ny)
            u_ref[x] = joined(ref[0, "u"][span, :], ref["rim", "u"][span, :])
            value = joined(ref[0, "r"][span, :], ref["rim", "r"][span, :])
            res_ref[x] = value * joined(ref[0, "dg"][span, :], ref["rim", "dg"][span, :])

        for lv in (first, middle, last):
            for slot in range(counters[lv.index]):
                for offset in OFFSETS:

                    @pl.when(exists[offset])
                    def _():
                        deep_link(lv, slot, offset, False).wait_send()

        gather_waits()

    def on_device(right_side, conductivity):
        out = jax.ShapeDtypeStruct(box, jnp.float32)
        return pl.pallas_call(
            kernel,
            out_shape=(out, out),
            in_specs=[pl.BlockSpec(memory_space=pltpu.VMEM)] * 2,
            out_specs=[pl.BlockSpec(memory_space=pltpu.VMEM)] * 2,
            scratch_shapes=shapes,
            compiler_params=pltpu.CompilerParams(
                collective_id=0, has_side_effects=True, vmem_limit_bytes=48 * 1024 * 1024
            ),
        )(right_side, conductivity)

    return on_device


def solution(mesh):
    sizes = tuple(mesh.shape[axis] for axis in ("gx", "gy", "gz"))
    spec = P("gx", "gy", "gz")
    return jax.shard_map(
        build(sizes, (32, 16, 128)), mesh=mesh, in_specs=(spec, spec), out_specs=(spec, spec), check_vma=False
    )
```

```python
import jax
import jax.numpy as jnp
from jax import lax
from jax.experimental import pallas as pl
from jax.experimental.pallas import tpu as pltpu
from jax.sharding import PartitionSpec as P

STEPS = 3
COARSE_STEPS = 8
LOWER_EDGE = 0.3
UPPER_EDGE = 2.0
MESH = pl.DeviceIdType.MESH
LANES = 128
DEEP = 4
HALO = 4
OFFSETS = [(i, j, k) for i in (-1, 0, 1) for j in (-1, 0, 1) for k in (-1, 0, 1) if i or j or k]
EDGES = [offset for offset in OFFSETS if offset[2]]


def chebyshev_factors(sweeps):
    centre_value = 0.5 * (UPPER_EDGE + LOWER_EDGE)
    half_width = 0.5 * (UPPER_EDGE - LOWER_EDGE)
    ratio_value = centre_value / half_width
    damping = 1.0 / ratio_value
    factors = [(0.0, 1.0 / centre_value)]
    for _ in range(1, sweeps):
        damping_next = 1.0 / (2.0 * ratio_value - damping)
        factors.append((damping_next * damping, 2.0 * damping_next / half_width))
        damping = damping_next
    return factors


def up8(value):
    return -(-value // 8) * 8


class Level:
    def __init__(self, index, nx, ny, nz, h, shared):
        self.index, self.nx, self.ny, self.nz, self.h, self.shared = index, nx, ny, nz, h, shared
        self.pitch = ny + 2 * h
        self.c0 = up8(self.pitch + 1)
        self.n = up8((nx + 2 * h - 2) * self.pitch)
        self.rows = self.c0 + self.n + up8(self.pitch + 1)
        self.zo = 0 if nz == LANES else h
        self.factor = 0.25**index
        self.wide = nz == LANES and not shared
        self.per = LANES // (2 * h)
        self.halves, self.parts = up8(ny) // 8, -(-nx // self.per)
        self.sends = not shared

    def row(self, x, y):
        return self.c0 + (x + self.h - 1) * self.pitch + y + self.h

    def scratch(self):
        field = pltpu.VMEM((self.n, LANES), jnp.float32)
        padded = pltpu.VMEM((self.rows, LANES), jnp.float32)
        shapes = {name: field for name in ("xm", "xp", "ym", "yp", "zm", "zp", "dg", "iv", "r", "u")}
        shapes.update({name: padded for name in ("d0", "d1", "v", "w")})
        if self.sends:
            for name in ("s", "q"):
                shapes[name + "x"] = pltpu.VMEM((DEEP, 2, self.h * self.ny, LANES), jnp.float32)
                shapes[name + "y"] = pltpu.VMEM((DEEP, 2, self.h * self.nx, LANES), jnp.float32)
                shapes[name + "c"] = pltpu.VMEM((DEEP, 4, self.h * self.h, LANES), jnp.float32)
            shapes["sz"] = pltpu.VMEM((DEEP, self.halves, self.parts, 8, LANES), jnp.float32)
            shapes["qz"] = pltpu.VMEM((DEEP, 18, self.halves, self.parts, 8, LANES), jnp.float32)
            shapes["zone"] = pltpu.VMEM((2 * (2 + self.parts), up8(self.pitch), LANES), jnp.float32)
            shapes["send"] = pltpu.SemaphoreType.DMA((DEEP, 26))
            shapes["recv"] = pltpu.SemaphoreType.DMA((DEEP, 26))
        return shapes

    def groups(self, skip=0):
        skip = skip * self.pitch if self.h > 1 else 0
        first, last = skip, self.n - skip
        count = -(-(last - first) // 96)
        size = up8(-(-(last - first) // count))
        return [(lo, min(size, last - lo)) for lo in range(first, last, size)]


def dot(a, b):
    return jnp.dot(a, b, precision=lax.Precision.HIGHEST, preferred_element_type=jnp.float32)


def iota(shape, dim):
    return lax.broadcasted_iota(jnp.int32, shape, dim)


def roll(value, shift):
    shift %= LANES
    return pltpu.roll(value, shift, 1) if shift else value


def build(mesh_shape, box):
    gxn, gyn, gzn = mesh_shape
    bx, by, bz = box
    local = [Level(i, bx >> i, by >> i, bz >> i, HALO, False) for i in range(3)]
    slab = bx // 4
    rim = Level(0, slab, by, 4 * HALO, HALO, False)
    rim.index, rim.sends = "rim", False
    cx, cy, cz = bx >> 3, by >> 3, bz >> 3
    three = Level(3, gxn * cx, gyn * cy, gzn * cz, 1, True)
    four = Level(4, three.nx // 2, three.ny // 2, three.nz // 2, 1, True)
    levels = local + [rim, three, four]
    blk = cx * cy
    names = [(lv.index, name) for lv in levels for name in lv.scratch()]
    shapes = [shape for lv in levels for shape in lv.scratch().values()]
    extra = {
        "t": pltpu.VMEM((max(lv.rows for lv in levels), LANES), jnp.float32),
        "te": pltpu.VMEM((max(lv.n for lv in levels) + 16, LANES), jnp.float32),
        "to": pltpu.VMEM((max(lv.n for lv in levels) + 16, LANES), jnp.float32),
        "half": pltpu.VMEM((128, LANES), jnp.float32),
        "kin": pltpu.VMEM(box, jnp.float32),
        "bin": pltpu.VMEM(box, jnp.float32),
        "insem": pltpu.SemaphoreType.DMA((2,)),
        "zs": pltpu.VMEM((2, blk, LANES), jnp.float32),
        "zr": pltpu.VMEM((2, gzn, blk, LANES), jnp.float32),
        "ps": pltpu.VMEM((2, blk, LANES), jnp.float32),
        "pr": pltpu.VMEM((2, gxn * gyn, blk, LANES), jnp.float32),
        "zsend": pltpu.SemaphoreType.DMA((2, gzn)),
        "zrecv": pltpu.SemaphoreType.DMA((2, gzn)),
        "psend": pltpu.SemaphoreType.DMA((2, gxn * gyn)),
        "precv": pltpu.SemaphoreType.DMA((2, gxn * gyn)),
    }
    names += [(None, name) for name in extra]
    shapes += list(extra.values())

    def kernel(b_ref, k_ref, u_ref, res_ref, *scratch):
        ref = {key: value for key, value in zip(names, scratch)}
        gx, gy, gz = lax.axis_index("gx"), lax.axis_index("gy"), lax.axis_index("gz")
        plane_peers = [(i, j) for i in range(gxn) for j in range(gyn) if i or j]

        def plane_peer(i, j):
            return lax.rem(gx + i, gxn), lax.rem(gy + j, gyn)

        def depth_peer(k):
            return lax.rem(gz + k, gzn)

        fetches = [
            pltpu.make_async_copy(source, ref[None, name], ref[None, "insem"].at[i])
            for i, (source, name) in enumerate(((k_ref, "kin"), (b_ref, "bin")))
        ]
        for fetch in fetches:
            fetch.start()

        barrier = pltpu.get_barrier_semaphore()
        for i, j in plane_peers:
            px, py = plane_peer(i, j)
            pl.semaphore_signal(barrier, inc=1, device_id=(px, py, gz), device_id_type=MESH)
        for k in range(1, gzn):
            pl.semaphore_signal(barrier, inc=1, device_id=(gx, gy, depth_peer(k)), device_id_type=MESH)

        counters = [0, 0, 0]
        first, middle, last = local
        at = (gx, gy, gz)
        sizes = (gxn, gyn, gzn)

        def there(offset):
            found = jnp.bool_(True)
            for a in range(3):
                if offset[a] < 0:
                    found = found & (at[a] > 0)
                elif offset[a] > 0:
                    found = found & (at[a] < sizes[a] - 1)
            return found

        exists = {offset: there(offset) for offset in OFFSETS}

        def device(offset):
            return tuple(at[a] + offset[a] for a in range(3))

        diagonal = [offset for offset in EDGES if offset[0] or offset[1]]
        for offset in diagonal:
            around_edge = tuple(lax.rem(at[a] + offset[a] + sizes[a], sizes[a]) for a in range(3))
            pl.semaphore_signal(barrier, inc=1, device_id=around_edge, device_id_type=MESH)

        for lv in (three, four):
            for name in ("d0", "d1", "v", "w"):
                ref[lv.index, name][...] = jnp.zeros((lv.rows, LANES), jnp.float32)

        def clear(lv):
            for offset in OFFSETS:

                @pl.when(jnp.logical_not(exists[offset]))
                def _():
                    name, place = landing(offset)
                    piece = ref[lv.index, "q" + name].at[:, place]
                    piece[...] = jnp.zeros(piece.shape, jnp.float32)

        def landing(offset):
            i, j, k = offset
            if k:
                return "z", EDGES.index(offset)
            if i and j:
                return "c", 2 * (i > 0) + (j > 0)
            return ("x", int(i > 0)) if i else ("y", int(j > 0))

        pending = []

        def drain(keep=()):
            for entry in [entry for entry in pending if entry not in keep]:
                pending.remove(entry)
                lv, slot = entry
                for offset in OFFSETS:

                    @pl.when(exists[offset])
                    def _():
                        deep_link(lv, slot, offset, False).wait_send()

        def deep_link(lv, slot, offset, arriving):
            i, j, k = offset
            sent = OFFSETS.index(offset)
            landed = sent if arriving else OFFSETS.index((-i, -j, -k))

            def part(kind, which):
                if k:
                    way_x, way_y = (-i, -j) if arriving else (i, j)
                    rows = pl.ds(0, lv.halves) if not way_y else pl.ds(0 if way_y < 0 else lv.halves - 1, 1)
                    planes = pl.ds(0, lv.parts) if not way_x else pl.ds(0 if way_x < 0 else lv.parts - 1, 1)
                    index = (slot,) if which is None else (slot, which)
                    return ref[lv.index, kind + "z"].at[index + (rows, planes)]
                name = "c" if i and j else "x" if i else "y"
                return ref[lv.index, kind + name].at[slot, which]

            def place(offset):
                if offset[2]:
                    return EDGES.index(offset)
                low_x, low_y = offset[0] > 0, offset[1] > 0
                return 2 * low_x + low_y if offset[0] and offset[1] else int(low_x or low_y)

            return pltpu.make_async_remote_copy(
                src_ref=part("s", None if k else place(offset)),
                dst_ref=part("q", place(OFFSETS[landed])),
                send_sem=ref[lv.index, "send"].at[slot, sent],
                recv_sem=ref[lv.index, "recv"].at[slot, landed],
                device_id=device(offset),
                device_id_type=MESH,
            )

        def deep_start(lv, slot, offsets):
            for offset in offsets:

                @pl.when(exists[offset])
                def _():
                    deep_link(lv, slot, offset, False).start()

        def deep_finish(lv, slot, offsets):
            for offset in offsets:

                @pl.when(exists[offset])
                def _():
                    deep_link(lv, slot, offset, True).wait_recv()

        def near_side(size, direction, h):
            return 0 if direction < 0 else size - h

        def far_side(size, direction, h):
            return -h if direction < 0 else size

        def begin_deep(lv, buf):
            slot = counters[lv.index]
            counters[lv.index] += 1
            pending.append((lv, slot))
            h, nx, ny, nz = lv.h, lv.nx, lv.ny, lv.nz
            out = ref[lv.index, "sz"]
            size = min(ny, 8)
            where = iota((size, LANES), 1)
            for part in range(lv.parts):
                for half in range(lv.halves):
                    packed = jnp.zeros((size, LANES), jnp.float32)
                    for x in range(part * lv.per, min(nx, (part + 1) * lv.per)):
                        value = buf[pl.ds(lv.row(x, 8 * half), size), :]
                        low = 2 * h * (x % lv.per)
                        packed = jnp.where(where >= low, roll(value, low - lv.zo), packed)
                        packed = jnp.where(where >= low + h, roll(value, low + 2 * h - nz - lv.zo), packed)
                    out[slot, half, part, pl.ds(0, size), :] = packed
                    if size < 8:
                        out[slot, half, part, pl.ds(size, 8 - size), :] = packed[: 8 - size]
            deep_start(lv, slot, EDGES)
            for side in (-1, 1):
                x0, y0 = near_side(nx, side, h), near_side(ny, side, h)
                for p in range(h):
                    ref[lv.index, "sx"][slot, int(side > 0), pl.ds(p * ny, ny), :] = buf[pl.ds(lv.row(x0 + p, 0), ny), :]
                    ref[lv.index, "sy"][slot, int(side > 0), pl.ds(p * nx, nx), :] = buf[
                        pl.ds(lv.row(0, y0 + p), nx, stride=lv.pitch), :
                    ]
            for i in (-1, 1):
                for j in (-1, 1):
                    x0, y0 = near_side(nx, i, h), near_side(ny, j, h)
                    for p in range(h):
                        ref[lv.index, "sc"][slot, 2 * (i > 0) + (j > 0), pl.ds(p * h, h), :] = buf[
                            pl.ds(lv.row(x0 + p, y0), h), :
                        ]
            deep_start(lv, slot, [offset for offset in OFFSETS if not offset[2]])
            return slot

        def end_deep(lv, buf, slot, target=None):
            h, nx, ny, nz = lv.h, lv.nx, lv.ny, lv.nz if target is None else rim.nz
            deep_finish(lv, slot, [offset for offset in OFFSETS if not offset[2]])
            for side in (-1, 1):
                x0, y0 = far_side(nx, side, h), far_side(ny, side, h)
                for p in range(h):
                    buf[pl.ds(lv.row(x0 + p, 0), ny), :] = ref[lv.index, "qx"][slot, int(side > 0), pl.ds(p * ny, ny), :]
                    buf[pl.ds(lv.row(0, y0 + p), nx, stride=lv.pitch), :] = ref[lv.index, "qy"][
                        slot, int(side > 0), pl.ds(p * nx, nx), :
                    ]
            for i in (-1, 1):
                for j in (-1, 1):
                    x0, y0 = far_side(nx, i, h), far_side(ny, j, h)
                    for p in range(h):
                        buf[pl.ds(lv.row(x0 + p, y0), h), :] = ref[lv.index, "qc"][
                            slot, 2 * (i > 0) + (j > 0), pl.ds(p * h, h), :
                        ]
            deep_finish(lv, slot, EDGES)
            got, zone = ref[lv.index, "qz"], ref[lv.index, "zone"]
            sources = [(-1, lv.parts - 1)] + [(0, part) for part in range(lv.parts)] + [(1, 0)]
            size = min(ny, 8)
            for place, (i, part) in enumerate(sources):
                for k in (0, 1):
                    side = 2 * k - 1
                    into = zone.at[2 * place + k]
                    into[pl.ds(0, h), :] = got[
                        slot, EDGES.index((i, -1, side)), lv.halves - 1, part, pl.ds(size - h, h), :
                    ]
                    for half in range(lv.halves):
                        into[pl.ds(h + 8 * half, size), :] = got[
                            slot, EDGES.index((i, 0, side)), half, part, pl.ds(0, size), :
                        ]
                    into[pl.ds(h + ny, h), :] = got[slot, EDGES.index((i, 1, side)), 0, part, pl.ds(0, h), :]
            where = iota((lv.pitch, LANES), 1)
            high = (where & (2 * h - 1)) >= h
            merged = []
            for place in range(len(sources)):
                low, up = (zone[2 * place + k, pl.ds(0, lv.pitch), :] for k in (0, 1))
                merged.append(jnp.where(high, low, roll(up, nz + 2 * h)))

            def shifted(x, more):
                i = -1 if x < 0 else 1 if x >= nx else 0
                source = (x - i * nx) % lv.per
                chosen = merged[0 if i < 0 else len(sources) - 1 if i > 0 else 1 + x // lv.per]
                return roll(chosen, more - (2 * h * source + h))

            if target is None:
                edge = (where < h) | ((where >= nz + h) & (where < nz + 2 * h))
                for x in range(-h, nx + h):
                    span = pl.ds(lv.row(x, -h), lv.pitch)
                    buf[span, :] = jnp.where(edge, shifted(x, 0), buf[span, :])
            else:
                group = where & 31
                edge = (group < h) | ((group >= nz + h) & (group < nz + 2 * h))
                for x in range(-h, slab + h):
                    total = jnp.zeros((lv.pitch, LANES), jnp.float32)
                    for g in range(4):
                        inner = buf[pl.ds(lv.row(slab * g + x, -h), lv.pitch), :]
                        inner = jnp.where(group < 3 * h, roll(inner, h + 32 * g), roll(inner, 5 * h + 32 * g))
                        inner = jnp.where(edge, shifted(slab * g + x, 32 * g), inner)
                        total = jnp.where(where >= 32 * g, inner, total)
                    target[pl.ds(rim.row(x, -h), lv.pitch), :] = jnp.where(group < nz + 2 * h, total, 0.0)

        def joined(name, x, from_y, rows):
            g = x // slab
            inner = ref[0, name][pl.ds(first.row(x, from_y) - first.c0, rows), :]
            outer = ref["rim", name][pl.ds(rim.row(x - g * slab, from_y) - rim.c0, rows), :]
            where = iota(inner.shape, 1)
            outer = jnp.where(
                where < LANES // 2, roll(outer, -HALO - 32 * g), roll(outer, LANES - 5 * HALO - 32 * g)
            )
            return jnp.where((where < HALO) | (where >= LANES - HALO), outer, inner)

        def around(lv, buf, lo, rows):
            base, p = lv.c0 + lo, lv.pitch
            if p % 8 == 0:
                block = buf[pl.ds(base - p, rows + 2 * p), :]
                before, mid, after = block[:rows], block[p : p + rows], block[2 * p :]
            else:
                mid = buf[pl.ds(base, rows), :]
                before, after = buf[pl.ds(base - p, rows), :], buf[pl.ds(base + p, rows), :]
            return mid, (
                before,
                after,
                buf[pl.ds(base - 1, rows), :],
                buf[pl.ds(base + 1, rows), :],
                roll(mid, 1),
                roll(mid, -1),
            )

        coeff_names = ("xm", "xp", "ym", "yp", "zm", "zp")

        def applied(lv, buf, lo, rows):
            mid, near = around(lv, buf, lo, rows)
            span = pl.ds(lo, rows)
            total = mid
            for name, value in zip(coeff_names, near):
                total = total - ref[lv.index, name][span, :] * value
            return mid, total

        def prepare(lv, buf):
            for lo, rows in lv.groups():
                span = pl.ds(lo, rows)
                mid, near = around(lv, buf, lo, rows)
                where = iota((rows, LANES), 1)
                near = list(near)
                if lv.shared and lv.nz == LANES:
                    near[4] = jnp.where(where == 0, 0.0, near[4])
                    near[5] = jnp.where(where == LANES - 1, 0.0, near[5])
                couple = [(0.5 * lv.factor) * (mid + value) for value in near]
                diagonal = couple[0]
                for value in couple[1:]:
                    diagonal = diagonal + value
                inverse = jnp.where(mid > 0.0, 1.0 / diagonal, 0.0)
                ref[lv.index, "dg"][span, :] = diagonal
                ref[lv.index, "iv"][span, :] = inverse
                couple = [value * inverse for value in couple]
                if lv.shared and lv.nz == LANES:
                    couple[4] = jnp.where(where == 0, 0.0, couple[4])
                    couple[5] = jnp.where(where == LANES - 1, 0.0, couple[5])
                for name, value in zip(coeff_names, couple):
                    ref[lv.index, name][span, :] = value

        def sweeps(lv, src, count, final):
            factors = chebyshev_factors(count)
            r, u = ref[lv.index, "r"], ref[lv.index, "u"]
            buffers = [ref[lv.index, "d0"], ref[lv.index, "d1"]]
            held, late = src, count == 3
            applications = count - 1 + (src is not None) + final
            skip = lv.h - 1 - applications
            for step in range(count):
                keep, push = factors[step]
                target = buffers[step % 2]
                if held is not None:
                    skip += 1
                for lo, rows in lv.groups(max(skip, 0)):
                    span = pl.ds(lo, rows)
                    value = r[span, :]
                    if held is not None:
                        mid, change = applied(lv, held, lo, rows)
                        value = value - change
                        r[span, :] = value
                    direction = push * value
                    if step > 0:
                        direction = direction + keep * mid
                    padded = pl.ds(lv.c0 + lo, rows)
                    if late and step == count - 1:
                        total = direction + mid + target[padded, :]
                        if src is not None:
                            total = total + src[padded, :] + u[span, :]
                        u[span, :] = total
                    target[padded, :] = direction
                    if not late:
                        u[span, :] = direction if step == 0 else u[span, :] + direction
                held = target
            if final:
                for lo, rows in lv.groups(max(skip + 1, 0)):
                    span = pl.ds(lo, rows)
                    mid, change = applied(lv, held, lo, rows)
                    r[span, :] = r[span, :] - change
            return held

        def halve(lv, buf):
            out = ref[None, "half"]
            nx, ny = lv.nx // 2, lv.ny // 2
            for x in range(nx):
                total = None
                for px in range(2):
                    for py in range(2):
                        at = lv.row(2 * x + px, py)
                        value = buf[pl.ds(at, ny, stride=2), :]
                        total = value if total is None else total + value
                out[pl.ds(x * ny, ny), :] = total
            return nx, ny

        def pair_matrix(lv, offset):
            fine, coarse = iota((LANES, LANES), 0), iota((LANES, LANES), 1)
            cell = fine - lv.zo
            inside = (cell >= 0) & (cell < lv.nz)
            match = lax.shift_right_arithmetic(cell, 1) + offset == coarse
            return jnp.where(inside & match, 0.125, 0.0)

        def restrict(lv, buf, offset):
            nx, ny = halve(lv, buf)
            return nx, ny, dot(ref[None, "half"][pl.ds(0, up8(nx * ny)), :], pair_matrix(lv, offset))

        def spread(nx, ny, value, coarse, buf):
            scratch_ref = ref[None, "half"]
            scratch_ref[pl.ds(0, up8(nx * ny)), :] = value
            for x in range(nx):
                buf[pl.ds(coarse.row(x, 0), ny), :] = scratch_ref[pl.ds(x * ny, ny), :]

        def stretch(cell, offset):
            coarse = iota((LANES, LANES), 0) - offset
            parent = lax.shift_right_arithmetic(cell, 1)
            other = parent + 2 * (cell & 1) - 1
            return jnp.where(coarse == parent, 0.75, 0.0) + jnp.where(coarse == other, 0.25, 0.0)

        def prolong(rows, pitch, origin, value, fine, buf):
            t, te, to = ref[None, "t"], ref[None, "te"], ref[None, "to"]
            t[pl.ds(0, rows), :] = value
            reach = fine.h // 2
            x0, nx, ny = -reach, fine.nx // 2 + 2 * reach, fine.ny // 2 + 2 * reach
            low = origin + x0 * pitch - reach - 1
            n = (nx - 1) * pitch + ny + 2
            mid = 0.75 * t[pl.ds(low, n), :]
            te[pl.ds(0, n), :] = mid + 0.25 * t[pl.ds(low - pitch, n), :]
            to[pl.ds(0, n), :] = mid + 0.25 * t[pl.ds(low + pitch, n), :]
            for x in range(nx):
                for px, src in ((0, te), (1, to)):
                    at = x * pitch + 1
                    mid = 0.75 * src[pl.ds(at, ny), :]
                    to_row = fine.row(2 * (x + x0) + px, -2 * reach)
                    buf[pl.ds(to_row, ny, stride=2), :] = mid + 0.25 * src[pl.ds(at - 1, ny), :]
                    buf[pl.ds(to_row + 1, ny, stride=2), :] = mid + 0.25 * src[pl.ds(at + 1, ny), :]

        def columns(fine):
            return iota((LANES, LANES), 1) - fine.zo

        def depth_copy(which, k):
            return pltpu.make_async_remote_copy(
                src_ref=ref[None, "zs"].at[which],
                dst_ref=ref[None, "zr"].at[which, gz],
                send_sem=ref[None, "zsend"].at[which, k],
                recv_sem=ref[None, "zrecv"].at[which, k],
                device_id=(gx, gy, depth_peer(k)),
                device_id_type=MESH,
            )

        def depth_arrival(which, k):
            source = lax.rem(gz + gzn - k, gzn)
            return pltpu.make_async_remote_copy(
                src_ref=ref[None, "zs"].at[which],
                dst_ref=ref[None, "zr"].at[which, source],
                send_sem=ref[None, "zsend"].at[which, k],
                recv_sem=ref[None, "zrecv"].at[which, k],
                device_id=(gx, gy, depth_peer(k)),
                device_id_type=MESH,
            )

        def plane_copy(which, i, j):
            px, py = plane_peer(i, j)
            return pltpu.make_async_remote_copy(
                src_ref=ref[None, "ps"].at[which],
                dst_ref=ref[None, "pr"].at[which, gx * gyn + gy],
                send_sem=ref[None, "psend"].at[which, i * gyn + j],
                recv_sem=ref[None, "precv"].at[which, i * gyn + j],
                device_id=(px, py, gz),
                device_id_type=MESH,
            )

        def plane_arrival(which, i, j):
            sx, sy = lax.rem(gx + gxn - i, gxn), lax.rem(gy + gyn - j, gyn)
            px, py = plane_peer(i, j)
            return pltpu.make_async_remote_copy(
                src_ref=ref[None, "ps"].at[which],
                dst_ref=ref[None, "pr"].at[which, sx * gyn + sy],
                send_sem=ref[None, "psend"].at[which, i * gyn + j],
                recv_sem=ref[None, "precv"].at[which, i * gyn + j],
                device_id=(px, py, gz),
                device_id_type=MESH,
            )

        def gather_depth_start(which, block):
            ref[None, "zs"][which] = block[:blk]
            for k in range(1, gzn):
                depth_copy(which, k).start()

        def gather_plane_start(which):
            total = ref[None, "zs"][which]
            for k in range(1, gzn):
                depth_arrival(which, k).wait_recv()
            for k in range(1, gzn):
                total = total + ref[None, "zr"][which, lax.rem(gz + k, gzn)]
            ref[None, "ps"][which] = total
            for i, j in plane_peers:
                plane_copy(which, i, j).start()
            ref[None, "pr"][which, gx * gyn + gy] = total

        def gather_end(which, buf):
            for i, j in plane_peers:
                plane_arrival(which, i, j).wait_recv()
            for i in range(gxn):
                for x in range(cx):
                    for y in range(cy):
                        rows = [ref[None, "pr"][which, i * gyn + j, pl.ds(x * cy + y, 1), :] for j in range(gyn)]
                        at = three.row(i * cx + x, y)
                        buf[pl.ds(at, gyn, stride=cy), :] = jnp.concatenate(rows, axis=0)

        def gather_waits():
            for which in range(2):
                for k in range(1, gzn):
                    depth_copy(which, k).wait_send()
                for i, j in plane_peers:
                    plane_copy(which, i, j).wait_send()

        fetches[0].wait()
        for x in range(first.nx):
            ref[0, "v"][pl.ds(first.row(x, 0), first.ny), :] = ref[None, "kin"][x]
        for fine, coarse in ((first, middle), (middle, last)):
            nx, ny, value = restrict(fine, ref[fine.index, "v"], coarse.zo)
            spread(nx, ny, value, coarse, ref[coarse.index, "v"])
        _, _, k_block = restrict(last, ref[2, "v"], gz * cz + three.zo)

        pl.semaphore_wait(barrier, len(plane_peers) + gzn - 1 + len(diagonal))
        slot0 = begin_deep(first, ref[0, "v"])
        fetches[1].wait()
        for x in range(first.nx):
            ref[0, "w"][pl.ds(first.row(x, 0), first.ny), :] = ref[None, "bin"][x]
        slot = begin_deep(first, ref[0, "w"])
        gather_depth_start(0, k_block)
        slot1 = begin_deep(middle, ref[1, "v"])
        slot2 = begin_deep(last, ref[2, "v"])
        for lv in local:
            clear(lv)
        end_deep(first, ref[0, "v"], slot0, ref["rim", "v"])
        prepare(first, ref[0, "v"])
        prepare(rim, ref["rim", "v"])
        end_deep(first, ref[0, "w"], slot, ref["rim", "w"])

        def load(lv):
            ref[lv.index, "r"][...] = ref[lv.index, "w"][pl.ds(lv.c0, lv.n), :] * ref[lv.index, "iv"][...]

        def residual(lv, name):
            ref[lv.index, name][pl.ds(lv.c0, lv.n), :] = ref[lv.index, "r"][...] * ref[lv.index, "dg"][...]

        for lv in (first, rim):
            load(lv)
            sweeps(lv, None, STEPS, True)
        for x in range(0, first.nx, 4):
            rows = 4 * first.pitch
            value = joined("r", x, -HALO, rows)
            ref[0, "v"][pl.ds(first.row(x, -HALO), rows), :] = value
            ref[0, "w"][pl.ds(first.row(x, -HALO), rows), :] = value * joined("dg", x, -HALO, rows)
        nx, ny, value = restrict(first, ref[0, "w"], middle.zo)
        spread(nx, ny, value, middle, ref[1, "w"])
        slot = begin_deep(middle, ref[1, "w"])
        slot0 = begin_deep(first, ref[0, "v"])
        drain(pending[-2:])
        end_deep(middle, ref[1, "v"], slot1)
        prepare(middle, ref[1, "v"])
        gather_plane_start(0)
        end_deep(middle, ref[1, "w"], slot)
        load(middle)
        sweeps(middle, None, STEPS, True)
        residual(middle, "w")
        nx, ny, value = restrict(middle, ref[1, "w"], last.zo)
        spread(nx, ny, value, last, ref[2, "w"])
        slot = begin_deep(last, ref[2, "w"])
        ref[1, "v"][pl.ds(middle.c0, middle.n), :] = ref[1, "r"][...]
        slot1 = begin_deep(middle, ref[1, "v"])
        drain(pending[-2:])
        end_deep(last, ref[2, "v"], slot2)
        prepare(last, ref[2, "v"])
        end_deep(last, ref[2, "w"], slot)
        load(last)
        sweeps(last, None, STEPS, True)
        residual(last, "w")
        _, _, b_block = restrict(last, ref[2, "w"], gz * cz + three.zo)
        gather_depth_start(1, b_block)
        ref[2, "v"][pl.ds(last.c0, last.n), :] = ref[2, "r"][...]
        slot2 = begin_deep(last, ref[2, "v"])
        gather_end(0, ref[3, "v"])
        prepare(three, ref[3, "v"])
        gather_plane_start(1)
        nx, ny, value = restrict(three, ref[3, "v"], four.zo)
        spread(nx, ny, value, four, ref[4, "v"])
        prepare(four, ref[4, "v"])
        end_deep(middle, ref[1, "v"], slot1)
        end_deep(last, ref[2, "v"], slot2)
        end_deep(first, ref[0, "v"], slot0, ref["rim", "v"])
        for lv in (first, rim, middle, last):
            ref[lv.index, "r"][...] = ref[lv.index, "v"][pl.ds(lv.c0, lv.n), :]
        gather_end(1, ref[3, "w"])

        load(three)
        sweeps(three, None, STEPS, True)
        residual(three, "w")
        nx, ny, value = restrict(three, ref[3, "w"], four.zo)
        spread(nx, ny, value, four, ref[4, "w"])
        load(four)
        sweeps(four, None, COARSE_STEPS, False)

        def lift(lv):
            span = pl.ds(lv.c0, lv.n)
            ref[lv.index, "v"][span, :] = jnp.where(ref[lv.index, "iv"][...] > 0.0, ref[lv.index, "v"][span, :], 0.0)
            sweeps(lv, ref[lv.index, "v"], STEPS, lv.index in (0, "rim"))

        def solved(lv):
            ref[lv.index, "w"][pl.ds(lv.c0, lv.n), :] = ref[lv.index, "u"][...]
            return ref[lv.index, "w"]

        field = solved(four)
        prolong(
            four.rows, four.pitch, four.row(0, 0), dot(field[...], stretch(columns(three), four.zo)), three, ref[3, "v"]
        )
        lift(three)
        field = solved(three)

        reach = HALO // 2 + 1
        pitch = cy + 2 * reach
        picked = up8((cx + 2 * reach) * pitch)
        row, source = iota((picked, three.rows), 0), iota((picked, three.rows), 1)
        plane = row // pitch
        cell_x, cell_y = gx * cx - reach + plane, gy * cy - reach + (row - plane * pitch)
        inside = (cell_x >= 0) & (cell_x < three.nx) & (cell_y >= 0) & (cell_y < three.ny)
        wanted = three.row(0, 0) + cell_x * three.pitch + cell_y
        window = dot(jnp.where(inside & (source == wanted), 1.0, 0.0), field[...])
        weights = stretch(columns(last) + gz * last.nz, three.zo)
        prolong(picked, pitch, reach * pitch + reach, dot(window, weights), last, ref[2, "v"])
        lift(last)
        field = solved(last)
        slot = begin_deep(last, field)
        drain(pending[-1:])
        gather_waits()
        end_deep(last, field, slot)
        weights = stretch(columns(middle), last.zo)
        prolong(last.rows, last.pitch, last.row(0, 0), dot(field[...], weights), middle, ref[1, "v"])
        lift(middle)
        field = solved(middle)
        end_deep(middle, field, begin_deep(middle, field))
        drain([pending[-1]])
        column = iota((LANES, LANES), 1)
        prolong(
            middle.rows, middle.pitch, middle.row(0, 0), dot(field[...], stretch(column, middle.zo)), first, ref[0, "v"]
        )
        lift(first)
        group = column & 31
        cells = jnp.where(group < 3 * HALO, group - HALO, group + (LANES - 5 * HALO))
        weights = jnp.where(group < 6 * HALO, stretch(cells, middle.zo), 0.0)
        total, planes = None, slab // 2 + 2 * (HALO // 2 + 1)
        for g in range(4):
            part = field[pl.ds(middle.row(slab // 2 * g - HALO // 2 - 1, -HALO), planes * middle.pitch), :]
            part = dot(part, jnp.where(lax.shift_right_arithmetic(column, 5) == g, weights, 0.0))
            total = part if total is None else total + part
        rows = planes * middle.pitch
        prolong(rows, middle.pitch, (HALO // 2 + 1) * middle.pitch + HALO, total, rim, ref["rim", "v"])
        lift(rim)

        for x in range(first.nx):
            u_ref[x] = joined("u", x, 0, first.ny)
            res_ref[x] = joined("r", x, 0, first.ny) * joined("dg", x, 0, first.ny)

        drain()

    def on_device(right_side, conductivity):
        out = jax.ShapeDtypeStruct(box, jnp.float32)
        return pl.pallas_call(
            kernel,
            out_shape=(out, out),
            in_specs=[pl.BlockSpec(memory_space=pltpu.HBM)] * 2,
            out_specs=[pl.BlockSpec(memory_space=pltpu.VMEM)] * 2,
            scratch_shapes=shapes,
            compiler_params=pltpu.CompilerParams(
                collective_id=0, has_side_effects=True, vmem_limit_bytes=48 * 1024 * 1024
            ),
        )(right_side, conductivity)

    return on_device


def solution(mesh):
    sizes = tuple(mesh.shape[axis] for axis in ("gx", "gy", "gz"))
    spec = P("gx", "gy", "gz")
    return jax.shard_map(
        build(sizes, (32, 16, 128)), mesh=mesh, in_specs=(spec, spec), out_specs=(spec, spec), check_vma=False
    )
```

```python
import jax
import jax.numpy as jnp
from jax import lax
from jax.experimental import pallas as pl
from jax.experimental.pallas import tpu as pltpu
from jax.sharding import PartitionSpec as P

STEPS = 3
COARSE_STEPS = 8
LOWER_EDGE = 0.3
UPPER_EDGE = 2.0
MESH = pl.DeviceIdType.MESH
LANES = 128
DEEP = 4
HALO = 4
OFFSETS = [(i, j, k) for i in (-1, 0, 1) for j in (-1, 0, 1) for k in (-1, 0, 1) if i or j or k]
EDGES = sorted((offset for offset in OFFSETS if offset[2]), key=lambda offset: -sum(map(abs, offset)))


def chebyshev_factors(sweeps):
    centre_value = 0.5 * (UPPER_EDGE + LOWER_EDGE)
    half_width = 0.5 * (UPPER_EDGE - LOWER_EDGE)
    ratio_value = centre_value / half_width
    damping = 1.0 / ratio_value
    factors = [(0.0, 1.0 / centre_value)]
    for _ in range(1, sweeps):
        damping_next = 1.0 / (2.0 * ratio_value - damping)
        factors.append((damping_next * damping, 2.0 * damping_next / half_width))
        damping = damping_next
    return factors


def up8(value):
    return -(-value // 8) * 8


class Level:
    def __init__(self, index, nx, ny, nz, h, shared):
        self.index, self.nx, self.ny, self.nz, self.h, self.shared = index, nx, ny, nz, h, shared
        self.pitch = ny + 2 * h
        self.c0 = up8(self.pitch + 1)
        self.n = up8((nx + 2 * h - 2) * self.pitch)
        self.rows = self.c0 + self.n + up8(self.pitch + 1)
        self.zo = 0 if nz == LANES else h
        self.factor = 0.25**index
        self.wide = nz == LANES and not shared
        self.per = LANES // (2 * h)
        self.halves, self.parts = up8(ny) // 8, -(-nx // self.per)
        self.sends = not shared

    def row(self, x, y):
        return self.c0 + (x + self.h - 1) * self.pitch + y + self.h

    def scratch(self):
        field = pltpu.VMEM((self.n, LANES), jnp.float32)
        padded = pltpu.VMEM((self.rows, LANES), jnp.float32)
        shapes = {name: field for name in ("xm", "xp", "ym", "yp", "zm", "zp", "dg", "iv", "r", "u")}
        shapes.update({name: padded for name in ("d0", "d1", "v", "w")})
        if self.sends:
            for name in ("s", "q"):
                shapes[name + "x"] = pltpu.VMEM((DEEP, 2, self.h * self.ny, LANES), jnp.float32)
                shapes[name + "y"] = pltpu.VMEM((DEEP, 2, self.h * self.nx, LANES), jnp.float32)
                shapes[name + "c"] = pltpu.VMEM((DEEP, 4, self.h * self.h, LANES), jnp.float32)
            shapes["sz"] = pltpu.VMEM((DEEP, self.halves, self.parts, 8, LANES), jnp.float32)
            shapes["qz"] = pltpu.VMEM((DEEP, 18, self.halves, self.parts, 8, LANES), jnp.float32)
            shapes["zone"] = pltpu.VMEM((2 * (2 + self.parts), up8(self.pitch), LANES), jnp.float32)
            shapes["send"] = pltpu.SemaphoreType.DMA((DEEP, 26))
            shapes["recv"] = pltpu.SemaphoreType.DMA((DEEP, 26))
        return shapes

    def groups(self, skip=0):
        skip = skip * self.pitch if self.h > 1 else 0
        first, last = skip, self.n - skip
        count = -(-(last - first) // 144)
        size = up8(-(-(last - first) // count))
        return [(lo, min(size, last - lo)) for lo in range(first, last, size)]


def thirds(value):
    high = value.astype(jnp.bfloat16)
    rest = value - high.astype(jnp.float32)
    middle = rest.astype(jnp.bfloat16)
    return (rest - middle.astype(jnp.float32)).astype(jnp.bfloat16), middle, high


def dot(a, b, exact_left=False):
    if exact_left:
        left = a.astype(jnp.bfloat16)
        pairs = [(left, part) for part in thirds(b)]
    else:
        right = b.astype(jnp.bfloat16)
        pairs = [(part, right) for part in thirds(a)]
    low, middle, high = (jnp.dot(x, y, preferred_element_type=jnp.float32) for x, y in pairs)
    return (low + middle) + high


def iota(shape, dim):
    return lax.broadcasted_iota(jnp.int32, shape, dim)


def roll(value, shift):
    shift %= LANES
    return pltpu.roll(value, shift, 1) if shift else value


def build(mesh_shape, box):
    gxn, gyn, gzn = mesh_shape
    bx, by, bz = box
    local = [Level(i, bx >> i, by >> i, bz >> i, HALO, False) for i in range(3)]
    slab = bx // 4
    rim = Level(0, slab, by, 4 * HALO, HALO, False)
    rim.index, rim.sends = "rim", False
    cx, cy, cz = bx >> 3, by >> 3, bz >> 3
    three = Level(3, gxn * cx, gyn * cy, gzn * cz, 1, True)
    four = Level(4, three.nx // 2, three.ny // 2, three.nz // 2, 1, True)
    levels = local + [rim, three, four]
    blk = cx * cy
    names = [(lv.index, name) for lv in levels for name in lv.scratch()]
    shapes = [shape for lv in levels for shape in lv.scratch().values()]
    extra = {
        "t": pltpu.VMEM((max(lv.rows for lv in levels), LANES), jnp.float32),
        "te": pltpu.VMEM((max(lv.n for lv in levels) + 16, LANES), jnp.float32),
        "to": pltpu.VMEM((max(lv.n for lv in levels) + 16, LANES), jnp.float32),
        "half": pltpu.VMEM((128, LANES), jnp.float32),
        "kin": pltpu.VMEM(box, jnp.float32),
        "bin": pltpu.VMEM(box, jnp.float32),
        "insem": pltpu.SemaphoreType.DMA((2,)),
        "zs": pltpu.VMEM((2, blk, LANES), jnp.float32),
        "zr": pltpu.VMEM((2, gzn, blk, LANES), jnp.float32),
        "ps": pltpu.VMEM((2, blk, LANES), jnp.float32),
        "pr": pltpu.VMEM((2, gxn * gyn, blk, LANES), jnp.float32),
        "zsend": pltpu.SemaphoreType.DMA((2, gzn)),
        "zrecv": pltpu.SemaphoreType.DMA((2, gzn)),
        "psend": pltpu.SemaphoreType.DMA((2, gxn * gyn)),
        "precv": pltpu.SemaphoreType.DMA((2, gxn * gyn)),
    }
    names += [(None, name) for name in extra]
    shapes += list(extra.values())

    def kernel(b_ref, k_ref, u_ref, res_ref, *scratch):
        ref = {key: value for key, value in zip(names, scratch)}
        gx, gy, gz = lax.axis_index("gx"), lax.axis_index("gy"), lax.axis_index("gz")
        plane_peers = [(i, j) for i in range(gxn) for j in range(gyn) if i or j]

        def plane_peer(i, j):
            return lax.rem(gx + i, gxn), lax.rem(gy + j, gyn)

        def depth_peer(k):
            return lax.rem(gz + k, gzn)

        fetches = [
            pltpu.make_async_copy(source, ref[None, name], ref[None, "insem"].at[i])
            for i, (source, name) in enumerate(((k_ref, "kin"), (b_ref, "bin")))
        ]
        for fetch in fetches:
            fetch.start()

        barrier = pltpu.get_barrier_semaphore()
        for i, j in plane_peers:
            px, py = plane_peer(i, j)
            pl.semaphore_signal(barrier, inc=1, device_id=(px, py, gz), device_id_type=MESH)
        for k in range(1, gzn):
            pl.semaphore_signal(barrier, inc=1, device_id=(gx, gy, depth_peer(k)), device_id_type=MESH)

        counters = [0, 0, 0]
        first, middle, last = local
        at = (gx, gy, gz)
        sizes = (gxn, gyn, gzn)

        def there(offset):
            found = jnp.bool_(True)
            for a in range(3):
                if offset[a] < 0:
                    found = found & (at[a] > 0)
                elif offset[a] > 0:
                    found = found & (at[a] < sizes[a] - 1)
            return found

        exists = {offset: there(offset) for offset in OFFSETS}

        def device(offset):
            return tuple(at[a] + offset[a] for a in range(3))

        diagonal = [offset for offset in EDGES if offset[0] or offset[1]]
        for offset in diagonal:
            around_edge = tuple(lax.rem(at[a] + offset[a] + sizes[a], sizes[a]) for a in range(3))
            pl.semaphore_signal(barrier, inc=1, device_id=around_edge, device_id_type=MESH)

        for lv in (three, four):
            for name in ("d0", "d1", "v", "w"):
                ref[lv.index, name][...] = jnp.zeros((lv.rows, LANES), jnp.float32)

        def clear(lv):
            for offset in OFFSETS:

                @pl.when(jnp.logical_not(exists[offset]))
                def _():
                    name, place = landing(offset)
                    piece = ref[lv.index, "q" + name].at[:, place]
                    piece[...] = jnp.zeros(piece.shape, jnp.float32)

        def landing(offset):
            i, j, k = offset
            if k:
                return "z", EDGES.index(offset)
            if i and j:
                return "c", 2 * (i > 0) + (j > 0)
            return ("x", int(i > 0)) if i else ("y", int(j > 0))

        pending = []

        def drain(keep=()):
            for entry in [entry for entry in pending if entry not in keep]:
                pending.remove(entry)
                lv, slot = entry
                for offset in OFFSETS:

                    @pl.when(exists[offset])
                    def _():
                        deep_link(lv, slot, offset, False).wait_send()

        def deep_link(lv, slot, offset, arriving):
            i, j, k = offset
            sent = OFFSETS.index(offset)
            landed = sent if arriving else OFFSETS.index((-i, -j, -k))

            def part(kind, which):
                if k:
                    way_x, way_y = (-i, -j) if arriving else (i, j)
                    rows = pl.ds(0, lv.halves) if not way_y else pl.ds(0 if way_y < 0 else lv.halves - 1, 1)
                    planes = pl.ds(0, lv.parts) if not way_x else pl.ds(0 if way_x < 0 else lv.parts - 1, 1)
                    index = (slot,) if which is None else (slot, which)
                    return ref[lv.index, kind + "z"].at[index + (rows, planes)]
                name = "c" if i and j else "x" if i else "y"
                return ref[lv.index, kind + name].at[slot, which]

            def place(offset):
                if offset[2]:
                    return EDGES.index(offset)
                low_x, low_y = offset[0] > 0, offset[1] > 0
                return 2 * low_x + low_y if offset[0] and offset[1] else int(low_x or low_y)

            return pltpu.make_async_remote_copy(
                src_ref=part("s", None if k else place(offset)),
                dst_ref=part("q", place(OFFSETS[landed])),
                send_sem=ref[lv.index, "send"].at[slot, sent],
                recv_sem=ref[lv.index, "recv"].at[slot, landed],
                device_id=device(offset),
                device_id_type=MESH,
            )

        def deep_start(lv, slot, offsets):
            for offset in offsets:

                @pl.when(exists[offset])
                def _():
                    deep_link(lv, slot, offset, False).start()

        def deep_finish(lv, slot, offsets):
            for offset in offsets:

                @pl.when(exists[offset])
                def _():
                    deep_link(lv, slot, offset, True).wait_recv()

        def near_side(size, direction, h):
            return 0 if direction < 0 else size - h

        def far_side(size, direction, h):
            return -h if direction < 0 else size

        def begin_deep(lv, buf):
            slot = counters[lv.index]
            counters[lv.index] += 1
            pending.append((lv, slot))
            h, nx, ny, nz = lv.h, lv.nx, lv.ny, lv.nz
            out = ref[lv.index, "sz"]
            size = min(ny, 8)
            where = iota((size, LANES), 1)
            for part in range(lv.parts):
                for half in range(lv.halves):
                    packed = jnp.zeros((size, LANES), jnp.float32)
                    for x in range(part * lv.per, min(nx, (part + 1) * lv.per)):
                        value = buf[pl.ds(lv.row(x, 8 * half), size), :]
                        low = 2 * h * (x % lv.per)
                        packed = jnp.where(where >= low, roll(value, low - lv.zo), packed)
                        packed = jnp.where(where >= low + h, roll(value, low + 2 * h - nz - lv.zo), packed)
                    out[slot, half, part, pl.ds(0, size), :] = packed
                    if size < 8:
                        out[slot, half, part, pl.ds(size, 8 - size), :] = packed[: 8 - size]
            deep_start(lv, slot, EDGES)
            for side in (-1, 1):
                x0, y0 = near_side(nx, side, h), near_side(ny, side, h)
                for p in range(h):
                    ref[lv.index, "sx"][slot, int(side > 0), pl.ds(p * ny, ny), :] = buf[pl.ds(lv.row(x0 + p, 0), ny), :]
                    ref[lv.index, "sy"][slot, int(side > 0), pl.ds(p * nx, nx), :] = buf[
                        pl.ds(lv.row(0, y0 + p), nx, stride=lv.pitch), :
                    ]
            for i in (-1, 1):
                for j in (-1, 1):
                    x0, y0 = near_side(nx, i, h), near_side(ny, j, h)
                    for p in range(h):
                        ref[lv.index, "sc"][slot, 2 * (i > 0) + (j > 0), pl.ds(p * h, h), :] = buf[
                            pl.ds(lv.row(x0 + p, y0), h), :
                        ]
            deep_start(lv, slot, [offset for offset in OFFSETS if not offset[2]])
            return slot

        def end_deep(lv, buf, slot, target=None):
            h, nx, ny, nz = lv.h, lv.nx, lv.ny, lv.nz if target is None else rim.nz
            deep_finish(lv, slot, [offset for offset in OFFSETS if not offset[2]])
            for side in (-1, 1):
                x0, y0 = far_side(nx, side, h), far_side(ny, side, h)
                for p in range(h):
                    buf[pl.ds(lv.row(x0 + p, 0), ny), :] = ref[lv.index, "qx"][slot, int(side > 0), pl.ds(p * ny, ny), :]
                    buf[pl.ds(lv.row(0, y0 + p), nx, stride=lv.pitch), :] = ref[lv.index, "qy"][
                        slot, int(side > 0), pl.ds(p * nx, nx), :
                    ]
            for i in (-1, 1):
                for j in (-1, 1):
                    x0, y0 = far_side(nx, i, h), far_side(ny, j, h)
                    for p in range(h):
                        buf[pl.ds(lv.row(x0 + p, y0), h), :] = ref[lv.index, "qc"][
                            slot, 2 * (i > 0) + (j > 0), pl.ds(p * h, h), :
                        ]
            deep_finish(lv, slot, EDGES)
            got, zone = ref[lv.index, "qz"], ref[lv.index, "zone"]
            sources = [(-1, lv.parts - 1)] + [(0, part) for part in range(lv.parts)] + [(1, 0)]
            size = min(ny, 8)
            for place, (i, part) in enumerate(sources):
                for k in (0, 1):
                    side = 2 * k - 1
                    into = zone.at[2 * place + k]
                    into[pl.ds(0, h), :] = got[
                        slot, EDGES.index((i, -1, side)), lv.halves - 1, part, pl.ds(size - h, h), :
                    ]
                    for half in range(lv.halves):
                        into[pl.ds(h + 8 * half, size), :] = got[
                            slot, EDGES.index((i, 0, side)), half, part, pl.ds(0, size), :
                        ]
                    into[pl.ds(h + ny, h), :] = got[slot, EDGES.index((i, 1, side)), 0, part, pl.ds(0, h), :]
            where = iota((lv.pitch, LANES), 1)
            high = (where & (2 * h - 1)) >= h
            merged = []
            for place in range(len(sources)):
                low, up = (zone[2 * place + k, pl.ds(0, lv.pitch), :] for k in (0, 1))
                merged.append(jnp.where(high, low, roll(up, nz + 2 * h)))

            def shifted(x, more):
                i = -1 if x < 0 else 1 if x >= nx else 0
                source = (x - i * nx) % lv.per
                chosen = merged[0 if i < 0 else len(sources) - 1 if i > 0 else 1 + x // lv.per]
                return roll(chosen, more - (2 * h * source + h))

            if target is None:
                edge = (where < h) | ((where >= nz + h) & (where < nz + 2 * h))
                for x in range(-h, nx + h):
                    span = pl.ds(lv.row(x, -h), lv.pitch)
                    buf[span, :] = jnp.where(edge, shifted(x, 0), buf[span, :])
            else:
                group = where & 31
                edge = (group < h) | ((group >= nz + h) & (group < nz + 2 * h))
                for x in range(-h, slab + h):
                    total = jnp.zeros((lv.pitch, LANES), jnp.float32)
                    for g in range(4):
                        inner = buf[pl.ds(lv.row(slab * g + x, -h), lv.pitch), :]
                        inner = jnp.where(group < 3 * h, roll(inner, h + 32 * g), roll(inner, 5 * h + 32 * g))
                        inner = jnp.where(edge, shifted(slab * g + x, 32 * g), inner)
                        total = jnp.where(where >= 32 * g, inner, total)
                    target[pl.ds(rim.row(x, -h), lv.pitch), :] = jnp.where(group < nz + 2 * h, total, 0.0)

        def joined(name, x, from_y, rows):
            g = x // slab
            inner = ref[0, name][pl.ds(first.row(x, from_y) - first.c0, rows), :]
            outer = ref["rim", name][pl.ds(rim.row(x - g * slab, from_y) - rim.c0, rows), :]
            where = iota(inner.shape, 1)
            outer = jnp.where(
                where < LANES // 2, roll(outer, -HALO - 32 * g), roll(outer, LANES - 5 * HALO - 32 * g)
            )
            return jnp.where((where < HALO) | (where >= LANES - HALO), outer, inner)

        def around(lv, buf, lo, rows):
            base, p = lv.c0 + lo, lv.pitch
            if p % 8 == 0:
                block = buf[pl.ds(base - p, rows + 2 * p), :]
                before, mid, after = block[:rows], block[p : p + rows], block[2 * p :]
            else:
                mid = buf[pl.ds(base, rows), :]
                before, after = buf[pl.ds(base - p, rows), :], buf[pl.ds(base + p, rows), :]
            return mid, (
                before,
                after,
                buf[pl.ds(base - 1, rows), :],
                buf[pl.ds(base + 1, rows), :],
                roll(mid, 1),
                roll(mid, -1),
            )

        coeff_names = ("xm", "xp", "ym", "yp", "zm", "zp")

        def applied(lv, buf, lo, rows):
            mid, near = around(lv, buf, lo, rows)
            span = pl.ds(lo, rows)
            total = mid
            for name, value in zip(coeff_names, near):
                total = total - ref[lv.index, name][span, :] * value
            return mid, total

        def prepare(lv, buf):
            for lo, rows in lv.groups():
                span = pl.ds(lo, rows)
                mid, near = around(lv, buf, lo, rows)
                where = iota((rows, LANES), 1)
                near = list(near)
                if lv.shared and lv.nz == LANES:
                    near[4] = jnp.where(where == 0, 0.0, near[4])
                    near[5] = jnp.where(where == LANES - 1, 0.0, near[5])
                couple = [(0.5 * lv.factor) * (mid + value) for value in near]
                diagonal = couple[0]
                for value in couple[1:]:
                    diagonal = diagonal + value
                inverse = jnp.where(mid > 0.0, 1.0 / diagonal, 0.0)
                ref[lv.index, "dg"][span, :] = diagonal
                ref[lv.index, "iv"][span, :] = inverse
                couple = [value * inverse for value in couple]
                if lv.shared and lv.nz == LANES:
                    couple[4] = jnp.where(where == 0, 0.0, couple[4])
                    couple[5] = jnp.where(where == LANES - 1, 0.0, couple[5])
                for name, value in zip(coeff_names, couple):
                    ref[lv.index, name][span, :] = value

        def sweeps(lv, src, count, final):
            factors = chebyshev_factors(count)
            r, u = ref[lv.index, "r"], ref[lv.index, "u"]
            buffers = [ref[lv.index, "d0"], ref[lv.index, "d1"]]
            held, late = src, count == 3
            applications = count - 1 + (src is not None) + final
            skip = lv.h - 1 - applications
            for step in range(count):
                keep, push = factors[step]
                target = buffers[step % 2]
                if held is not None:
                    skip += 1
                for lo, rows in lv.groups(max(skip, 0)):
                    span = pl.ds(lo, rows)
                    value = r[span, :]
                    if held is not None:
                        mid, change = applied(lv, held, lo, rows)
                        value = value - change
                        r[span, :] = value
                    direction = push * value
                    if step > 0:
                        direction = direction + keep * mid
                    padded = pl.ds(lv.c0 + lo, rows)
                    if late and step == count - 1:
                        total = direction + mid + target[padded, :]
                        if src is not None:
                            total = total + src[padded, :] + u[span, :]
                        u[span, :] = total
                    target[padded, :] = direction
                    if not late:
                        u[span, :] = direction if step == 0 else u[span, :] + direction
                held = target
            if final:
                for lo, rows in lv.groups(max(skip + 1, 0)):
                    span = pl.ds(lo, rows)
                    mid, change = applied(lv, held, lo, rows)
                    r[span, :] = r[span, :] - change
            return held

        def halve(lv, buf):
            out = ref[None, "half"]
            nx, ny = lv.nx // 2, lv.ny // 2
            for x in range(nx):
                total = None
                for px in range(2):
                    for py in range(2):
                        at = lv.row(2 * x + px, py)
                        value = buf[pl.ds(at, ny, stride=2), :]
                        total = value if total is None else total + value
                out[pl.ds(x * ny, ny), :] = total
            return nx, ny

        def pair_matrix(lv, offset):
            fine, coarse = iota((LANES, LANES), 0), iota((LANES, LANES), 1)
            cell = fine - lv.zo
            inside = (cell >= 0) & (cell < lv.nz)
            match = lax.shift_right_arithmetic(cell, 1) + offset == coarse
            return jnp.where(inside & match, 0.125, 0.0)

        def restrict(lv, buf, offset):
            nx, ny = halve(lv, buf)
            return nx, ny, dot(ref[None, "half"][pl.ds(0, up8(nx * ny)), :], pair_matrix(lv, offset))

        def spread(nx, ny, value, coarse, buf):
            scratch_ref = ref[None, "half"]
            scratch_ref[pl.ds(0, up8(nx * ny)), :] = value
            for x in range(nx):
                buf[pl.ds(coarse.row(x, 0), ny), :] = scratch_ref[pl.ds(x * ny, ny), :]

        def stretch(cell, offset):
            coarse = iota((LANES, LANES), 0) - offset
            parent = lax.shift_right_arithmetic(cell, 1)
            other = parent + 2 * (cell & 1) - 1
            return jnp.where(coarse == parent, 0.75, 0.0) + jnp.where(coarse == other, 0.25, 0.0)

        def prolong(rows, pitch, origin, value, fine, buf):
            t, te, to = ref[None, "t"], ref[None, "te"], ref[None, "to"]
            t[pl.ds(0, rows), :] = value
            reach = fine.h // 2
            x0, nx, ny = -reach, fine.nx // 2 + 2 * reach, fine.ny // 2 + 2 * reach
            low = origin + x0 * pitch - reach - 1
            n = (nx - 1) * pitch + ny + 2
            mid = 0.75 * t[pl.ds(low, n), :]
            te[pl.ds(0, n), :] = mid + 0.25 * t[pl.ds(low - pitch, n), :]
            to[pl.ds(0, n), :] = mid + 0.25 * t[pl.ds(low + pitch, n), :]
            for x in range(nx):
                for px, src in ((0, te), (1, to)):
                    at = x * pitch + 1
                    mid = 0.75 * src[pl.ds(at, ny), :]
                    to_row = fine.row(2 * (x + x0) + px, -2 * reach)
                    buf[pl.ds(to_row, ny, stride=2), :] = mid + 0.25 * src[pl.ds(at - 1, ny), :]
                    buf[pl.ds(to_row + 1, ny, stride=2), :] = mid + 0.25 * src[pl.ds(at + 1, ny), :]

        def columns(fine):
            return iota((LANES, LANES), 1) - fine.zo

        def depth_copy(which, k):
            return pltpu.make_async_remote_copy(
                src_ref=ref[None, "zs"].at[which],
                dst_ref=ref[None, "zr"].at[which, gz],
                send_sem=ref[None, "zsend"].at[which, k],
                recv_sem=ref[None, "zrecv"].at[which, k],
                device_id=(gx, gy, depth_peer(k)),
                device_id_type=MESH,
            )

        def depth_arrival(which, k):
            source = lax.rem(gz + gzn - k, gzn)
            return pltpu.make_async_remote_copy(
                src_ref=ref[None, "zs"].at[which],
                dst_ref=ref[None, "zr"].at[which, source],
                send_sem=ref[None, "zsend"].at[which, k],
                recv_sem=ref[None, "zrecv"].at[which, k],
                device_id=(gx, gy, depth_peer(k)),
                device_id_type=MESH,
            )

        def plane_copy(which, i, j):
            px, py = plane_peer(i, j)
            return pltpu.make_async_remote_copy(
                src_ref=ref[None, "ps"].at[which],
                dst_ref=ref[None, "pr"].at[which, gx * gyn + gy],
                send_sem=ref[None, "psend"].at[which, i * gyn + j],
                recv_sem=ref[None, "precv"].at[which, i * gyn + j],
                device_id=(px, py, gz),
                device_id_type=MESH,
            )

        def plane_arrival(which, i, j):
            sx, sy = lax.rem(gx + gxn - i, gxn), lax.rem(gy + gyn - j, gyn)
            px, py = plane_peer(i, j)
            return pltpu.make_async_remote_copy(
                src_ref=ref[None, "ps"].at[which],
                dst_ref=ref[None, "pr"].at[which, sx * gyn + sy],
                send_sem=ref[None, "psend"].at[which, i * gyn + j],
                recv_sem=ref[None, "precv"].at[which, i * gyn + j],
                device_id=(px, py, gz),
                device_id_type=MESH,
            )

        def gather_depth_start(which, block):
            ref[None, "zs"][which] = block[:blk]
            for k in range(1, gzn):
                depth_copy(which, k).start()

        def gather_plane_start(which):
            total = ref[None, "zs"][which]
            for k in range(1, gzn):
                depth_arrival(which, k).wait_recv()
            for k in range(1, gzn):
                total = total + ref[None, "zr"][which, lax.rem(gz + k, gzn)]
            ref[None, "ps"][which] = total
            for i, j in plane_peers:
                plane_copy(which, i, j).start()
            ref[None, "pr"][which, gx * gyn + gy] = total

        def gather_end(which, buf):
            for i, j in plane_peers:
                plane_arrival(which, i, j).wait_recv()
            for i in range(gxn):
                for x in range(cx):
                    for y in range(cy):
                        rows = [ref[None, "pr"][which, i * gyn + j, pl.ds(x * cy + y, 1), :] for j in range(gyn)]
                        at = three.row(i * cx + x, y)
                        buf[pl.ds(at, gyn, stride=cy), :] = jnp.concatenate(rows, axis=0)

        def gather_waits():
            for which in range(2):
                for k in range(1, gzn):
                    depth_copy(which, k).wait_send()
                for i, j in plane_peers:
                    plane_copy(which, i, j).wait_send()

        fetches[0].wait()
        for x in range(first.nx):
            ref[0, "v"][pl.ds(first.row(x, 0), first.ny), :] = ref[None, "kin"][x]
        for fine, coarse in ((first, middle), (middle, last)):
            nx, ny, value = restrict(fine, ref[fine.index, "v"], coarse.zo)
            spread(nx, ny, value, coarse, ref[coarse.index, "v"])
        _, _, k_block = restrict(last, ref[2, "v"], gz * cz + three.zo)

        pl.semaphore_wait(barrier, len(plane_peers) + gzn - 1 + len(diagonal))
        slot0 = begin_deep(first, ref[0, "v"])
        fetches[1].wait()
        for x in range(first.nx):
            ref[0, "w"][pl.ds(first.row(x, 0), first.ny), :] = ref[None, "bin"][x]
        slot = begin_deep(first, ref[0, "w"])
        gather_depth_start(0, k_block)
        slot1 = begin_deep(middle, ref[1, "v"])
        slot2 = begin_deep(last, ref[2, "v"])
        for lv in local:
            clear(lv)
        end_deep(first, ref[0, "v"], slot0, ref["rim", "v"])
        prepare(first, ref[0, "v"])
        prepare(rim, ref["rim", "v"])
        end_deep(first, ref[0, "w"], slot, ref["rim", "w"])

        def load(lv):
            ref[lv.index, "r"][...] = ref[lv.index, "w"][pl.ds(lv.c0, lv.n), :] * ref[lv.index, "iv"][...]

        def residual(lv, name):
            ref[lv.index, name][pl.ds(lv.c0, lv.n), :] = ref[lv.index, "r"][...] * ref[lv.index, "dg"][...]

        for lv in (first, rim):
            load(lv)
            sweeps(lv, None, STEPS, True)
        for x in range(0, first.nx, 4):
            rows = 4 * first.pitch
            value = joined("r", x, -HALO, rows)
            ref[0, "v"][pl.ds(first.row(x, -HALO), rows), :] = value
            ref[0, "w"][pl.ds(first.row(x, -HALO), rows), :] = value * joined("dg", x, -HALO, rows)
        nx, ny, value = restrict(first, ref[0, "w"], middle.zo)
        spread(nx, ny, value, middle, ref[1, "w"])
        slot = begin_deep(middle, ref[1, "w"])
        slot0 = begin_deep(first, ref[0, "v"])
        drain(pending[-2:])
        end_deep(middle, ref[1, "v"], slot1)
        prepare(middle, ref[1, "v"])
        gather_plane_start(0)
        end_deep(middle, ref[1, "w"], slot)
        load(middle)
        sweeps(middle, None, STEPS, True)
        residual(middle, "w")
        nx, ny, value = restrict(middle, ref[1, "w"], last.zo)
        spread(nx, ny, value, last, ref[2, "w"])
        slot = begin_deep(last, ref[2, "w"])
        ref[1, "v"][pl.ds(middle.c0, middle.n), :] = ref[1, "r"][...]
        slot1 = begin_deep(middle, ref[1, "v"])
        drain(pending[-2:])
        end_deep(last, ref[2, "v"], slot2)
        prepare(last, ref[2, "v"])
        end_deep(last, ref[2, "w"], slot)
        load(last)
        sweeps(last, None, STEPS, True)
        residual(last, "w")
        _, _, b_block = restrict(last, ref[2, "w"], gz * cz + three.zo)
        gather_depth_start(1, b_block)
        ref[2, "v"][pl.ds(last.c0, last.n), :] = ref[2, "r"][...]
        slot2 = begin_deep(last, ref[2, "v"])
        gather_end(0, ref[3, "v"])
        prepare(three, ref[3, "v"])
        gather_plane_start(1)
        nx, ny, value = restrict(three, ref[3, "v"], four.zo)
        spread(nx, ny, value, four, ref[4, "v"])
        prepare(four, ref[4, "v"])
        end_deep(middle, ref[1, "v"], slot1)
        end_deep(last, ref[2, "v"], slot2)
        end_deep(first, ref[0, "v"], slot0, ref["rim", "v"])
        for lv in (first, rim, middle, last):
            ref[lv.index, "r"][...] = ref[lv.index, "v"][pl.ds(lv.c0, lv.n), :]
        gather_end(1, ref[3, "w"])

        load(three)
        sweeps(three, None, STEPS, True)
        residual(three, "w")
        nx, ny, value = restrict(three, ref[3, "w"], four.zo)
        spread(nx, ny, value, four, ref[4, "w"])
        load(four)
        sweeps(four, None, COARSE_STEPS, False)

        def lift(lv):
            span = pl.ds(lv.c0, lv.n)
            ref[lv.index, "v"][span, :] = jnp.where(ref[lv.index, "iv"][...] > 0.0, ref[lv.index, "v"][span, :], 0.0)
            sweeps(lv, ref[lv.index, "v"], STEPS, lv.index in (0, "rim"))

        def solved(lv):
            ref[lv.index, "w"][pl.ds(lv.c0, lv.n), :] = ref[lv.index, "u"][...]
            return ref[lv.index, "w"]

        field = solved(four)
        prolong(
            four.rows, four.pitch, four.row(0, 0), dot(field[...], stretch(columns(three), four.zo)), three, ref[3, "v"]
        )
        lift(three)
        field = solved(three)

        reach = HALO // 2 + 1
        pitch = cy + 2 * reach
        picked = up8((cx + 2 * reach) * pitch)
        row, source = iota((picked, three.rows), 0), iota((picked, three.rows), 1)
        plane = row // pitch
        cell_x, cell_y = gx * cx - reach + plane, gy * cy - reach + (row - plane * pitch)
        inside = (cell_x >= 0) & (cell_x < three.nx) & (cell_y >= 0) & (cell_y < three.ny)
        wanted = three.row(0, 0) + cell_x * three.pitch + cell_y
        window = dot(jnp.where(inside & (source == wanted), 1.0, 0.0), field[...], True)
        weights = stretch(columns(last) + gz * last.nz, three.zo)
        prolong(picked, pitch, reach * pitch + reach, dot(window, weights), last, ref[2, "v"])
        lift(last)
        field = solved(last)
        slot = begin_deep(last, field)
        drain(pending[-1:])
        gather_waits()
        end_deep(last, field, slot)
        weights = stretch(columns(middle), last.zo)
        prolong(last.rows, last.pitch, last.row(0, 0), dot(field[...], weights), middle, ref[1, "v"])
        lift(middle)
        field = solved(middle)
        end_deep(middle, field, begin_deep(middle, field))
        drain([pending[-1]])
        column = iota((LANES, LANES), 1)
        prolong(
            middle.rows, middle.pitch, middle.row(0, 0), dot(field[...], stretch(column, middle.zo)), first, ref[0, "v"]
        )
        lift(first)
        group = column & 31
        cells = jnp.where(group < 3 * HALO, group - HALO, group + (LANES - 5 * HALO))
        weights = jnp.where(group < 6 * HALO, stretch(cells, middle.zo), 0.0)
        total, planes = None, slab // 2 + 2 * (HALO // 2 + 1)
        for g in range(4):
            part = field[pl.ds(middle.row(slab // 2 * g - HALO // 2 - 1, -HALO), planes * middle.pitch), :]
            part = dot(part, jnp.where(lax.shift_right_arithmetic(column, 5) == g, weights, 0.0))
            total = part if total is None else total + part
        rows = planes * middle.pitch
        prolong(rows, middle.pitch, (HALO // 2 + 1) * middle.pitch + HALO, total, rim, ref["rim", "v"])
        lift(rim)

        for x in range(first.nx):
            u_ref[x] = joined("u", x, 0, first.ny)
            res_ref[x] = joined("r", x, 0, first.ny) * joined("dg", x, 0, first.ny)

        drain()

    def on_device(right_side, conductivity):
        out = jax.ShapeDtypeStruct(box, jnp.float32)
        return pl.pallas_call(
            kernel,
            out_shape=(out, out),
            in_specs=[pl.BlockSpec(memory_space=pltpu.HBM)] * 2,
            out_specs=[pl.BlockSpec(memory_space=pltpu.VMEM)] * 2,
            scratch_shapes=shapes,
            compiler_params=pltpu.CompilerParams(
                collective_id=0, has_side_effects=True, vmem_limit_bytes=48 * 1024 * 1024
            ),
        )(right_side, conductivity)

    return on_device


def solution(mesh):
    sizes = tuple(mesh.shape[axis] for axis in ("gx", "gy", "gz"))
    spec = P("gx", "gy", "gz")
    return jax.shard_map(
        build(sizes, (32, 16, 128)), mesh=mesh, in_specs=(spec, spec), out_specs=(spec, spec), check_vma=False
    )
```

```python
import jax
import jax.numpy as jnp
from jax import lax
from jax.experimental import pallas as pl
from jax.experimental.pallas import tpu as pltpu
from jax.sharding import PartitionSpec as P

STEPS = 3
COARSE_STEPS = 8
LOWER_EDGE = 0.3
UPPER_EDGE = 2.0
MESH = pl.DeviceIdType.MESH
LANES = 128
DEEP = 4
HALO = 4
OFFSETS = [(i, j, k) for i in (-1, 0, 1) for j in (-1, 0, 1) for k in (-1, 0, 1) if i or j or k]
EDGES = sorted((offset for offset in OFFSETS if offset[2]), key=lambda offset: -sum(map(abs, offset)))


def chebyshev_factors(sweeps):
    centre_value = 0.5 * (UPPER_EDGE + LOWER_EDGE)
    half_width = 0.5 * (UPPER_EDGE - LOWER_EDGE)
    ratio_value = centre_value / half_width
    damping = 1.0 / ratio_value
    factors = [(0.0, 1.0 / centre_value)]
    for _ in range(1, sweeps):
        damping_next = 1.0 / (2.0 * ratio_value - damping)
        factors.append((damping_next * damping, 2.0 * damping_next / half_width))
        damping = damping_next
    return factors


def up8(value):
    return -(-value // 8) * 8


class Level:
    def __init__(self, index, nx, ny, nz, h, shared):
        self.index, self.nx, self.ny, self.nz, self.h, self.shared = index, nx, ny, nz, h, shared
        self.pitch = ny + 2 * h
        self.c0 = up8(self.pitch + 1)
        self.n = up8((nx + 2 * h - 2) * self.pitch)
        self.rows = self.c0 + self.n + up8(self.pitch + 1)
        self.zo = 0 if nz == LANES else h
        self.factor = 0.25**index
        self.wide = nz == LANES and not shared
        self.per = LANES // (2 * h)
        self.halves, self.parts = up8(ny) // 8, -(-nx // self.per)
        self.sends = not shared

    def row(self, x, y):
        return self.c0 + (x + self.h - 1) * self.pitch + y + self.h

    def scratch(self):
        field = pltpu.VMEM((self.n, LANES), jnp.float32)
        padded = pltpu.VMEM((self.rows, LANES), jnp.float32)
        shapes = {name: field for name in ("xm", "xp", "ym", "yp", "zm", "zp", "dg", "iv", "r", "u")}
        shapes.update({name: padded for name in ("d0", "d1", "v", "w")})
        if self.sends:
            for name in ("s", "q"):
                shapes[name + "x"] = pltpu.VMEM((DEEP, 2, self.h * self.ny, LANES), jnp.float32)
                shapes[name + "y"] = pltpu.VMEM((DEEP, 2, self.h * self.nx, LANES), jnp.float32)
                shapes[name + "c"] = pltpu.VMEM((DEEP, 4, self.h * self.h, LANES), jnp.float32)
            shapes["sz"] = pltpu.VMEM((DEEP, self.halves, self.parts, 8, LANES), jnp.float32)
            shapes["qz"] = pltpu.VMEM((DEEP, 18, self.halves, self.parts, 8, LANES), jnp.float32)
            shapes["zone"] = pltpu.VMEM((2 * (2 + self.parts), up8(self.pitch), LANES), jnp.float32)
            shapes["send"] = pltpu.SemaphoreType.DMA((DEEP, 26))
            shapes["recv"] = pltpu.SemaphoreType.DMA((DEEP, 26))
        return shapes

    def groups(self, skip=0):
        skip = skip * self.pitch if self.h > 1 else 0
        first, last = skip, self.n - skip
        count = -(-(last - first) // 144)
        size = up8(-(-(last - first) // count))
        return [(lo, min(size, last - lo)) for lo in range(first, last, size)]


def thirds(value):
    high = value.astype(jnp.bfloat16)
    rest = value - high.astype(jnp.float32)
    middle = rest.astype(jnp.bfloat16)
    return (rest - middle.astype(jnp.float32)).astype(jnp.bfloat16), middle, high


def dot(a, b, exact_left=False):
    if exact_left:
        left = a.astype(jnp.bfloat16)
        pairs = [(left, part) for part in thirds(b)]
    else:
        right = b.astype(jnp.bfloat16)
        pairs = [(part, right) for part in thirds(a)]
    low, middle, high = (jnp.dot(x, y, preferred_element_type=jnp.float32) for x, y in pairs)
    return (low + middle) + high


def iota(shape, dim):
    return lax.broadcasted_iota(jnp.int32, shape, dim)


def roll(value, shift):
    shift %= LANES
    return pltpu.roll(value, shift, 1) if shift else value


def build(mesh_shape, box):
    gxn, gyn, gzn = mesh_shape
    bx, by, bz = box
    local = [Level(i, bx >> i, by >> i, bz >> i, HALO, False) for i in range(3)]
    slab = bx // 4
    rim = Level(0, slab, by, 4 * HALO, HALO, False)
    rim.index, rim.sends = "rim", False
    cx, cy, cz = bx >> 3, by >> 3, bz >> 3
    three = Level(3, gxn * cx, gyn * cy, gzn * cz, 1, True)
    four = Level(4, three.nx // 2, three.ny // 2, three.nz // 2, 1, True)
    levels = local + [rim, three, four]
    blk = cx * cy
    names = [(lv.index, name) for lv in levels for name in lv.scratch()]
    shapes = [shape for lv in levels for shape in lv.scratch().values()]
    extra = {
        "t": pltpu.VMEM((max(lv.rows for lv in levels), LANES), jnp.float32),
        "te": pltpu.VMEM((max(lv.n for lv in levels) + 16, LANES), jnp.float32),
        "to": pltpu.VMEM((max(lv.n for lv in levels) + 16, LANES), jnp.float32),
        "half": pltpu.VMEM((128, LANES), jnp.float32),
        "kin": pltpu.VMEM(box, jnp.float32),
        "bin": pltpu.VMEM(box, jnp.float32),
        "insem": pltpu.SemaphoreType.DMA((2,)),
        "zs": pltpu.VMEM((2, blk, LANES), jnp.float32),
        "zr": pltpu.VMEM((2, gzn, blk, LANES), jnp.float32),
        "ps": pltpu.VMEM((2, blk, LANES), jnp.float32),
        "pr": pltpu.VMEM((2, gxn * gyn, blk, LANES), jnp.float32),
        "zsend": pltpu.SemaphoreType.DMA((2, gzn)),
        "zrecv": pltpu.SemaphoreType.DMA((2, gzn)),
        "psend": pltpu.SemaphoreType.DMA((2, gxn * gyn)),
        "precv": pltpu.SemaphoreType.DMA((2, gxn * gyn)),
    }
    names += [(None, name) for name in extra]
    shapes += list(extra.values())

    def kernel(b_ref, k_ref, u_ref, res_ref, *scratch):
        ref = {key: value for key, value in zip(names, scratch)}
        gx, gy, gz = lax.axis_index("gx"), lax.axis_index("gy"), lax.axis_index("gz")
        plane_peers = [(i, j) for i in range(gxn) for j in range(gyn) if i or j]
        plane_peers.sort(key=lambda peer: -min(peer[0], gxn - peer[0]) - 0.5 * min(peer[1], gyn - peer[1]))
        depth_peers = sorted(range(1, gzn), key=lambda k: -min(k, gzn - k))

        def plane_peer(i, j):
            return lax.rem(gx + i, gxn), lax.rem(gy + j, gyn)

        def depth_peer(k):
            return lax.rem(gz + k, gzn)

        fetches = [
            pltpu.make_async_copy(source, ref[None, name], ref[None, "insem"].at[i])
            for i, (source, name) in enumerate(((k_ref, "kin"), (b_ref, "bin")))
        ]
        for fetch in fetches:
            fetch.start()

        barrier = pltpu.get_barrier_semaphore()
        counters = [0, 0, 0]
        first, middle, last = local
        at = (gx, gy, gz)
        sizes = (gxn, gyn, gzn)

        def there(offset):
            found = jnp.bool_(True)
            for a in range(3):
                if offset[a] < 0:
                    found = found & (at[a] > 0)
                elif offset[a] > 0:
                    found = found & (at[a] < sizes[a] - 1)
            return found

        exists = {offset: there(offset) for offset in OFFSETS}

        def device(offset):
            return tuple(at[a] + offset[a] for a in range(3))

        diagonal = [offset for offset in EDGES if offset[0] or offset[1]]
        for k in depth_peers:
            pl.semaphore_signal(barrier, inc=1, device_id=(gx, gy, depth_peer(k)), device_id_type=MESH)
        greeted = [(*plane_peer(i, j), gz) for i, j in plane_peers]
        around_edge = [tuple(lax.rem(at[a] + o[a] + sizes[a], sizes[a]) for a in range(3)) for o in diagonal]
        for place in greeted[:16] + around_edge + greeted[16:]:
            pl.semaphore_signal(barrier, inc=1, device_id=place, device_id_type=MESH)

        for lv in (three, four):
            for name in ("d0", "d1", "v", "w"):
                ref[lv.index, name][...] = jnp.zeros((lv.rows, LANES), jnp.float32)

        def clear(lv):
            for offset in OFFSETS:

                @pl.when(jnp.logical_not(exists[offset]))
                def _():
                    name, place = landing(offset)
                    piece = ref[lv.index, "q" + name].at[:, place]
                    piece[...] = jnp.zeros(piece.shape, jnp.float32)

        def landing(offset):
            i, j, k = offset
            if k:
                return "z", EDGES.index(offset)
            if i and j:
                return "c", 2 * (i > 0) + (j > 0)
            return ("x", int(i > 0)) if i else ("y", int(j > 0))

        pending = []

        def drain(keep=()):
            for entry in [entry for entry in pending if entry not in keep]:
                pending.remove(entry)
                lv, slot = entry
                for offset in OFFSETS:

                    @pl.when(exists[offset])
                    def _():
                        deep_link(lv, slot, offset, False).wait_send()

        def deep_link(lv, slot, offset, arriving):
            i, j, k = offset
            sent = OFFSETS.index(offset)
            landed = sent if arriving else OFFSETS.index((-i, -j, -k))

            def part(kind, which):
                if k:
                    way_x, way_y = (-i, -j) if arriving else (i, j)
                    rows = pl.ds(0, lv.halves) if not way_y else pl.ds(0 if way_y < 0 else lv.halves - 1, 1)
                    planes = pl.ds(0, lv.parts) if not way_x else pl.ds(0 if way_x < 0 else lv.parts - 1, 1)
                    index = (slot,) if which is None else (slot, which)
                    return ref[lv.index, kind + "z"].at[index + (rows, planes)]
                name = "c" if i and j else "x" if i else "y"
                return ref[lv.index, kind + name].at[slot, which]

            def place(offset):
                if offset[2]:
                    return EDGES.index(offset)
                low_x, low_y = offset[0] > 0, offset[1] > 0
                return 2 * low_x + low_y if offset[0] and offset[1] else int(low_x or low_y)

            return pltpu.make_async_remote_copy(
                src_ref=part("s", None if k else place(offset)),
                dst_ref=part("q", place(OFFSETS[landed])),
                send_sem=ref[lv.index, "send"].at[slot, sent],
                recv_sem=ref[lv.index, "recv"].at[slot, landed],
                device_id=device(offset),
                device_id_type=MESH,
            )

        def deep_start(lv, slot, offsets):
            for offset in offsets:

                @pl.when(exists[offset])
                def _():
                    deep_link(lv, slot, offset, False).start()

        def deep_finish(lv, slot, offsets):
            for offset in offsets:

                @pl.when(exists[offset])
                def _():
                    deep_link(lv, slot, offset, True).wait_recv()

        def near_side(size, direction, h):
            return 0 if direction < 0 else size - h

        def far_side(size, direction, h):
            return -h if direction < 0 else size

        def begin_deep(lv, buf):
            slot = counters[lv.index]
            counters[lv.index] += 1
            pending.append((lv, slot))
            h, nx, ny, nz = lv.h, lv.nx, lv.ny, lv.nz
            out = ref[lv.index, "sz"]
            size = min(ny, 8)
            where = iota((size, LANES), 1)
            for part in range(lv.parts):
                for half in range(lv.halves):
                    packed = jnp.zeros((size, LANES), jnp.float32)
                    for x in range(part * lv.per, min(nx, (part + 1) * lv.per)):
                        value = buf[pl.ds(lv.row(x, 8 * half), size), :]
                        low = 2 * h * (x % lv.per)
                        packed = jnp.where(where >= low, roll(value, low - lv.zo), packed)
                        packed = jnp.where(where >= low + h, roll(value, low + 2 * h - nz - lv.zo), packed)
                    out[slot, half, part, pl.ds(0, size), :] = packed
                    if size < 8:
                        out[slot, half, part, pl.ds(size, 8 - size), :] = packed[: 8 - size]
            deep_start(lv, slot, EDGES)
            for side in (-1, 1):
                x0, y0 = near_side(nx, side, h), near_side(ny, side, h)
                for p in range(h):
                    ref[lv.index, "sx"][slot, int(side > 0), pl.ds(p * ny, ny), :] = buf[pl.ds(lv.row(x0 + p, 0), ny), :]
                    ref[lv.index, "sy"][slot, int(side > 0), pl.ds(p * nx, nx), :] = buf[
                        pl.ds(lv.row(0, y0 + p), nx, stride=lv.pitch), :
                    ]
            for i in (-1, 1):
                for j in (-1, 1):
                    x0, y0 = near_side(nx, i, h), near_side(ny, j, h)
                    for p in range(h):
                        ref[lv.index, "sc"][slot, 2 * (i > 0) + (j > 0), pl.ds(p * h, h), :] = buf[
                            pl.ds(lv.row(x0 + p, y0), h), :
                        ]
            deep_start(lv, slot, [offset for offset in OFFSETS if not offset[2]])
            return slot

        def end_deep(lv, buf, slot, target=None):
            h, nx, ny, nz = lv.h, lv.nx, lv.ny, lv.nz if target is None else rim.nz
            deep_finish(lv, slot, [offset for offset in OFFSETS if not offset[2]])
            for side in (-1, 1):
                x0, y0 = far_side(nx, side, h), far_side(ny, side, h)
                for p in range(h):
                    buf[pl.ds(lv.row(x0 + p, 0), ny), :] = ref[lv.index, "qx"][slot, int(side > 0), pl.ds(p * ny, ny), :]
                    buf[pl.ds(lv.row(0, y0 + p), nx, stride=lv.pitch), :] = ref[lv.index, "qy"][
                        slot, int(side > 0), pl.ds(p * nx, nx), :
                    ]
            for i in (-1, 1):
                for j in (-1, 1):
                    x0, y0 = far_side(nx, i, h), far_side(ny, j, h)
                    for p in range(h):
                        buf[pl.ds(lv.row(x0 + p, y0), h), :] = ref[lv.index, "qc"][
                            slot, 2 * (i > 0) + (j > 0), pl.ds(p * h, h), :
                        ]
            deep_finish(lv, slot, EDGES)
            got, zone = ref[lv.index, "qz"], ref[lv.index, "zone"]
            sources = [(-1, lv.parts - 1)] + [(0, part) for part in range(lv.parts)] + [(1, 0)]
            size = min(ny, 8)
            for place, (i, part) in enumerate(sources):
                for k in (0, 1):
                    side = 2 * k - 1
                    into = zone.at[2 * place + k]
                    into[pl.ds(0, h), :] = got[
                        slot, EDGES.index((i, -1, side)), lv.halves - 1, part, pl.ds(size - h, h), :
                    ]
                    for half in range(lv.halves):
                        into[pl.ds(h + 8 * half, size), :] = got[
                            slot, EDGES.index((i, 0, side)), half, part, pl.ds(0, size), :
                        ]
                    into[pl.ds(h + ny, h), :] = got[slot, EDGES.index((i, 1, side)), 0, part, pl.ds(0, h), :]
            where = iota((lv.pitch, LANES), 1)
            high = (where & (2 * h - 1)) >= h
            merged = []
            for place in range(len(sources)):
                low, up = (zone[2 * place + k, pl.ds(0, lv.pitch), :] for k in (0, 1))
                merged.append(jnp.where(high, low, roll(up, nz + 2 * h)))

            def shifted(x, more):
                i = -1 if x < 0 else 1 if x >= nx else 0
                source = (x - i * nx) % lv.per
                chosen = merged[0 if i < 0 else len(sources) - 1 if i > 0 else 1 + x // lv.per]
                return roll(chosen, more - (2 * h * source + h))

            if target is None:
                edge = (where < h) | ((where >= nz + h) & (where < nz + 2 * h))
                for x in range(-h, nx + h):
                    span = pl.ds(lv.row(x, -h), lv.pitch)
                    buf[span, :] = jnp.where(edge, shifted(x, 0), buf[span, :])
            else:
                group = where & 31
                edge = (group < h) | ((group >= nz + h) & (group < nz + 2 * h))
                for x in range(-h, slab + h):
                    total = jnp.zeros((lv.pitch, LANES), jnp.float32)
                    for g in range(4):
                        inner = buf[pl.ds(lv.row(slab * g + x, -h), lv.pitch), :]
                        inner = jnp.where(group < 3 * h, roll(inner, h + 32 * g), roll(inner, 5 * h + 32 * g))
                        inner = jnp.where(edge, shifted(slab * g + x, 32 * g), inner)
                        total = jnp.where(where >= 32 * g, inner, total)
                    target[pl.ds(rim.row(x, -h), lv.pitch), :] = jnp.where(group < nz + 2 * h, total, 0.0)

        def joined(name, x, from_y, rows):
            g = x // slab
            inner = ref[0, name][pl.ds(first.row(x, from_y) - first.c0, rows), :]
            outer = ref["rim", name][pl.ds(rim.row(x - g * slab, from_y) - rim.c0, rows), :]
            where = iota(inner.shape, 1)
            outer = jnp.where(
                where < LANES // 2, roll(outer, -HALO - 32 * g), roll(outer, LANES - 5 * HALO - 32 * g)
            )
            return jnp.where((where < HALO) | (where >= LANES - HALO), outer, inner)

        def around(lv, buf, lo, rows):
            base, p = lv.c0 + lo, lv.pitch
            if p % 8 == 0:
                block = buf[pl.ds(base - p, rows + 2 * p), :]
                before, mid, after = block[:rows], block[p : p + rows], block[2 * p :]
            else:
                mid = buf[pl.ds(base, rows), :]
                before, after = buf[pl.ds(base - p, rows), :], buf[pl.ds(base + p, rows), :]
            return mid, (
                before,
                after,
                buf[pl.ds(base - 1, rows), :],
                buf[pl.ds(base + 1, rows), :],
                roll(mid, 1),
                roll(mid, -1),
            )

        coeff_names = ("xm", "xp", "ym", "yp", "zm", "zp")

        def applied(lv, buf, lo, rows):
            mid, near = around(lv, buf, lo, rows)
            span = pl.ds(lo, rows)
            total = mid
            for name, value in zip(coeff_names, near):
                total = total - ref[lv.index, name][span, :] * value
            return mid, total

        def prepare(lv, buf):
            for lo, rows in lv.groups():
                span = pl.ds(lo, rows)
                mid, near = around(lv, buf, lo, rows)
                where = iota((rows, LANES), 1)
                near = list(near)
                if lv.shared and lv.nz == LANES:
                    near[4] = jnp.where(where == 0, 0.0, near[4])
                    near[5] = jnp.where(where == LANES - 1, 0.0, near[5])
                couple = [(0.5 * lv.factor) * (mid + value) for value in near]
                diagonal = couple[0]
                for value in couple[1:]:
                    diagonal = diagonal + value
                inverse = jnp.where(mid > 0.0, 1.0 / diagonal, 0.0)
                ref[lv.index, "dg"][span, :] = diagonal
                ref[lv.index, "iv"][span, :] = inverse
                couple = [value * inverse for value in couple]
                if lv.shared and lv.nz == LANES:
                    couple[4] = jnp.where(where == 0, 0.0, couple[4])
                    couple[5] = jnp.where(where == LANES - 1, 0.0, couple[5])
                for name, value in zip(coeff_names, couple):
                    ref[lv.index, name][span, :] = value

        def sweeps(lv, src, count, final):
            factors = chebyshev_factors(count)
            r, u = ref[lv.index, "r"], ref[lv.index, "u"]
            buffers = [ref[lv.index, "d0"], ref[lv.index, "d1"]]
            held, late = src, count == 3
            applications = count - 1 + (src is not None) + final
            skip = lv.h - 1 - applications
            for step in range(count):
                keep, push = factors[step]
                target = buffers[step % 2]
                if held is not None:
                    skip += 1
                for lo, rows in lv.groups(max(skip, 0)):
                    span = pl.ds(lo, rows)
                    value = r[span, :]
                    if held is not None:
                        mid, change = applied(lv, held, lo, rows)
                        value = value - change
                        r[span, :] = value
                    direction = push * value
                    if step > 0:
                        direction = direction + keep * mid
                    padded = pl.ds(lv.c0 + lo, rows)
                    if late and step == count - 1:
                        total = direction + mid + target[padded, :]
                        if src is not None:
                            total = total + src[padded, :] + u[span, :]
                        u[span, :] = total
                    target[padded, :] = direction
                    if not late:
                        u[span, :] = direction if step == 0 else u[span, :] + direction
                held = target
            if final:
                for lo, rows in lv.groups(max(skip + 1, 0)):
                    span = pl.ds(lo, rows)
                    mid, change = applied(lv, held, lo, rows)
                    r[span, :] = r[span, :] - change
            return held

        def halve(lv, buf):
            out = ref[None, "half"]
            nx, ny = lv.nx // 2, lv.ny // 2
            for x in range(nx):
                total = None
                for px in range(2):
                    for py in range(2):
                        at = lv.row(2 * x + px, py)
                        value = buf[pl.ds(at, ny, stride=2), :]
                        total = value if total is None else total + value
                out[pl.ds(x * ny, ny), :] = total
            return nx, ny

        def pair_matrix(lv, offset):
            fine, coarse = iota((LANES, LANES), 0), iota((LANES, LANES), 1)
            cell = fine - lv.zo
            inside = (cell >= 0) & (cell < lv.nz)
            match = lax.shift_right_arithmetic(cell, 1) + offset == coarse
            return jnp.where(inside & match, 0.125, 0.0)

        def restrict(lv, buf, offset):
            nx, ny = halve(lv, buf)
            return nx, ny, dot(ref[None, "half"][pl.ds(0, up8(nx * ny)), :], pair_matrix(lv, offset))

        def spread(nx, ny, value, coarse, buf):
            scratch_ref = ref[None, "half"]
            scratch_ref[pl.ds(0, up8(nx * ny)), :] = value
            for x in range(nx):
                buf[pl.ds(coarse.row(x, 0), ny), :] = scratch_ref[pl.ds(x * ny, ny), :]

        def stretch(cell, offset):
            coarse = iota((LANES, LANES), 0) - offset
            parent = lax.shift_right_arithmetic(cell, 1)
            other = parent + 2 * (cell & 1) - 1
            return jnp.where(coarse == parent, 0.75, 0.0) + jnp.where(coarse == other, 0.25, 0.0)

        def prolong(rows, pitch, origin, value, fine, buf):
            t, te, to = ref[None, "t"], ref[None, "te"], ref[None, "to"]
            t[pl.ds(0, rows), :] = value
            reach = fine.h // 2
            x0, nx, ny = -reach, fine.nx // 2 + 2 * reach, fine.ny // 2 + 2 * reach
            low = origin + x0 * pitch - reach - 1
            n = (nx - 1) * pitch + ny + 2
            mid = 0.75 * t[pl.ds(low, n), :]
            te[pl.ds(0, n), :] = mid + 0.25 * t[pl.ds(low - pitch, n), :]
            to[pl.ds(0, n), :] = mid + 0.25 * t[pl.ds(low + pitch, n), :]
            for x in range(nx):
                for px, src in ((0, te), (1, to)):
                    at = x * pitch + 1
                    mid = 0.75 * src[pl.ds(at, ny), :]
                    to_row = fine.row(2 * (x + x0) + px, -2 * reach)
                    buf[pl.ds(to_row, ny, stride=2), :] = mid + 0.25 * src[pl.ds(at - 1, ny), :]
                    buf[pl.ds(to_row + 1, ny, stride=2), :] = mid + 0.25 * src[pl.ds(at + 1, ny), :]

        def columns(fine):
            return iota((LANES, LANES), 1) - fine.zo

        def depth_copy(which, k):
            return pltpu.make_async_remote_copy(
                src_ref=ref[None, "zs"].at[which],
                dst_ref=ref[None, "zr"].at[which, gz],
                send_sem=ref[None, "zsend"].at[which, k],
                recv_sem=ref[None, "zrecv"].at[which, k],
                device_id=(gx, gy, depth_peer(k)),
                device_id_type=MESH,
            )

        def depth_arrival(which, k):
            source = lax.rem(gz + gzn - k, gzn)
            return pltpu.make_async_remote_copy(
                src_ref=ref[None, "zs"].at[which],
                dst_ref=ref[None, "zr"].at[which, source],
                send_sem=ref[None, "zsend"].at[which, k],
                recv_sem=ref[None, "zrecv"].at[which, k],
                device_id=(gx, gy, depth_peer(k)),
                device_id_type=MESH,
            )

        def plane_copy(which, i, j):
            px, py = plane_peer(i, j)
            return pltpu.make_async_remote_copy(
                src_ref=ref[None, "ps"].at[which],
                dst_ref=ref[None, "pr"].at[which, gx * gyn + gy],
                send_sem=ref[None, "psend"].at[which, i * gyn + j],
                recv_sem=ref[None, "precv"].at[which, i * gyn + j],
                device_id=(px, py, gz),
                device_id_type=MESH,
            )

        def plane_arrival(which, i, j):
            sx, sy = lax.rem(gx + gxn - i, gxn), lax.rem(gy + gyn - j, gyn)
            px, py = plane_peer(i, j)
            return pltpu.make_async_remote_copy(
                src_ref=ref[None, "ps"].at[which],
                dst_ref=ref[None, "pr"].at[which, sx * gyn + sy],
                send_sem=ref[None, "psend"].at[which, i * gyn + j],
                recv_sem=ref[None, "precv"].at[which, i * gyn + j],
                device_id=(px, py, gz),
                device_id_type=MESH,
            )

        def gather_depth_start(which, block):
            ref[None, "zs"][which] = block[:blk]
            for k in depth_peers:
                depth_copy(which, k).start()

        def gather_plane_start(which):
            total = ref[None, "zs"][which]
            for k in range(1, gzn):
                depth_arrival(which, k).wait_recv()
            for k in range(1, gzn):
                total = total + ref[None, "zr"][which, lax.rem(gz + k, gzn)]
            ref[None, "ps"][which] = total
            for i, j in plane_peers:
                plane_copy(which, i, j).start()
            ref[None, "pr"][which, gx * gyn + gy] = total

        def gather_end(which, buf):
            for i, j in plane_peers:
                plane_arrival(which, i, j).wait_recv()
            for i in range(gxn):
                for x in range(cx):
                    for y in range(cy):
                        rows = [ref[None, "pr"][which, i * gyn + j, pl.ds(x * cy + y, 1), :] for j in range(gyn)]
                        at = three.row(i * cx + x, y)
                        buf[pl.ds(at, gyn, stride=cy), :] = jnp.concatenate(rows, axis=0)

        def gather_waits():
            for which in range(2):
                for k in range(1, gzn):
                    depth_copy(which, k).wait_send()
                for i, j in plane_peers:
                    plane_copy(which, i, j).wait_send()

        fetches[0].wait()
        for x in range(first.nx):
            ref[0, "v"][pl.ds(first.row(x, 0), first.ny), :] = ref[None, "kin"][x]
        for fine, coarse in ((first, middle), (middle, last)):
            nx, ny, value = restrict(fine, ref[fine.index, "v"], coarse.zo)
            spread(nx, ny, value, coarse, ref[coarse.index, "v"])
        _, _, k_block = restrict(last, ref[2, "v"], gz * cz + three.zo)

        pl.semaphore_wait(barrier, len(plane_peers) + gzn - 1 + len(diagonal))
        slot0 = begin_deep(first, ref[0, "v"])
        fetches[1].wait()
        for x in range(first.nx):
            ref[0, "w"][pl.ds(first.row(x, 0), first.ny), :] = ref[None, "bin"][x]
        slot = begin_deep(first, ref[0, "w"])
        gather_depth_start(0, k_block)
        slot1 = begin_deep(middle, ref[1, "v"])
        slot2 = begin_deep(last, ref[2, "v"])
        for lv in local:
            clear(lv)
        end_deep(first, ref[0, "v"], slot0, ref["rim", "v"])
        prepare(first, ref[0, "v"])
        prepare(rim, ref["rim", "v"])
        end_deep(first, ref[0, "w"], slot, ref["rim", "w"])

        def load(lv):
            ref[lv.index, "r"][...] = ref[lv.index, "w"][pl.ds(lv.c0, lv.n), :] * ref[lv.index, "iv"][...]

        def residual(lv, name):
            ref[lv.index, name][pl.ds(lv.c0, lv.n), :] = ref[lv.index, "r"][...] * ref[lv.index, "dg"][...]

        for lv in (first, rim):
            load(lv)
            sweeps(lv, None, STEPS, True)
        for x in range(0, first.nx, 4):
            rows = 4 * first.pitch
            value = joined("r", x, -HALO, rows)
            ref[0, "v"][pl.ds(first.row(x, -HALO), rows), :] = value
            ref[0, "w"][pl.ds(first.row(x, -HALO), rows), :] = value * joined("dg", x, -HALO, rows)
        nx, ny, value = restrict(first, ref[0, "w"], middle.zo)
        spread(nx, ny, value, middle, ref[1, "w"])
        slot = begin_deep(middle, ref[1, "w"])
        slot0 = begin_deep(first, ref[0, "v"])
        drain(pending[-2:])
        end_deep(middle, ref[1, "v"], slot1)
        prepare(middle, ref[1, "v"])
        gather_plane_start(0)
        end_deep(middle, ref[1, "w"], slot)
        load(middle)
        sweeps(middle, None, STEPS, True)
        residual(middle, "w")
        nx, ny, value = restrict(middle, ref[1, "w"], last.zo)
        spread(nx, ny, value, last, ref[2, "w"])
        slot = begin_deep(last, ref[2, "w"])
        ref[1, "v"][pl.ds(middle.c0, middle.n), :] = ref[1, "r"][...]
        slot1 = begin_deep(middle, ref[1, "v"])
        drain(pending[-2:])
        end_deep(last, ref[2, "v"], slot2)
        prepare(last, ref[2, "v"])
        end_deep(last, ref[2, "w"], slot)
        load(last)
        sweeps(last, None, STEPS, True)
        residual(last, "w")
        _, _, b_block = restrict(last, ref[2, "w"], gz * cz + three.zo)
        gather_depth_start(1, b_block)
        ref[2, "v"][pl.ds(last.c0, last.n), :] = ref[2, "r"][...]
        slot2 = begin_deep(last, ref[2, "v"])
        gather_end(0, ref[3, "v"])
        prepare(three, ref[3, "v"])
        gather_plane_start(1)
        nx, ny, value = restrict(three, ref[3, "v"], four.zo)
        spread(nx, ny, value, four, ref[4, "v"])
        prepare(four, ref[4, "v"])
        end_deep(middle, ref[1, "v"], slot1)
        end_deep(last, ref[2, "v"], slot2)
        end_deep(first, ref[0, "v"], slot0, ref["rim", "v"])
        for lv in (first, rim, middle, last):
            ref[lv.index, "r"][...] = ref[lv.index, "v"][pl.ds(lv.c0, lv.n), :]
        gather_end(1, ref[3, "w"])

        load(three)
        sweeps(three, None, STEPS, True)
        residual(three, "w")
        nx, ny, value = restrict(three, ref[3, "w"], four.zo)
        spread(nx, ny, value, four, ref[4, "w"])
        load(four)
        sweeps(four, None, COARSE_STEPS, False)

        def lift(lv):
            span = pl.ds(lv.c0, lv.n)
            ref[lv.index, "v"][span, :] = jnp.where(ref[lv.index, "iv"][...] > 0.0, ref[lv.index, "v"][span, :], 0.0)
            sweeps(lv, ref[lv.index, "v"], STEPS, lv.index in (0, "rim"))

        def solved(lv):
            ref[lv.index, "w"][pl.ds(lv.c0, lv.n), :] = ref[lv.index, "u"][...]
            return ref[lv.index, "w"]

        field = solved(four)
        prolong(
            four.rows, four.pitch, four.row(0, 0), dot(field[...], stretch(columns(three), four.zo)), three, ref[3, "v"]
        )
        lift(three)
        field = solved(three)

        reach = HALO // 2 + 1
        pitch = cy + 2 * reach
        picked = up8((cx + 2 * reach) * pitch)
        row, source = iota((picked, three.rows), 0), iota((picked, three.rows), 1)
        plane = row // pitch
        cell_x, cell_y = gx * cx - reach + plane, gy * cy - reach + (row - plane * pitch)
        inside = (cell_x >= 0) & (cell_x < three.nx) & (cell_y >= 0) & (cell_y < three.ny)
        wanted = three.row(0, 0) + cell_x * three.pitch + cell_y
        window = dot(jnp.where(inside & (source == wanted), 1.0, 0.0), field[...], True)
        weights = stretch(columns(last) + gz * last.nz, three.zo)
        prolong(picked, pitch, reach * pitch + reach, dot(window, weights), last, ref[2, "v"])
        lift(last)
        field = solved(last)
        slot = begin_deep(last, field)
        drain(pending[-1:])
        gather_waits()
        end_deep(last, field, slot)
        weights = stretch(columns(middle), last.zo)
        prolong(last.rows, last.pitch, last.row(0, 0), dot(field[...], weights), middle, ref[1, "v"])
        lift(middle)
        field = solved(middle)
        end_deep(middle, field, begin_deep(middle, field))
        drain([pending[-1]])
        column = iota((LANES, LANES), 1)
        prolong(
            middle.rows, middle.pitch, middle.row(0, 0), dot(field[...], stretch(column, middle.zo)), first, ref[0, "v"]
        )
        lift(first)
        group = column & 31
        cells = jnp.where(group < 3 * HALO, group - HALO, group + (LANES - 5 * HALO))
        weights = jnp.where(group < 6 * HALO, stretch(cells, middle.zo), 0.0)
        total, planes = None, slab // 2 + 2 * (HALO // 2 + 1)
        for g in range(4):
            part = field[pl.ds(middle.row(slab // 2 * g - HALO // 2 - 1, -HALO), planes * middle.pitch), :]
            part = dot(part, jnp.where(lax.shift_right_arithmetic(column, 5) == g, weights, 0.0))
            total = part if total is None else total + part
        rows = planes * middle.pitch
        prolong(rows, middle.pitch, (HALO // 2 + 1) * middle.pitch + HALO, total, rim, ref["rim", "v"])
        lift(rim)

        for x in range(first.nx):
            u_ref[x] = joined("u", x, 0, first.ny)
            res_ref[x] = joined("r", x, 0, first.ny) * joined("dg", x, 0, first.ny)

        drain()

    def on_device(right_side, conductivity):
        out = jax.ShapeDtypeStruct(box, jnp.float32)
        return pl.pallas_call(
            kernel,
            out_shape=(out, out),
            in_specs=[pl.BlockSpec(memory_space=pltpu.HBM)] * 2,
            out_specs=[pl.BlockSpec(memory_space=pltpu.VMEM)] * 2,
            scratch_shapes=shapes,
            compiler_params=pltpu.CompilerParams(
                collective_id=0, has_side_effects=True, vmem_limit_bytes=48 * 1024 * 1024
            ),
        )(right_side, conductivity)

    return on_device


def solution(mesh):
    sizes = tuple(mesh.shape[axis] for axis in ("gx", "gy", "gz"))
    spec = P("gx", "gy", "gz")
    return jax.shard_map(
        build(sizes, (32, 16, 128)), mesh=mesh, in_specs=(spec, spec), out_specs=(spec, spec), check_vma=False
    )
```
